32 devices in a mesh: fsdp: 4 (over y, core), ctx: 8 (over z, x).
Axes of the slice: x: 2, y: 2, z: 4, core: 2. Of those that a mesh axis runs over, the one named last changes fastest.
Arguments:
- stream_in: bfloat16 [8192, 767], P(('fsdp', 'ctx')), as said below
- gain_attn: bfloat16 [768], P('fsdp'), may hold values from 0.5 to 1.5
- w_qkv: bfloat16 [768, 2304], P('fsdp'), may hold values from -0.3125 to 0.3125
- bias_qv: bfloat16 [1536], P('fsdp'), may hold values from -4 to 4
- w_out: bfloat16 [768, 768], P('fsdp'), may hold values from -2 to 2
- bias_out: bfloat16 [768], P('fsdp'), may hold values from -4 to 4
- gain_mlp: bfloat16 [768], P('fsdp'), may hold values from 0.5 to 1.5
- w_up: bfloat16 [768, 3072], P('fsdp'), may hold values from -0.21875 to 0.21875
- bias_up: bfloat16 [3072], P('fsdp'), may hold values from -4 to 4
- w_down: bfloat16 [3072, 768], P('fsdp'), may hold values from -0.109375 to 0.109375
- bias_down: bfloat16 [768], P('fsdp'), may hold values from -4 to 4
- grad_out: bfloat16 [8192, 767], P(('fsdp', 'ctx')), may hold values from -6 to 6
Outputs:
- stream_out: bfloat16 [8192, 767], P(('fsdp', 'ctx'))
- grad_stream: float32 [8192, 767], P(('fsdp', 'ctx'))
- grad_gain_attn: float32 [768], P('fsdp')
- grad_w_qkv: float32 [768, 2304], P('fsdp')
- grad_bias_qv: float32 [1536], P('fsdp')
- grad_w_out: float32 [768, 768], P('fsdp')
- grad_bias_out: float32 [768], P('fsdp')
- grad_gain_mlp: float32 [768], P('fsdp')
- grad_w_up: float32 [768, 3072], P('fsdp')
- grad_bias_up: float32 [3072], P('fsdp')
- grad_w_down: float32 [3072, 768], P('fsdp')
- grad_bias_down: float32 [768], P('fsdp')
The draws below stay inside these ranges and needn't reach their ends.
Inputs may be any that keep to these rules, and one draw needn't show every extreme that they name: `stream_in`: every row is the first 767 entries of a zero-mean row of 768 entries, given as differences of neighbouring entries of a random row.
All inputs are finite; a program needn't handle non-finite values.
Results may differ from the reference program's by a relative error of at most 0.018.
Values may be sent and summed in bfloat16 or wider, within the bound.
No kernel may reach another device: no remote copies, remote signals or barrier semaphores. Data moves between devices by JAX's collectives and lax.ppermute only.
A program may use at most 192 MiB of HBM per device.

```python
import jax
import jax.numpy as jnp
from jax import lax

D = 768
H = 12
HD = 64
FF = 3072
DC = 767
BLOCK = 256
SEQ_LEN = 2048
SEQS = 4
TOKENS = 8192


def draw_stream_in(key, part):
    base_rows = jax.random.normal(key, (TOKENS, D), jnp.float32)
    return ((base_rows[:, :-1] - base_rows[:, 1:]) * 0.7071).astype(jnp.bfloat16)


def block_scale(stream_key, extent, pieces, low, high):
    def one(axis_at, parts):
        draws = jax.random.uniform(jax.random.fold_in(jax.random.fold_in(stream_key, 6), axis_at), (parts,), jnp.float32, low / len(pieces), high / len(pieces))
        return jnp.repeat(jnp.exp(draws), extent[axis_at] // parts).reshape((-1,) + (1,) * (len(extent) - axis_at - 1))

    loudness = one(*pieces[0])
    for cut in pieces[1:]:
        loudness = loudness * one(*cut)
    return loudness


def gaussian(key, dims, spread, bound, cuts=(), kind=jnp.bfloat16):
    drawn = jax.random.normal(key, dims, jnp.float32) * spread
    if len(cuts) > 0:
        drawn = block_scale(key, dims, cuts, -0.22, 0.18) * drawn
    return jnp.clip(drawn, min=-bound, max=bound).astype(kind)


def setup_inputs(seed: int = 0) -> dict:
    seeds = jax.random.split(jax.random.key(seed), 13)
    stream_in = draw_stream_in(jax.random.fold_in(seeds[12], 71), 0)
    gain_attn = jnp.clip(1.0 + 0.1 * jax.random.normal(seeds[1], (D,), jnp.float32), 0.5, 1.5).astype(jnp.bfloat16)
    w_qkv = gaussian(seeds[2], (D, 3 * D), (D // 2) ** -0.5, 0.3125, ((0, 4),))
    bias_qv = gaussian(seeds[3], (2 * D,), 0.3, 4.0, ((0, 4),))
    w_out = gaussian(seeds[4], (D, D), 8 ** -0.5, 2.0, ((0, 4),))
    bias_out = gaussian(seeds[5], (D,), 0.3, 4.0, ((0, 4),))
    gain_mlp = jnp.clip(1.0 + 0.1 * jax.random.normal(seeds[6], (D,), jnp.float32), 0.5, 1.5).astype(jnp.bfloat16)
    w_up = gaussian(seeds[7], (D, FF), D ** -0.5, 0.21875, ((0, 4),))
    bias_up = gaussian(seeds[8], (FF,), 0.3, 4.0, ((0, 4),))
    w_down = gaussian(seeds[9], (FF, D), FF ** -0.5, 0.109375, ((0, 4),))
    bias_down = gaussian(seeds[10], (D,), 0.3, 4.0, ((0, 4),))
    grad_out = gaussian(seeds[11], (TOKENS, DC), 1.0, 6.0, ((0, 32),))
    return dict(stream_in=stream_in, gain_attn=gain_attn, w_qkv=w_qkv, bias_qv=bias_qv, w_out=w_out, bias_out=bias_out, gain_mlp=gain_mlp, w_up=w_up, bias_up=bias_up, w_down=w_down, bias_down=bias_down, grad_out=grad_out)


norm_eps = 1e-05
highest = lax.Precision.HIGHEST

@jax.custom_vjp
def low(v):
    return lax.optimization_barrier(v.astype(jnp.bfloat16)).astype(jnp.float32)

@jax.custom_vjp
def low_back(v):
    return v

def low_keep(v):
    return (low(v), None)

def low_pass(kept, grad):
    return (grad,)

def back_keep(v):
    return (v, None)

def back_low(kept, grad):
    return (low(grad),)
low.defvjp(low_keep, low_pass)
low_back.defvjp(back_keep, back_low)

def matmul(left_mat, right_mat):
    return jnp.dot(left_mat, right_mat, precision=highest, preferred_element_type=jnp.float32)

def scaled_norm(stream, gain_vec):
    return stream * lax.rsqrt(lax.optimization_barrier(jnp.mean(stream * stream, axis=1, keepdims=True)) + norm_eps) * gain_vec

def centered(branch):
    return branch - lax.optimization_barrier(jnp.mean(branch, axis=1, keepdims=True))

def sequence_attention(queries, key_rows, values):
    block_width = 512 if SEQ_LEN % 512 == 0 else SEQ_LEN
    block_count = SEQ_LEN // block_width
    key_pos = jnp.arange(SEQ_LEN, dtype=jnp.int32)

    @jax.checkpoint
    def one_block(inputs):
        query_block, row_start = inputs
        scores = low_back(jnp.einsum('qhd,khd->hqk', query_block, key_rows, precision=highest))
        query_pos = row_start + jnp.arange(block_width, dtype=jnp.int32)
        allowed = (key_pos[None, :] // BLOCK <= query_pos[:, None] // BLOCK)[None]
        scores = jnp.where(allowed, scores, -1e+30)
        weights = low(jax.nn.softmax(scores, axis=2))
        return jnp.einsum('hqk,khd->qhd', weights, values, precision=highest)
    query_blocks = queries.reshape(block_count, block_width, H, HD)
    block_starts = (jnp.arange(block_count, dtype=jnp.int32) * block_width).astype(jnp.int32)
    return lax.map(one_block, (query_blocks, block_starts)).reshape(SEQ_LEN, H, HD)

def attention(queries, key_rows, values):
    shaped = (SEQS, SEQ_LEN, H, HD)

    def per_sequence(seq_group):
        return sequence_attention(seq_group[0], seq_group[1], seq_group[2])
    result = lax.map(per_sequence, (queries.reshape(shaped), key_rows.reshape(shaped), values.reshape(shaped)))
    return result.reshape(TOKENS, D)

def forward(stream_in, gain_attn, w_qkv, bias_qv, w_out, bias_out, gain_mlp, w_up, bias_up, w_down, bias_down):
    resid = jnp.concatenate([stream_in, -lax.optimization_barrier(jnp.sum(stream_in, axis=1, keepdims=True))], axis=1)
    normed = low(scaled_norm(resid, gain_attn))
    zero_bias = jnp.zeros((D,), bias_qv.dtype)
    joined_rows = low_back(matmul(normed, w_qkv) + jnp.concatenate([bias_qv[:D], zero_bias, bias_qv[D:]]))
    queries = low(joined_rows[:, :D] * HD ** (-0.5))
    key_rows = low(joined_rows[:, D:2 * D])
    values = low(joined_rows[:, 2 * D:])
    attended = low_back(low(attention(queries, key_rows, values)))
    branch = low_back(matmul(attended, w_out) + bias_out)
    middle = resid + centered(branch)
    normed_mlp = low(scaled_norm(middle, gain_mlp))
    hidden = low_back(matmul(normed_mlp, w_up) + bias_up)
    active = low(jax.nn.gelu(hidden, approximate=True))
    branch_mlp = low_back(matmul(active, w_down) + bias_down)
    result = middle + centered(branch_mlp)
    return result[:, :D - 1]

def reference(stream_in, gain_attn, w_qkv, bias_qv, w_out, bias_out, gain_mlp, w_up, bias_up, w_down, bias_down, grad_out):
    inputs = tuple((argument.astype(jnp.float32) for argument in (stream_in, gain_attn, w_qkv, bias_qv, w_out, bias_out, gain_mlp, w_up, bias_up, w_down, bias_down)))
    result, pull_back = jax.vjp(forward, *inputs)
    gradients = pull_back(grad_out.astype(jnp.float32))
    return (result.astype(jnp.bfloat16), gradients[0], gradients[1], gradients[2], gradients[3], gradients[4], gradients[5], gradients[6], gradients[7], gradients[8], gradients[9], gradients[10])
```

```python
import jax
import jax.numpy as jnp
from jax import lax
from jax.experimental import pallas as pl
from jax.experimental.pallas import tpu as pltpu
from jax.sharding import PartitionSpec as P

D = 768
H = 12
HD = 64
BLOCK = 256
HEAD_GROUPS = 4
GROUP_HEADS = H // HEAD_GROUPS
GROUP_COLS = GROUP_HEADS * HD
HEAD_SCALE = HD ** (-0.5)
NORM_EPS = 1e-05
NEG_BIG = -1e30
AXES = ("fsdp", "ctx")
VMEM_LIMIT = 100 << 19

f32 = jnp.float32
bf16 = jnp.bfloat16


def dot(left, right):
    return jnp.dot(left, right, preferred_element_type=f32)


def dot_tn(left, right):
    return lax.dot_general(left, right, (((0,), (0,)), ((), ())), preferred_element_type=f32)


def dot_nt(left, right):
    return lax.dot_general(left, right, (((1,), (1,)), ((), ())), preferred_element_type=f32)


def pick(value, index, axis=0):
    return lax.dynamic_index_in_dim(value, index, axis, keepdims=False)


def in_order(own, other, bit):
    return jnp.where(bit == 0, jnp.stack([own, other]), jnp.stack([other, own]))


def centered(branch):
    return branch - jnp.mean(branch, axis=1, keepdims=True)


def inverse_rms(stream):
    return lax.rsqrt(jnp.mean(stream * stream, axis=1, keepdims=True) + NORM_EPS)


def head_masked(value, head):
    if head == GROUP_HEADS - 1 and GROUP_HEADS % 2 == 1:
        return value[:, head * HD :], head * HD, HD
    start = (head // 2) * 2 * HD
    lanes = value[:, start : start + 2 * HD]
    at = lax.broadcasted_iota(jnp.int32, lanes.shape, 1) // HD
    return jnp.where(at == head % 2, lanes, jnp.zeros_like(lanes)), start, 2 * HD


def forward_kernel(member_ref, q_ref, k_ref, vt_ref, out_ref, log_ref):
    blocks, query_rows, _ = q_ref.shape
    rows = k_ref.shape[1]
    member = member_ref[0]

    def one_query_block(block, _):
        queries = q_ref[block ^ member]
        masked = [head_masked(queries, head) for head in range(GROUP_HEADS)]

        def one_key_block(key_block, carried):
            slot = key_block ^ member
            at = pl.multiple_of(slot * rows, rows)
            kept = []
            for head in range(GROUP_HEADS):
                top, total, acc = carried[head]
                query, start, width = masked[head]
                scores = dot_nt(k_ref[slot, :, start : start + width], query)
                new_top = jnp.maximum(top, jnp.max(scores, axis=0, keepdims=True))
                weights = jnp.exp(scores - new_top)
                fading = jnp.exp(top - new_top)
                total = total * fading + jnp.sum(weights, axis=0, keepdims=True)
                values = vt_ref[head * HD : (head + 1) * HD, pl.ds(at, rows)]
                acc = acc * fading + dot(values, weights.astype(bf16))
                kept.append((new_top, total, acc))
            return tuple(kept)

        start_state = tuple(
            (
                jnp.full((1, query_rows), NEG_BIG, f32),
                jnp.zeros((1, query_rows), f32),
                jnp.zeros((HD, query_rows), f32),
            )
            for _ in range(GROUP_HEADS)
        )
        ended = lax.fori_loop(0, block + 1, one_key_block, start_state)
        heads = jnp.concatenate([acc / total for _, total, acc in ended], axis=0)
        out_ref[block] = heads.T.astype(bf16)
        for head, (top, total, _) in enumerate(ended):
            log_ref[block, head : head + 1, :] = top + jnp.log(total)
        return 0

    lax.fori_loop(0, blocks, one_query_block, 0)


def attention_forward(member, queries, key_rows, values_t):
    blocks, query_rows, cols = queries.shape
    rows = key_rows.shape[1]
    scores = GROUP_HEADS * query_rows * rows * blocks * (blocks + 1) // 2
    return pl.pallas_call(
        forward_kernel,
        out_shape=(
            jax.ShapeDtypeStruct((blocks, query_rows, cols), bf16),
            jax.ShapeDtypeStruct((blocks, 8, query_rows), f32),
        ),
        in_specs=[pl.BlockSpec(memory_space=pltpu.SMEM)] + [pl.BlockSpec(memory_space=pltpu.VMEM)] * 3,
        out_specs=(pl.BlockSpec(memory_space=pltpu.VMEM),) * 2,
        compiler_params=pltpu.CompilerParams(vmem_limit_bytes=VMEM_LIMIT),
        cost_estimate=pl.CostEstimate(
            flops=4 * HD * scores, bytes_accessed=4 * rows * blocks * cols, transcendentals=scores
        ),
        name="attend",
    )(member, queries, key_rows, values_t)


def backward_kernel(
    member_ref, q_ref, k_ref, v_ref, kt_ref, g_ref, out_ref, log_ref, dq_ref, dk_ref, dv_ref, dk_acc, dv_acc, dq_acc, delta_ref
):
    blocks = q_ref.shape[0]
    rows = k_ref.shape[1]
    member = member_ref[0]

    def prepare(block, _):
        products = (g_ref[block].astype(f32) * out_ref[block].astype(f32)).T
        for head in range(GROUP_HEADS):
            part = products[head * HD : (head + 1) * HD]
            delta_ref[block, head : head + 1, :] = jnp.sum(part, axis=0, keepdims=True)
        return 0

    lax.fori_loop(0, blocks, prepare, 0)
    dq_acc[...] = jnp.zeros_like(dq_acc)

    def one_key_block(key_block, _):
        slot = key_block ^ member
        at = pl.multiple_of(slot * rows, rows)
        dk_acc[...] = jnp.zeros_like(dk_acc)
        dv_acc[...] = jnp.zeros_like(dv_acc)

        def one_query_block(block, _):
            queries, grads = q_ref[block ^ member], g_ref[block]
            for head in range(GROUP_HEADS):
                query, start, width = head_masked(queries, head)
                grad, _, _ = head_masked(grads, head)
                lanes = slice(start, start + width)
                scores = dot_nt(k_ref[slot, :, lanes], query)
                prob = jnp.exp(scores - log_ref[block, head : head + 1, :])
                grad_prob = dot_nt(v_ref[slot, :, lanes], grad)
                grad_scores = (prob * (grad_prob - delta_ref[block, head : head + 1, :])).astype(bf16)
                dv_acc[:, lanes] += dot(prob.astype(bf16), grad)
                dk_acc[:, lanes] += dot(grad_scores, query)
                part = slice(head * HD, (head + 1) * HD)
                dq_acc[block, part, :] += dot(kt_ref[part, pl.ds(at, rows)], grad_scores)
            return 0

        lax.fori_loop(key_block, blocks, one_query_block, 0)
        dk_ref[slot] = dk_acc[...].astype(bf16)
        dv_ref[slot] = dv_acc[...].astype(bf16)
        return 0

    lax.fori_loop(0, blocks, one_key_block, 0)

    def write(block, _):
        dq_ref[block ^ member] = (dq_acc[block].T * HEAD_SCALE).astype(bf16)
        return 0

    lax.fori_loop(0, blocks, write, 0)


def attention_backward(member, queries, key_rows, values, keys_t, grads, outs, logs):
    blocks, query_rows, cols = queries.shape
    rows = key_rows.shape[1]
    scores = GROUP_HEADS * query_rows * rows * blocks * (blocks + 1) // 2
    return pl.pallas_call(
        backward_kernel,
        out_shape=(
            jax.ShapeDtypeStruct((blocks, query_rows, cols), bf16),
            jax.ShapeDtypeStruct((blocks, rows, cols), bf16),
            jax.ShapeDtypeStruct((blocks, rows, cols), bf16),
        ),
        in_specs=[pl.BlockSpec(memory_space=pltpu.SMEM)] + [pl.BlockSpec(memory_space=pltpu.VMEM)] * 7,
        out_specs=(pl.BlockSpec(memory_space=pltpu.VMEM),) * 3,
        scratch_shapes=[
            pltpu.VMEM((rows, cols), f32),
            pltpu.VMEM((rows, cols), f32),
            pltpu.VMEM((blocks, cols, query_rows), f32),
            pltpu.VMEM((blocks, 8, query_rows), f32),
        ],
        compiler_params=pltpu.CompilerParams(vmem_limit_bytes=VMEM_LIMIT),
        cost_estimate=pl.CostEstimate(
            flops=10 * HD * scores, bytes_accessed=10 * rows * blocks * cols, transcendentals=scores
        ),
        name="attend_back",
    )(member, queries, key_rows, values, keys_t, grads, outs, logs)


def solution(mesh):
    fsdp_count, ctx_count = mesh.shape["fsdp"], mesh.shape["ctx"]
    half = ctx_count // 2
    steps = half.bit_length() - 1
    ctx_steps = steps + 1
    splits = ctx_count // HEAD_GROUPS
    shard = D // fsdp_count

    def send(value, target):
        pairs = []
        for source in range(fsdp_count * ctx_count):
            row, at = target(*divmod(source, ctx_count))
            pairs.append((source, row * ctx_count + at))
        return lax.ppermute(value, AXES, pairs)

    def to_core(value):
        return send(value, lambda row, at: (row ^ 1, at))

    def to_chip_row(value):
        return send(value, lambda row, at: (row ^ 2, at))

    def to_ctx(value, bit):
        return send(value, lambda row, at: (row, at ^ bit))

    def swap_sequences(value):
        return send(
            value, lambda row, at: (row, at) if (row & 1) == at // half else (row ^ 1, at ^ half)
        )

    groups = [
        [(row + core) * ctx_count + side * half + at for core in range(2) for at in range(half)]
        for row in range(0, fsdp_count, 2)
        for side in range(2)
    ]

    def group_all_to_all(value):
        return lax.all_to_all(value, AXES, 0, 0, axis_index_groups=groups, tiled=True)

    def reversed_bits(value):
        out = 0
        for at in range(steps):
            out = out | (((value >> at) & 1) << (steps - 1 - at))
        return out

    def local(
        stream_in,
        gain_attn,
        w_qkv,
        bias_qv,
        w_out,
        bias_out,
        gain_mlp,
        w_up,
        bias_up,
        w_down,
        bias_down,
        grad_out,
    ):
        rows = stream_in.shape[0]
        query_rows = rows // splits
        fsdp_at, ctx_at = lax.axis_index("fsdp"), lax.axis_index("ctx")
        core, chip_row = fsdp_at & 1, fsdp_at >> 1
        side, inner = ctx_at // half, ctx_at % half
        member = core * half + inner
        member_at = member.astype(jnp.int32).reshape(1)
        head_group = inner % HEAD_GROUPS
        query_split = member // HEAD_GROUPS

        def over_fsdp(value):
            pair = in_order(value, to_chip_row(value), chip_row)
            return jnp.swapaxes(in_order(pair, to_core(pair), core), 0, 1).reshape(
                (fsdp_count,) + value.shape
            )

        stream = swap_sequences(stream_in).astype(f32)
        grad_top = swap_sequences(grad_out).astype(f32)
        vectors = over_fsdp(
            jnp.concatenate([gain_attn, bias_qv, bias_out, gain_mlp, bias_up, bias_down])
        ).astype(f32)
        cuts, at = [], 0
        for part in (gain_attn, bias_qv, bias_out, gain_mlp, bias_up, bias_down):
            cuts.append(vectors[:, at : at + part.shape[0]])
            at += part.shape[0]
        gain_attn_all, bias_qv_all, bias_out_all, gain_mlp_all, _, bias_down_all = [
            cut.reshape(-1) for cut in cuts
        ]
        bias_up_half = pick(cuts[4].reshape(2, 2, -1), core, 1).reshape(-1)
        w_heads = over_fsdp(
            pick(w_qkv.reshape(shard, 3, HEAD_GROUPS, GROUP_COLS), head_group, 2).reshape(shard, -1)
        ).reshape(D, 3 * GROUP_COLS)
        w_out_all = over_fsdp(w_out).reshape(D, D)
        w_down_half = in_order(w_down, to_chip_row(w_down), chip_row).reshape(-1, D)
        up_parts = w_up.reshape(shard, 2, 2, -1)
        up_rows = in_order(pick(up_parts, core, 2), to_core(pick(up_parts, 1 - core, 2)), core)
        w_up_half = in_order(up_rows, to_chip_row(up_rows), chip_row).reshape(D, -1)

        resid = jnp.concatenate([stream, -jnp.sum(stream, axis=1, keepdims=True)], axis=1)
        inv_attn = inverse_rms(resid)
        unit = resid * inv_attn
        unit_low = unit.astype(bf16)
        first, second = unit_low[None, : rows // 2], unit_low[None, rows // 2 :]
        for step in range(steps):
            got = (to_ctx(first, 1 << step), to_ctx(second, 1 << (steps - 1 - step)))
            got = lax.optimization_barrier(got)
            first, second = jnp.concatenate([first, got[0]]), jnp.concatenate([second, got[1]])
        second = jnp.stack([second[reversed_bits(slot)] for slot in range(half)])
        both = jnp.concatenate([first, second], axis=1)
        gathered = jnp.concatenate([both, to_core(both)])
        normed = (gathered.astype(f32) * gain_attn_all).astype(bf16)
        normed_query = pick(normed.reshape(ctx_count, splits, query_rows, D), query_split, 1)

        wq, wk, wv = (w_heads[:, at * GROUP_COLS : (at + 1) * GROUP_COLS] for at in range(3))
        bias_parts = pick(bias_qv_all.reshape(2, HEAD_GROUPS, GROUP_COLS), head_group, 1)
        queries = ((dot(normed_query, wq) + bias_parts[0]) * HEAD_SCALE).astype(bf16)
        key_rows = dot(normed, wk).astype(bf16)
        values = (dot(normed, wv) + bias_parts[1]).astype(bf16)
        flat = normed.reshape(-1, D)
        keys_t = lax.dot_general(wk, flat, (((0,), (1,)), ((), ())), preferred_element_type=f32)
        values_t = lax.dot_general(wv, flat, (((0,), (1,)), ((), ())), preferred_element_type=f32)
        keys_t = keys_t.astype(bf16)
        values_t = (values_t + bias_parts[1][:, None]).astype(bf16)
        outs, logs = attention_forward(member_at, queries, key_rows, values_t)
        attended = group_all_to_all(outs)
        attended = (
            attended.reshape(splits, HEAD_GROUPS, query_rows, GROUP_COLS)
            .transpose(0, 2, 1, 3)
            .reshape(rows, D)
        )

        middle = resid + centered(dot(attended, w_out_all) + bias_out_all)
        inv_mlp = inverse_rms(middle)
        unit_mlp = middle * inv_mlp
        normed_mlp = (unit_mlp * gain_mlp_all).astype(bf16)
        grad_result = jnp.concatenate([grad_top, jnp.zeros((rows, 1), f32)], axis=1)
        grad_branch_mlp = centered(grad_result).astype(bf16)
        two_norm = jnp.concatenate([normed_mlp, to_core(normed_mlp)])
        two_grad = jnp.concatenate([grad_branch_mlp, to_core(grad_branch_mlp)])
        hidden = dot(two_norm, w_up_half) + bias_up_half
        active, gelu_back = jax.vjp(lambda h: jax.nn.gelu(h, approximate=True), hidden)
        active = active.astype(bf16)
        part_mlp = dot(active, w_down_half)
        grad_hidden = gelu_back(dot_nt(two_grad, w_down_half))[0].astype(bf16)
        part_norm = dot_nt(grad_hidden, w_up_half)
        part = jnp.stack([part_mlp, part_norm]).reshape(2, 2, rows, D)
        part_other = to_core(part[:, 1].astype(bf16))
        branch_mlp = part[0, 0] + part_other[0] + bias_down_all
        grad_norm = part[1, 0] + part_other[1]
        stream_out = (middle + centered(branch_mlp))[:, : D - 1].astype(bf16)
        grad_down = dot_tn(active, two_grad).astype(bf16)
        grad_up = dot_tn(two_norm, grad_hidden).astype(bf16)

        sum_gain_mlp = jnp.sum(grad_norm * unit_mlp, axis=0)
        scaled = grad_norm * gain_mlp_all
        grad_middle = grad_result + inv_mlp * (
            scaled - unit_mlp * jnp.mean(scaled * unit_mlp, axis=1, keepdims=True)
        )
        grad_branch = centered(grad_middle).astype(bf16)
        grad_out_w = dot_tn(attended, grad_branch).astype(bf16)
        grad_attended = dot_nt(grad_branch, w_out_all).astype(bf16)
        grad_attended = (
            grad_attended.reshape(splits, query_rows, HEAD_GROUPS, GROUP_COLS)
            .transpose(0, 2, 1, 3)
            .reshape(ctx_count, query_rows, GROUP_COLS)
        )
        grads = group_all_to_all(grad_attended)
        dq, dk, dv = attention_backward(
            member_at, queries, key_rows, values, keys_t, grads, outs, logs
        )

        grad_normed = dot_nt(dk.reshape(-1, GROUP_COLS), wk) + dot_nt(dv.reshape(-1, GROUP_COLS), wv)
        from_query = dot_nt(dq.reshape(-1, GROUP_COLS), wq).reshape(ctx_count, 1, query_rows, D)
        chosen = (jnp.arange(splits) == query_split)[None, :, None, None]
        grad_normed = grad_normed.reshape(ctx_count, splits, query_rows, D) + jnp.where(
            chosen, from_query, 0.0
        )
        grad_normed = grad_normed.reshape(ctx_count, rows, D).astype(bf16)
        both = grad_normed[:half] + to_core(grad_normed[half:])
        first, second = both[:, : rows // 2], both[:, rows // 2 :]
        second = jnp.stack([second[reversed_bits(slot)] for slot in range(half)])
        for step in reversed(range(steps)):
            keep = 1 << step
            got = (
                to_ctx(first[keep:], 1 << step),
                to_ctx(second[keep:], 1 << (steps - 1 - step)),
            )
            got = lax.optimization_barrier(got)
            first, second = first[:keep] + got[0], second[:keep] + got[1]
        grad_normed = jnp.concatenate([first[0], second[0]]).astype(f32)

        sum_gain_attn = jnp.sum(grad_normed * unit, axis=0)
        scaled = grad_normed * gain_attn_all
        grad_resid = grad_middle + inv_attn * (
            scaled - unit * jnp.mean(scaled * unit, axis=1, keepdims=True)
        )
        grad_stream = (grad_resid[:, : D - 1] - grad_resid[:, D - 1 :]).astype(bf16)

        def scatter_ctx(value, first_bit=0):
            for step in range(first_bit, ctx_steps):
                bit = (ctx_at >> step) & 1
                parts = value.reshape((value.shape[0] // 2, 2) + value.shape[1:])
                value = pick(parts, bit, 1) + to_ctx(pick(parts, 1 - bit, 1), 1 << step)
            return value[0]

        def gather_ctx(value, first_bit, last_bit):
            value = value[None]
            for step in reversed(range(first_bit, last_bit)):
                pair = in_order(value, to_ctx(value, 1 << step), (ctx_at >> step) & 1)
                value = jnp.swapaxes(pair, 0, 1).reshape((-1,) + value.shape[1:])
            return value

        down = grad_down.reshape(2, -1, D)
        down = pick(down, chip_row) + to_chip_row(pick(down, 1 - chip_row))
        down = scatter_ctx(down.reshape(ctx_count, -1, D))
        grad_w_down = gather_ctx(down, 0, ctx_steps).reshape(-1, D).astype(f32)

        up = grad_up.reshape(2, 2, shard, -1)
        up = pick(up, chip_row) + to_chip_row(pick(up, 1 - chip_row))
        up = scatter_ctx(
            up.reshape(2, ctx_count, shard // ctx_count, -1).transpose(1, 0, 2, 3)
        ).reshape(2, shard // ctx_count, 2, -1)
        up = in_order(pick(up, core), to_core(pick(up, 1 - core)), core)
        up = up.transpose(1, 2, 0, 3).reshape(shard // ctx_count, -1)
        grad_w_up = gather_ctx(up, 0, ctx_steps).reshape(shard, -1).astype(f32)

        def over_rows(value):
            value = value.reshape((2, 2, shard) + value.shape[1:])
            value = pick(value, core, 1) + to_core(pick(value, 1 - core, 1))
            return pick(value, chip_row) + to_chip_row(pick(value, 1 - chip_row))

        out_w = scatter_ctx(over_rows(grad_out_w).reshape(ctx_count, -1, D))
        grad_w_out = gather_ctx(out_w, 0, ctx_steps).reshape(shard, D).astype(f32)

        heads_w = jnp.concatenate(
            [
                dot_tn(normed_query.reshape(-1, D), dq.reshape(-1, GROUP_COLS)),
                dot_tn(flat, dk.reshape(-1, GROUP_COLS)),
                dot_tn(flat, dv.reshape(-1, GROUP_COLS)),
            ],
            axis=1,
        ).astype(bf16)
        heads_w = over_rows(heads_w).reshape(splits, -1, 3 * GROUP_COLS)
        heads_w = scatter_ctx(heads_w, 2)
        heads_w = gather_ctx(heads_w, 2, ctx_steps).reshape(shard, 3, GROUP_COLS)
        heads_w = gather_ctx(heads_w, 0, 2)
        grad_w_qkv = heads_w.transpose(1, 2, 0, 3).reshape(shard, 3 * D).astype(f32)

        def placed(value, parts, index):
            return jnp.where(
                (jnp.arange(parts) == index)[:, None], value.reshape(1, -1), 0.0
            ).reshape(-1)

        up_sum = jnp.sum(grad_hidden.astype(f32), axis=0).reshape(2, 1, -1)
        up_sum = jnp.where((jnp.arange(2) == core)[None, :, None], up_sum, 0.0).reshape(-1)
        sums = (
            sum_gain_attn,
            placed(jnp.sum(dq.astype(f32), axis=(0, 1)), HEAD_GROUPS, head_group),
            placed(jnp.sum(dv.astype(f32), axis=(0, 1)), HEAD_GROUPS, head_group),
            jnp.sum(grad_branch.astype(f32), axis=0),
            sum_gain_mlp,
            up_sum,
            jnp.sum(grad_branch_mlp.astype(f32), axis=0),
        )
        total = lax.psum(jnp.concatenate(sums), AXES)
        vector_outs, at = [], 0
        for width in (D, 2 * D, D, D, up_sum.shape[0], D):
            vector_outs.append(pick(total[at : at + width].reshape(fsdp_count, -1), fsdp_at))
            at += width
        v_gain_attn, v_bias_qv, v_bias_out, v_gain_mlp, v_bias_up, v_bias_down = vector_outs

        return (
            swap_sequences(stream_out),
            swap_sequences(grad_stream).astype(f32),
            v_gain_attn,
            grad_w_qkv,
            v_bias_qv,
            grad_w_out,
            v_bias_out,
            v_gain_mlp,
            grad_w_up,
            v_bias_up,
            grad_w_down,
            v_bias_down,
        )

    rows_spec, matrix_spec, vector_spec = P(AXES, None), P("fsdp", None), P("fsdp")
    return jax.shard_map(
        local,
        mesh=mesh,
        in_specs=(
            rows_spec,
            vector_spec,
            matrix_spec,
            vector_spec,
            matrix_spec,
            vector_spec,
            vector_spec,
            matrix_spec,
            vector_spec,
            matrix_spec,
            vector_spec,
            rows_spec,
        ),
        out_specs=(
            rows_spec,
            rows_spec,
            vector_spec,
            matrix_spec,
            vector_spec,
            matrix_spec,
            vector_spec,
            vector_spec,
            matrix_spec,
            vector_spec,
            matrix_spec,
            vector_spec,
        ),
        check_vma=False,
    )
```

```python
import jax
import jax.numpy as jnp
from jax import lax
from jax.experimental import pallas as pl
from jax.experimental.pallas import tpu as pltpu
from jax.sharding import PartitionSpec as P

D = 768
H = 12
HD = 64
HEAD_GROUPS = 4
GROUP_HEADS = H // HEAD_GROUPS
GROUP_COLS = GROUP_HEADS * HD
HEAD_SCALE = HD ** (-0.5)
NORM_EPS = 1e-05
NEG_BIG = -1e30
GELU_A = 0.7978845608028654
GELU_B = 0.044715
LANES = 128
PIECES = 8
EXTRA = 8
AXES = ("fsdp", "ctx")
VMEM_LIMIT = 120 << 19
UNROLL_BLOCKS = 8

f32 = jnp.float32
bf16 = jnp.bfloat16


def dot(left, right):
    return lax.dot_general(left, right, (((1,), (0,)), ((), ())), preferred_element_type=f32)


def dot_tn(left, right):
    return lax.dot_general(left, right, (((0,), (0,)), ((), ())), preferred_element_type=f32)


def dot_nt(left, right):
    return lax.dot_general(left, right, (((1,), (1,)), ((), ())), preferred_element_type=f32)


def centered(branch):
    return branch - jnp.mean(branch, axis=1, keepdims=True)


def inverse_rms(stream):
    return lax.rsqrt(jnp.mean(stream * stream, axis=1, keepdims=True) + NORM_EPS)


def norm_back(grad, unit, inverse):
    return inverse * (grad - unit * jnp.mean(grad * unit, axis=1, keepdims=True))


def slab_at(relative):
    return ((relative & 1) << 1) | (relative >> 1)


def piece_at(relative):
    return ((relative & 1) << 2) | (relative & 2) | ((relative >> 2) & 1)


def loop(start, stop, body, carried):
    if isinstance(start, int) and isinstance(stop, int) and stop - start <= UNROLL_BLOCKS:
        for at in range(start, stop):
            carried = body(at, carried)
        return carried
    return lax.fori_loop(start, stop, body, carried)


def call(body, name, outs, args, flops=0, exps=0, scratch=(), **grid):
    moved = sum(x.size * x.dtype.itemsize for x in tuple(args) + tuple(outs))
    specs = dict(
        in_specs=[pl.BlockSpec(memory_space=pltpu.SMEM)]
        + [pl.BlockSpec(memory_space=pltpu.VMEM)] * (len(args) - 1),
        out_specs=tuple(pl.BlockSpec(memory_space=pltpu.VMEM) for _ in outs),
    )
    specs.update(grid)
    return pl.pallas_call(
        body,
        out_shape=tuple(outs),
        scratch_shapes=list(scratch),
        compiler_params=pltpu.CompilerParams(vmem_limit_bytes=VMEM_LIMIT),
        cost_estimate=pl.CostEstimate(flops=flops, bytes_accessed=moved, transcendentals=exps),
        name=name,
        **specs,
    )(*args)


def shape(dims, kind):
    return jax.ShapeDtypeStruct(tuple(dims), kind)


def norm_kernel(place, x_ref, resid_ref, first_ref, second_ref):
    x = x_ref[...].astype(f32)
    last = lax.broadcasted_iota(jnp.int32, x.shape, 1) == D - 1
    resid = jnp.where(last, -jnp.sum(x, axis=1, keepdims=True), x)
    resid_ref[...] = resid
    unit = (resid * inverse_rms(resid)).astype(bf16)
    rows = x.shape[0] // 2
    first_ref[0] = unit[:rows]
    second_ref[0] = unit[rows:]


def load_heads(place, slab_ref, weights):
    shard = slab_ref.shape[1]
    for row in range(slab_ref.shape[0]):
        slab = slab_ref[slab_at(row ^ place[1])]
        for part, weight in enumerate(weights):
            weight[row * shard : (row + 1) * shard, :] = slab[
                :, part * GROUP_COLS : (part + 1) * GROUP_COLS
            ]


def project_kernel(
    place, n_ref, slab_ref, gain_ref, bias_ref, k_ref, v_ref, kt_ref, vt_ref, qt_ref, wq, wk, wv
):
    @pl.when(pl.program_id(0) == 0)
    def _():
        load_heads(place, slab_ref, (wq, wk, wv))

    query_rows = qt_ref.shape[2]
    gain = gain_ref[...]
    normed = (n_ref[0].astype(f32) * gain).astype(bf16)
    keys = dot(normed, wk[...])
    k_ref[0] = keys.astype(bf16)
    kt_ref[...] = keys.T.astype(bf16)
    values = dot(normed, wv[...]) + bias_ref[1:2, :]
    v_ref[0] = values.astype(bf16)
    vt_ref[...] = values.T.astype(bf16)
    at = pl.multiple_of(place[2] * query_rows, query_rows)
    mine = (n_ref[0, pl.ds(at, query_rows), :].astype(f32) * gain).astype(bf16)
    queries = (dot(mine, wq[...]) + bias_ref[0:1, :]) * HEAD_SCALE
    qt_ref[0] = queries.T.astype(bf16)


def by_head(value):
    head = lax.broadcasted_iota(jnp.int32, value.shape, 0) // HD
    zero = jnp.zeros_like(value)
    return jnp.concatenate([jnp.where(head == at, value, zero) for at in range(GROUP_HEADS)], axis=1)


def attend_kernel(place, qt_ref, k_ref, vt_ref, out_ref, log_ref):
    blocks, _, width = qt_ref.shape
    rows = k_ref.shape[1]
    member = place[0]

    def one_query_block(block, _):
        queries = by_head(qt_ref[block ^ member])

        def one_key_block(key_block, carried):
            top, total, accs = carried
            slot = key_block ^ member
            at = pl.multiple_of(slot * rows, rows)
            scores = dot(k_ref[slot], queries)
            new_top = jnp.maximum(top, jnp.max(scores, axis=0, keepdims=True))
            weights = jnp.exp(scores - new_top)
            fading = jnp.exp(top - new_top)
            total = total * fading + jnp.sum(weights, axis=0, keepdims=True)
            low = weights.astype(bf16)
            kept = []
            for head in range(GROUP_HEADS):
                lanes = slice(head * width, (head + 1) * width)
                values = vt_ref[head * HD : (head + 1) * HD, pl.ds(at, rows)]
                kept.append(accs[head] * fading[:, lanes] + dot(values, low[:, lanes]))
            return new_top, total, tuple(kept)

        start_state = (
            jnp.full((1, GROUP_HEADS * width), NEG_BIG, f32),
            jnp.zeros((1, GROUP_HEADS * width), f32),
            tuple(jnp.zeros((HD, width), f32) for _ in range(GROUP_HEADS)),
        )
        top, total, accs = loop(0, block + 1, one_key_block, start_state)
        for head in range(GROUP_HEADS):
            lanes = slice(head * width, (head + 1) * width)
            out_ref[block, head * HD : (head + 1) * HD, :] = (accs[head] / total[:, lanes]).astype(bf16)
        log_ref[block] = top + jnp.log(total)
        return 0

    loop(0, blocks, one_query_block, 0)


def attend_back_kernel(
    place, qt_ref, k_ref, v_ref, kt_ref, gt_ref, out_ref, log_ref, dq_ref, dk_ref, dv_ref, dk_acc, dv_acc, dq_acc, delta_ref
):
    blocks, _, width = qt_ref.shape
    rows = k_ref.shape[1]
    member = place[0]

    def prepare(block, _):
        products = gt_ref[block].astype(f32) * out_ref[block].astype(f32)
        for head in range(GROUP_HEADS):
            delta_ref[block, :, head * width : (head + 1) * width] = jnp.sum(
                products[head * HD : (head + 1) * HD], axis=0, keepdims=True
            )
        return 0

    lax.fori_loop(0, blocks, prepare, 0)
    dq_acc[...] = jnp.zeros_like(dq_acc)

    def one_key_block(key_block, _):
        slot = key_block ^ member
        at = pl.multiple_of(slot * rows, rows)
        dk_acc[...] = jnp.zeros_like(dk_acc)
        dv_acc[...] = jnp.zeros_like(dv_acc)

        def one_query_block(block, _):
            queries, grads = by_head(qt_ref[block ^ member]), by_head(gt_ref[block])
            prob = jnp.exp(dot(k_ref[slot], queries) - log_ref[block])
            grad_prob = dot(v_ref[slot], grads)
            grad_scores = (prob * (grad_prob - delta_ref[block])).astype(bf16)
            dv_acc[...] += dot_nt(prob.astype(bf16), grads)
            dk_acc[...] += dot_nt(grad_scores, queries)
            for head in range(GROUP_HEADS):
                part = slice(head * HD, (head + 1) * HD)
                lanes = slice(head * width, (head + 1) * width)
                dq_acc[block, part, :] += dot(kt_ref[part, pl.ds(at, rows)], grad_scores[:, lanes])
            return 0

        loop(key_block, blocks, one_query_block, 0)
        dk_ref[slot] = dk_acc[...].astype(bf16)
        dv_ref[slot] = dv_acc[...].astype(bf16)
        return 0

    loop(0, blocks, one_key_block, 0)

    def write(block, _):
        dq_ref[block ^ member] = (dq_acc[block].T * HEAD_SCALE).astype(bf16)
        return 0

    lax.fori_loop(0, blocks, write, 0)


def middle_kernel(place, att_ref, resid_ref, slab_ref, vec_ref, middle_ref, normed_ref, branch):
    query_rows = att_ref.shape[2]
    weights = [slab_ref[slab_at(row ^ place[1])] for row in range(HEAD_GROUPS)]
    for split in range(att_ref.shape[0] // HEAD_GROUPS):
        total = None
        for group in range(HEAD_GROUPS):
            part = dot_tn(att_ref[split * HEAD_GROUPS + group], weights[group])
            total = part if total is None else total + part
        branch[split * query_rows : (split + 1) * query_rows, :] = total
    middle = resid_ref[...] + centered(branch[...] + vec_ref[1:2, :])
    middle_ref[...] = middle
    normed = (middle * inverse_rms(middle) * vec_ref[2:3, :]).astype(bf16)
    cols = normed_ref.shape[2]
    for row in range(normed_ref.shape[0]):
        normed_ref[row] = normed[:, row * cols : (row + 1) * cols]


def mlp_kernel(
    place,
    n_own,
    n_mate,
    g_own,
    g_mate,
    up_own,
    up_far,
    down_own,
    down_far,
    bias_ref,
    branch_own,
    branch_mate,
    grad_own,
    grad_mate,
    down_keep,
    down_give,
    up_keep,
    up_give,
    bias_grad,
    total_own,
    total_mate,
):
    rows, piece = up_own.shape[2], up_keep.shape[3]
    wide = down_own.shape[0] // PIECES
    distances = range(up_own.shape[0] * 2)
    mine = place[1]
    up = (up_own, up_far)

    for part in range(2):
        down = (down_own, down_far)[part][...]
        normed = [[ref[distance ^ mine] for distance in distances] for ref in (n_own, n_mate)]
        active, grad_hidden = [], []
        for tile, g_ref in enumerate((g_own, g_mate)):
            hidden = None
            for distance in distances:
                far, core = distance >> 1, distance & 1
                product = dot(normed[tile][distance], up[far][core, part ^ far])
                hidden = product if hidden is None else hidden + product
            hidden = hidden + bias_ref[part : part + 1, :]
            square = hidden * hidden
            bent = jnp.tanh(GELU_A * hidden * (1.0 + GELU_B * square))
            half = 0.5 * (1.0 + bent)
            active.append((hidden * half).astype(bf16))
            slope = half + 0.5 * hidden * (1.0 - bent * bent) * (
                GELU_A * (1.0 + 3.0 * GELU_B * square)
            )
            back = dot_nt(g_ref[...], down)
            grad_hidden.append((back * slope).astype(bf16))
        for tile, (branch_total, grad_out) in enumerate(
            ((total_own, grad_own), (total_mate, grad_mate))
        ):
            branch = dot(active[tile], down)
            if part == 0:
                branch_total[...] = branch
            else:
                branch_ref = (branch_own, branch_mate)[tile]
                branch_ref[...] = (branch_total[...] + branch).astype(branch_ref.dtype)
        grad_down = dot_tn(active[0], g_own[...]) + dot_tn(active[1], g_mate[...])
        for at in range(PIECES):
            target = (down_keep, down_give)[part]
            target[piece_at(at ^ place[3])] = grad_down[at * wide : (at + 1) * wide].astype(bf16)
        for distance in distances:
            far, core = distance >> 1, distance & 1
            grad_up = dot_tn(normed[0][distance], grad_hidden[0]) + dot_tn(
                normed[1][distance], grad_hidden[1]
            )
            target = (up_keep, up_give)[far]
            for at in range(PIECES):
                target[piece_at(at ^ place[3]), core, part ^ far] = grad_up[
                    at * piece : (at + 1) * piece
                ].astype(bf16)
        bias_grad[part : part + 1, :] = sum(
            jnp.sum(grad.astype(f32), axis=0, keepdims=True) for grad in grad_hidden
        )
        keep = (grad_own, grad_mate)
        for tile in range(2):
            for distance in distances:
                far, core = distance >> 1, distance & 1
                back = dot_nt(grad_hidden[tile], up[far][core, part ^ far])
                at = distance ^ mine
                if part == 0:
                    keep[tile][at] = back.astype(keep[tile].dtype)
                else:
                    keep[tile][at] = (keep[tile][at].astype(f32) + back).astype(keep[tile].dtype)


def branch_back_kernel(
    place,
    own_ref,
    other_ref,
    middle_ref,
    top_ref,
    att_ref,
    slab_ref,
    vec_ref,
    bias_up_ref,
    grad_middle_ref,
    ga_ref,
    chunk_ref,
):
    query_rows = att_ref.shape[2]
    groups, rows = own_ref.shape[0], own_ref.shape[1]
    cols = own_ref.shape[2]
    piece = chunk_ref.shape[2] - EXTRA
    mine = place[1]
    grad = jnp.concatenate(
        [own_ref[row] + other_ref[row].astype(f32) for row in range(groups)], axis=1
    )
    middle = middle_ref[...]
    inverse = inverse_rms(middle)
    unit = middle * inverse
    gain_sum = jnp.sum(grad * unit, axis=0, keepdims=True)
    grad_top = top_ref[...].astype(f32)
    grad_middle = grad_top + norm_back(grad * vec_ref[2:3, :], unit, inverse)
    grad_middle_ref[...] = grad_middle
    grad_branch = centered(grad_middle).astype(bf16)
    splits = att_ref.shape[0] // groups
    parts = [grad_branch[at * query_rows : (at + 1) * query_rows] for at in range(splits)]
    for group in range(groups):
        weights = slab_ref[slab_at(group ^ mine)]
        for split in range(splits):
            ga_ref[split * groups + group] = dot_nt(weights, parts[split]).astype(bf16)
    out_sum = jnp.sum(grad_branch.astype(f32), axis=0, keepdims=True)
    down_sum = jnp.sum(centered(grad_top).astype(bf16).astype(f32), axis=0, keepdims=True)
    empty = jnp.zeros((1, D - 3 * cols), f32)
    for group in range(groups):
        relative = group ^ mine
        weight = None
        for split in range(splits):
            product = dot(att_ref[split * groups + group], parts[split])
            weight = product if weight is None else weight + product
        lanes = slice(group * cols, (group + 1) * cols)
        row = jnp.concatenate([out_sum[:, lanes], gain_sum[:, lanes], down_sum[:, lanes], empty], axis=1)
        up_row = jnp.where((relative & 1) == 0, bias_up_ref[pl.ds(relative >> 1, 1), :], 0.0)
        extra = jnp.concatenate([row, up_row, jnp.zeros((EXTRA - 2, D), f32)], axis=0)
        for at in range(PIECES):
            both = jnp.concatenate([weight[at * piece : (at + 1) * piece], extra], axis=0)
            chunk_ref[slab_at(relative), piece_at(at ^ place[3])] = both.astype(bf16)


def project_back_kernel(
    place,
    n_ref,
    slab_ref,
    gain_ref,
    dq_ref,
    dk_ref,
    dv_ref,
    keep_ref,
    give_ref,
    chunk_ref,
    wq,
    wk,
    wv,
    aq,
    ak,
    av,
    sums,
):
    step, steps = pl.program_id(0), pl.num_programs(0)
    mine = place[1]
    query_rows = dq_ref.shape[1]

    @pl.when(step == 0)
    def _():
        load_heads(place, slab_ref, (wq, wk, wv))
        for ref in (aq, ak, av, sums):
            ref[...] = jnp.zeros_like(ref)

    gain = gain_ref[...]
    unit = n_ref[0].astype(f32)
    normed = (unit * gain).astype(bf16)
    at = pl.multiple_of(place[2] * query_rows, query_rows)
    unit_query = n_ref[0, pl.ds(at, query_rows), :].astype(f32)
    normed_query = (unit_query * gain).astype(bf16)
    dq, dk, dv = dq_ref[0], dk_ref[0], dv_ref[0]
    ak[...] += dot_tn(normed, dk)
    av[...] += dot_tn(normed, dv)
    aq[...] += dot_tn(normed_query, dq)
    grad = dot_nt(dk, wk[...]) + dot_nt(dv, wv[...])
    grad_query = dot_nt(dq, wq[...])
    sums[0:1, :] += jnp.sum(grad * unit, axis=0, keepdims=True) + jnp.sum(
        grad_query * unit_query, axis=0, keepdims=True
    )
    sums[1:2, :GROUP_COLS] += jnp.sum(dq.astype(f32), axis=0, keepdims=True)
    sums[2:3, :GROUP_COLS] += jnp.sum(dv.astype(f32), axis=0, keepdims=True)

    def write(ref):
        ref[0] = grad.astype(bf16)
        low = ref[0, pl.ds(at, query_rows), :].astype(f32)
        ref[0, pl.ds(at, query_rows), :] = (low + grad_query).astype(bf16)

    @pl.when(step < steps // 2)
    def _():
        write(keep_ref)

    @pl.when(step >= steps // 2)
    def _():
        write(give_ref)

    @pl.when(step == steps - 1)
    def _():
        shard, piece = slab_ref.shape[1], chunk_ref.shape[2] - EXTRA
        group = place[0] % HEAD_GROUPS
        for row in range(slab_ref.shape[0]):
            lanes = slice(row * shard, (row + 1) * shard)
            first = jnp.where(group // 2 == row, sums[1:2, :GROUP_COLS], 0.0)
            second = jnp.where(2 + group // 2 == row, sums[2:3, :GROUP_COLS], 0.0)
            extra = jnp.concatenate([sums[0:1, lanes], first, second], axis=1)
            extra = jnp.concatenate([extra, jnp.zeros((EXTRA - 1, extra.shape[1]), f32)], axis=0)
            for part in range(2):
                at_row = slice(row * shard + part * piece, row * shard + (part + 1) * piece)
                block = jnp.concatenate([aq[at_row, :], ak[at_row, :], av[at_row, :]], axis=1)
                both = jnp.concatenate([block, extra], axis=0)
                chunk_ref[slab_at(row ^ mine), part ^ ((place[3] >> 2) & 1)] = both.astype(bf16)


def stream_back_kernel(
    place, first_ref, first_got, second_ref, second_got, resid_ref, grad_middle_ref, vec_ref, out_ref
):
    grad = jnp.concatenate(
        [
            first_ref[0].astype(f32) + first_got[0].astype(f32),
            second_ref[0].astype(f32) + second_got[0].astype(f32),
        ],
        axis=0,
    )
    resid = resid_ref[...]
    inverse = inverse_rms(resid)
    total = grad_middle_ref[...] + norm_back(grad * vec_ref[0:1, :], resid * inverse, inverse)
    out_ref[...] = (total - total[:, D - 1 :]).astype(bf16)


def down_out_kernel(place, piece_ref, out_ref):
    wide = piece_ref.shape[1]
    for at in range(PIECES):
        out_ref[at * wide : (at + 1) * wide, :] = piece_ref[piece_at(at ^ place[3])].astype(f32)


def up_out_kernel(place, piece_ref, up_ref, out_ref):
    slabs, rows = piece_ref.shape[1] - 1, piece_ref.shape[2]
    for at in range(PIECES):
        piece = piece_at(at ^ place[3])
        here = slice(at * rows, (at + 1) * rows)
        for row in range(slabs):
            up_ref[here, row * D : (row + 1) * D] = piece_ref[piece, slab_at(row ^ place[1])].astype(f32)
        out_ref[here, :] = piece_ref[piece, slabs].astype(f32)


def heads_out_kernel(place, piece_ref, out_ref, gain_ref, bias_ref):
    piece = piece_ref.shape[1] - EXTRA
    mine = place[1]
    gain = jnp.zeros(gain_ref.shape, f32)
    for part in range(2):
        for group in range(HEAD_GROUPS):
            value = piece_ref[piece_at((part << 2 | group) ^ place[3])].astype(f32)
            for kind in range(3):
                start = kind * D + group * GROUP_COLS
                out_ref[part * piece : (part + 1) * piece, start : start + GROUP_COLS] = value[
                    :piece, kind * GROUP_COLS : (kind + 1) * GROUP_COLS
                ]
            if part == 0:
                gain = gain + value[piece : piece + 1, :GROUP_COLS]
    gain_ref[...] = gain
    sides = []
    for side in range(2):
        group = ((2 * mine) & 3) + side
        value = piece_ref[piece_at(group ^ place[3])].astype(f32)[piece : piece + 1]
        sides.append(
            jnp.where(
                mine < 2,
                value[:, GROUP_COLS : 2 * GROUP_COLS],
                value[:, 2 * GROUP_COLS : 3 * GROUP_COLS],
            )
        )
    bias_ref[...] = jnp.concatenate(sides, axis=1)


def solution(mesh):
    fsdp_count, ctx_count = mesh.shape["fsdp"], mesh.shape["ctx"]
    half = ctx_count // 2
    steps = half.bit_length() - 1
    ctx_steps = steps + 1
    splits = ctx_count // HEAD_GROUPS
    shard = D // fsdp_count

    def send(value, target):
        pairs = []
        for source in range(fsdp_count * ctx_count):
            row, at = target(*divmod(source, ctx_count))
            pairs.append((source, row * ctx_count + at))
        return lax.ppermute(value, AXES, pairs)

    def to_core(value):
        return send(value, lambda row, at: (row ^ 1, at))

    def to_chip_row(value):
        return send(value, lambda row, at: (row ^ 2, at))

    def to_ctx(value, bit):
        return send(value, lambda row, at: (row, at ^ bit))

    def swap_sequences(value):
        return send(
            value, lambda row, at: (row, at) if (row & 1) == at // half else (row ^ 1, at ^ half)
        )

    groups = [
        [(row + core) * ctx_count + side * half + at for core in range(2) for at in range(half)]
        for row in range(0, fsdp_count, 2)
        for side in range(2)
    ]

    def group_all_to_all(value):
        return lax.all_to_all(value, AXES, 0, 0, axis_index_groups=groups, tiled=True)

    def reversed_bits(value):
        out = 0
        for at in range(steps):
            out = out | (((value >> at) & 1) << (steps - 1 - at))
        return out

    def over_fsdp(value):
        pair = jnp.stack([value, to_chip_row(value)])
        return jnp.concatenate([pair, to_core(pair)])

    def scatter_pieces(value, first_step=0):
        for step in range(first_step, 3):
            keep = value.shape[0] // 2
            value = value[:keep] + to_ctx(value[keep:], 1 << step)
        for step in range(3, ctx_steps):
            value = value + to_ctx(value, 1 << step)
        return value[0]

    def gather_pieces(value):
        value = value[None]
        for step in (2, 1, 0):
            value = jnp.concatenate([value, to_ctx(value, 1 << step)])
        return value

    def widened(value):
        width = value.shape[-1]
        return value if width >= LANES else jnp.pad(value, ((0, 0), (0, 0), (0, LANES - width)))

    def local(
        stream_in,
        gain_attn,
        w_qkv,
        bias_qv,
        w_out,
        bias_out,
        gain_mlp,
        w_up,
        bias_up,
        w_down,
        bias_down,
        grad_out,
    ):
        rows = stream_in.shape[0]
        query_rows = rows // splits
        width = max(query_rows, LANES)
        hidden = w_down.shape[0]
        fsdp_at, ctx_at = lax.axis_index("fsdp"), lax.axis_index("ctx")
        core, inner = fsdp_at & 1, ctx_at % half
        member = core * half + inner
        head_group = inner % HEAD_GROUPS
        place = jnp.stack([member, fsdp_at, member // HEAD_GROUPS, ctx_at & 7]).astype(jnp.int32)

        pad = ((0, 0), (0, 1))
        stream = swap_sequences(jnp.pad(stream_in, pad))
        w_part = w_qkv.reshape(shard, 3, HEAD_GROUPS, GROUP_COLS)
        w_part = lax.dynamic_index_in_dim(w_part, head_group, 2, keepdims=False)
        w_heads = over_fsdp(w_part.reshape(shard, 3 * GROUP_COLS))
        vectors = jnp.concatenate(
            [
                part.astype(f32).reshape(1, -1)
                for part in (gain_attn, bias_out, gain_mlp, bias_down, bias_qv, bias_up)
            ],
            axis=1,
        )
        vectors = over_fsdp(vectors).reshape(2, 2, -1)
        vectors = jnp.where(core == 0, vectors, vectors[::-1])
        vectors = jnp.where(fsdp_at < 2, vectors, vectors[:, ::-1])
        vectors = vectors.transpose(1, 0, 2).reshape(fsdp_count, -1)
        vec = vectors[:, :D].reshape(fsdp_count, 4, shard).transpose(1, 0, 2).reshape(4, D)
        bias_heads = vectors[:, D : D + 2 * shard].reshape(2, HEAD_GROUPS, GROUP_COLS)
        bias_heads = lax.dynamic_index_in_dim(bias_heads, head_group, 1, keepdims=False)
        bias_hidden = jnp.concatenate(
            [
                lax.dynamic_slice_in_dim(vectors[:, D + 2 * shard :], at, 1)
                for at in (fsdp_at, fsdp_at ^ 2)
            ]
        )
        gain = vec[0:1]

        resid, first, second = call(
            norm_kernel,
            "norm",
            (
                shape((rows, D), f32),
                shape((1, rows // 2, D), bf16),
                shape((1, rows // 2, D), bf16),
            ),
            (place, stream),
        )
        for step in range(steps):
            got = (to_ctx(first, 1 << step), to_ctx(second, 1 << (steps - 1 - step)))
            got = lax.optimization_barrier(got)
            first, second = jnp.concatenate([first, got[0]]), jnp.concatenate([second, got[1]])
        second = jnp.stack([second[reversed_bits(slot)] for slot in range(half)])
        both = jnp.concatenate([first, second], axis=1)
        gathered = jnp.concatenate([both, to_core(both)])

        block = lambda *dims: pl.BlockSpec((1,) + dims, lambda at: (at, 0, 0))
        across = pl.BlockSpec((GROUP_COLS, rows), lambda at: (0, at))
        whole = lambda *dims: pl.BlockSpec(dims, lambda at: (0,) * len(dims))
        head_weights = [pltpu.VMEM((D, GROUP_COLS), bf16)] * 3
        tokens = ctx_count * rows
        keys, values, keys_t, values_t, queries_t = call(
            project_kernel,
            "project",
            (
                shape((ctx_count, rows, GROUP_COLS), bf16),
                shape((ctx_count, rows, GROUP_COLS), bf16),
                shape((GROUP_COLS, tokens), bf16),
                shape((GROUP_COLS, tokens), bf16),
                shape((ctx_count, GROUP_COLS, query_rows), bf16),
            ),
            (place, gathered, w_heads, gain, bias_heads),
            flops=5 * tokens * D * GROUP_COLS,
            scratch=head_weights,
            grid=(ctx_count,),
            in_specs=[
                pl.BlockSpec(memory_space=pltpu.SMEM),
                block(rows, D),
                whole(fsdp_count, shard, 3 * GROUP_COLS),
                whole(1, D),
                whole(2, GROUP_COLS),
            ],
            out_specs=(
                block(rows, GROUP_COLS),
                block(rows, GROUP_COLS),
                across,
                across,
                block(GROUP_COLS, query_rows),
            ),
        )
        queries_t = widened(queries_t)
        pairs = GROUP_HEADS * query_rows * rows * ctx_count * (ctx_count + 1) // 2
        outs, logs = call(
            attend_kernel,
            "attend",
            (
                shape((ctx_count, GROUP_COLS, width), bf16),
                shape((ctx_count, 1, GROUP_HEADS * width), f32),
            ),
            (place, queries_t, keys, values_t),
            flops=4 * HD * pairs,
            exps=pairs,
        )
        attended = group_all_to_all(outs[:, :, :query_rows])

        w_out_all = over_fsdp(w_out)
        up_parts = w_up.reshape(shard, fsdp_count, hidden)
        at_slab = lambda slab: lax.dynamic_index_in_dim(up_parts, slab, 1, keepdims=False)
        up_mine = jnp.stack([at_slab(fsdp_at), at_slab(fsdp_at ^ 2)])
        up_mate = jnp.stack([at_slab(fsdp_at ^ 1), at_slab(fsdp_at ^ 3)])
        up_own = jnp.stack([up_mine, to_core(up_mate)])
        up_far = to_chip_row(up_own)
        down_far = to_chip_row(w_down)
        top = swap_sequences(jnp.pad(grad_out, pad))
        grad_branch_mlp = centered(top.astype(f32)).astype(bf16)
        grad_mate = to_core(grad_branch_mlp)
        middle, normed_mlp = call(
            middle_kernel,
            "middle",
            (shape((rows, D), f32), shape((fsdp_count, rows, shard), bf16)),
            (place, attended, resid, w_out_all, vec),
            flops=2 * rows * D * D,
            scratch=[pltpu.VMEM((rows, D), f32)],
        )
        (
            branch_own,
            branch_give,
            norm_own,
            norm_give,
            down_keep,
            down_give,
            up_keep,
            up_give,
            bias_up_sum,
        ) = call(
            mlp_kernel,
            "mlp",
            (
                shape((rows, D), f32),
                shape((rows, D), bf16),
                shape((fsdp_count, rows, shard), f32),
                shape((fsdp_count, rows, shard), bf16),
                shape((PIECES, hidden // PIECES, D), bf16),
                shape((PIECES, hidden // PIECES, D), bf16),
                shape((PIECES, 2, 2, shard // PIECES, hidden), bf16),
                shape((PIECES, 2, 2, shard // PIECES, hidden), bf16),
                shape((2, hidden), f32),
            ),
            (
                place,
                normed_mlp,
                to_core(normed_mlp),
                grad_branch_mlp,
                grad_mate,
                up_own,
                up_far,
                w_down,
                down_far,
                bias_hidden,
            ),
            flops=48 * rows * D * hidden,
            exps=4 * rows * hidden,
            scratch=[pltpu.VMEM((rows, D), f32)] * 2,
        )
        norm_got = to_core(norm_give)
        branch_mlp = branch_own + to_core(branch_give) + vec[3:4]
        stream_out = (middle + centered(branch_mlp)).astype(bf16)
        piece = shard // PIECES
        grad_middle, grad_attended, out_chunk = call(
            branch_back_kernel,
            "branch_back",
            (
                shape((rows, D), f32),
                shape((ctx_count, GROUP_COLS, query_rows), bf16),
                shape((fsdp_count, PIECES, piece + EXTRA, D), bf16),
            ),
            (place, norm_own, norm_got, middle, top, attended, w_out_all, vec, bias_up_sum),
            flops=4 * rows * D * D,
        )
        grads = widened(group_all_to_all(grad_attended))
        dq, dk, dv = call(
            attend_back_kernel,
            "attend_back",
            (
                shape((ctx_count, width, GROUP_COLS), bf16),
                shape((ctx_count, rows, GROUP_COLS), bf16),
                shape((ctx_count, rows, GROUP_COLS), bf16),
            ),
            (place, queries_t, keys, values, keys_t, grads, outs, logs),
            flops=10 * HD * pairs,
            exps=pairs,
            scratch=[
                pltpu.VMEM((rows, GROUP_COLS), f32),
                pltpu.VMEM((rows, GROUP_COLS), f32),
                pltpu.VMEM((ctx_count, GROUP_COLS, width), f32),
                pltpu.VMEM((ctx_count, 1, GROUP_HEADS * width), f32),
            ],
        )
        dq = dq[:, :query_rows]

        keep_rows, give_rows, head_chunk = call(
            project_back_kernel,
            "project_back",
            (
                shape((half, rows, D), bf16),
                shape((half, rows, D), bf16),
                shape((fsdp_count, 2, shard // 2 + EXTRA, 3 * GROUP_COLS), bf16),
            ),
            (place, gathered, w_heads, gain, dq, dk, dv),
            flops=10 * tokens * D * GROUP_COLS,
            scratch=head_weights + [pltpu.VMEM((D, GROUP_COLS), f32)] * 3 + [pltpu.VMEM((8, D), f32)],
            grid=(ctx_count,),
            in_specs=[
                pl.BlockSpec(memory_space=pltpu.SMEM),
                block(rows, D),
                whole(fsdp_count, shard, 3 * GROUP_COLS),
                whole(1, D),
                block(query_rows, GROUP_COLS),
                block(rows, GROUP_COLS),
                block(rows, GROUP_COLS),
            ],
            out_specs=(
                pl.BlockSpec((1, rows, D), lambda at: (jnp.minimum(at, half - 1), 0, 0)),
                pl.BlockSpec((1, rows, D), lambda at: (jnp.maximum(at - half, 0), 0, 0)),
                whole(fsdp_count, 2, shard // 2 + EXTRA, 3 * GROUP_COLS),
            ),
        )
        both = keep_rows + to_core(give_rows)
        first, second = both[:, : rows // 2], both[:, rows // 2 :]
        second = jnp.stack([second[reversed_bits(slot)] for slot in range(half)])
        for step in reversed(range(steps)):
            keep = 1 << step
            got = (
                to_ctx(first[keep:], 1 << step),
                to_ctx(second[keep:], 1 << (steps - 1 - step)),
            )
            got = lax.optimization_barrier(got)
            first, second = first[:keep], second[:keep]
            if step:
                first, second = first + got[0], second + got[1]
        (grad_stream,) = call(
            stream_back_kernel,
            "stream_back",
            (shape((rows, D), bf16),),
            (place, first, got[0], second, got[1], resid, grad_middle, vec),
        )

        down = scatter_pieces(down_keep + to_chip_row(down_give))
        (grad_w_down,) = call(
            down_out_kernel, "down_out", (shape((hidden, D), f32),), (place, gather_pieces(down))
        )

        out_sum = out_chunk[:2] + to_core(out_chunk[2:])
        out_sum = out_sum[0] + to_chip_row(out_sum[1])
        up_sum = (up_keep + to_chip_row(up_give)).reshape(PIECES, 4 * piece, hidden)
        chunk = scatter_pieces(jnp.concatenate([up_sum, out_sum], axis=1))
        up_two = chunk[: 4 * piece].reshape(2, 2, piece, hidden)
        sums = chunk[5 * piece :].astype(f32)
        up_two = jnp.concatenate([up_two[0], to_core(up_two[1]), chunk[None, 4 * piece : 5 * piece]])
        grad_w_up, grad_w_out = call(
            up_out_kernel,
            "up_out",
            (shape((shard, fsdp_count * hidden), f32), shape((shard, D), f32)),
            (place, gather_pieces(up_two)),
        )

        heads_sum = head_chunk[:2] + to_core(head_chunk[2:])
        heads_sum = heads_sum[0] + to_chip_row(heads_sum[1])
        heads_sum = scatter_pieces(heads_sum, 2)
        grad_w_qkv, grad_gain_attn, grad_bias_qv = call(
            heads_out_kernel,
            "heads_out",
            (
                shape((shard, 3 * D), f32),
                shape((1, shard), f32),
                shape((1, 2 * shard), f32),
            ),
            (place, gather_pieces(heads_sum)),
        )

        return (
            swap_sequences(stream_out)[:, : D - 1],
            swap_sequences(grad_stream)[:, : D - 1].astype(f32),
            grad_gain_attn.reshape(-1),
            grad_w_qkv,
            grad_bias_qv.reshape(-1),
            grad_w_out,
            sums[0, :shard],
            sums[0, shard : 2 * shard],
            grad_w_up,
            sums[1],
            grad_w_down,
            sums[0, 2 * shard : 3 * shard],
        )

    rows_spec, matrix_spec, vector_spec = P(AXES, None), P("fsdp", None), P("fsdp")
    return jax.shard_map(
        local,
        mesh=mesh,
        in_specs=(
            rows_spec,
            vector_spec,
            matrix_spec,
            vector_spec,
            matrix_spec,
            vector_spec,
            vector_spec,
            matrix_spec,
            vector_spec,
            matrix_spec,
            vector_spec,
            rows_spec,
        ),
        out_specs=(
            rows_spec,
            rows_spec,
            vector_spec,
            matrix_spec,
            vector_spec,
            matrix_spec,
            vector_spec,
            vector_spec,
            matrix_spec,
            vector_spec,
            matrix_spec,
            vector_spec,
        ),
        check_vma=False,
    )
```

```python
import jax
import jax.numpy as jnp
from jax import lax
from jax.experimental import pallas as pl
from jax.experimental.pallas import tpu as pltpu
from jax.sharding import PartitionSpec as P

D = 768
H = 12
HD = 64
HEAD_GROUPS = 4
GROUP_HEADS = H // HEAD_GROUPS
GROUP_COLS = GROUP_HEADS * HD
HEAD_SCALE = HD ** (-0.5)
NORM_EPS = 1e-05
NEG_BIG = -1e30
GELU_A = 0.7978845608028654
GELU_B = 0.044715
LANES = 128
PIECES = 8
EXTRA = 8
AXES = ("fsdp", "ctx")
VMEM_LIMIT = 120 << 19
UNROLL_BLOCKS = 8

f32 = jnp.float32
bf16 = jnp.bfloat16


def dot(left, right):
    return lax.dot_general(left, right, (((1,), (0,)), ((), ())), preferred_element_type=f32)


def dot_tn(left, right):
    return lax.dot_general(left, right, (((0,), (0,)), ((), ())), preferred_element_type=f32)


def dot_nt(left, right):
    return lax.dot_general(left, right, (((1,), (1,)), ((), ())), preferred_element_type=f32)


def centered(branch):
    return branch - jnp.mean(branch, axis=1, keepdims=True)


def inverse_rms(stream):
    return lax.rsqrt(jnp.mean(stream * stream, axis=1, keepdims=True) + NORM_EPS)


def norm_back(grad, unit, inverse):
    return inverse * (grad - unit * jnp.mean(grad * unit, axis=1, keepdims=True))


def slab_at(relative):
    return ((relative & 1) << 1) | (relative >> 1)


def loop(start, stop, body, carried):
    if isinstance(start, int) and isinstance(stop, int) and stop - start <= UNROLL_BLOCKS:
        for at in range(start, stop):
            carried = body(at, carried)
        return carried
    return lax.fori_loop(start, stop, body, carried)


def call(body, name, outs, args, flops=0, exps=0, scratch=(), **grid):
    moved = sum(x.size * x.dtype.itemsize for x in tuple(args) + tuple(outs))
    specs = dict(
        in_specs=[pl.BlockSpec(memory_space=pltpu.SMEM)]
        + [pl.BlockSpec(memory_space=pltpu.VMEM)] * (len(args) - 1),
        out_specs=tuple(pl.BlockSpec(memory_space=pltpu.VMEM) for _ in outs),
    )
    specs.update(grid)
    return pl.pallas_call(
        body,
        out_shape=tuple(outs),
        scratch_shapes=list(scratch),
        compiler_params=pltpu.CompilerParams(vmem_limit_bytes=VMEM_LIMIT),
        cost_estimate=pl.CostEstimate(flops=flops, bytes_accessed=moved, transcendentals=exps),
        name=name,
        **specs,
    )(*args)


def shape(dims, kind):
    return jax.ShapeDtypeStruct(tuple(dims), kind)


def norm_kernel(place, x_ref, resid_ref, unit_ref):
    x = x_ref[...].astype(f32)
    resid_ref[:, : D - 1] = x
    resid_ref[:, D - 1 :] = -jnp.sum(x, axis=1, keepdims=True)
    resid = resid_ref[...]
    unit_ref[0] = (resid * inverse_rms(resid)).astype(bf16)


def cut_kernel(place, qkv_ref, up_ref, heads_ref, *slabs):
    group = place[0] % HEAD_GROUPS
    for at in range(HEAD_GROUPS):

        @pl.when(group == at)
        def _():
            for kind in range(3):
                start = kind * D + at * GROUP_COLS
                heads_ref[:, kind * GROUP_COLS : (kind + 1) * GROUP_COLS] = qkv_ref[
                    :, start : start + GROUP_COLS
                ]

    hidden = slabs[0].shape[1]
    for distance, slab in enumerate(slabs):
        at = pl.multiple_of((distance ^ place[1]) * hidden, LANES)
        slab[...] = up_ref[:, pl.ds(at, hidden)]


def load_heads(place, slab_refs, wq, wkv):
    shard = slab_refs[0].shape[0]
    for distance, slab_ref in enumerate(slab_refs):
        at = pl.ds(pl.multiple_of((distance ^ place[1]) * shard, shard), shard)
        wq[at, :] = slab_ref[:, :GROUP_COLS]
        wkv[at, :] = slab_ref[:, GROUP_COLS:]


def project(place, normed_ref, slots, base, bias_ref, k_ref, v_ref, vt_ref, qt_ref, wq, wkv):
    rows, query_rows = normed_ref.shape[1], qt_ref.shape[2]
    own = pl.ds(pl.multiple_of(place[2] * query_rows, query_rows), query_rows)
    for start in range(0, slots, 2):
        pair = range(start, min(start + 2, slots))
        normed = jnp.concatenate([normed_ref[slot] for slot in pair], axis=0)
        both = dot(normed, wkv[...])
        keys, values = both[:, :GROUP_COLS], both[:, GROUP_COLS:] + bias_ref[1:2, :]
        mine = jnp.concatenate([normed_ref[slot, own, :] for slot in pair], axis=0)
        queries = (dot(mine, wq[...]) + bias_ref[0:1, :]) * HEAD_SCALE
        for at, slot in enumerate(pair):
            here = slice(at * rows, (at + 1) * rows)
            k_ref[slot] = keys[here].astype(bf16)
            v_ref[slot] = values[here].astype(bf16)
            vt_ref[:, slot * rows : (slot + 1) * rows] = values[here].T.astype(bf16)
            qt_ref[slot] = queries[at * query_rows : (at + 1) * query_rows].T.astype(bf16)


def project_kernel(place, *refs):
    slabs, (gain_ref, bias_ref) = refs[:4], refs[4:6]
    pieces = refs[6:-7]
    normed_ref, k_ref, v_ref, vt_ref, qt_ref, wq, wkv = refs[-7:]
    load_heads(place, slabs, wq, wkv)
    gain = gain_ref[...]
    slot = 0
    for ref in pieces:
        for at in range(ref.shape[0]):
            normed_ref[slot] = (ref[at].astype(f32) * gain).astype(bf16)
            slot += 1
    project(place, normed_ref, slot, 0, bias_ref, k_ref, v_ref, vt_ref, qt_ref, wq, wkv)


def project_block_kernel(place, *refs):
    slabs, bias_ref, normed_ref = refs[:4], refs[4], refs[5]
    k_ref, v_ref, vt_ref, qt_ref, wq, wkv = refs[6:]

    @pl.when(pl.program_id(0) == 0)
    def _():
        load_heads(place, slabs, wq, wkv)

    slots = normed_ref.shape[0]
    project(place, normed_ref, slots, 0, bias_ref, k_ref, v_ref, vt_ref, qt_ref, wq, wkv)


def collect_kernel(place, normed_ref, k_ref, normed_t_ref, query_t_ref, kt_ref):
    blocks, rows, _ = k_ref.shape
    query_rows = query_t_ref.shape[1] // blocks
    own = pl.ds(pl.multiple_of(place[2] * query_rows, query_rows), query_rows)
    for slot in range(blocks):
        tokens = slice(slot * rows, (slot + 1) * rows)
        normed_t_ref[:, tokens] = normed_ref[slot].T
        query_t_ref[:, slot * query_rows : (slot + 1) * query_rows] = normed_ref[slot, own, :].T
        kt_ref[:, tokens] = k_ref[slot].T


def by_head(value):
    head = lax.broadcasted_iota(jnp.int32, value.shape, 0) // HD
    zero = jnp.zeros_like(value)
    return jnp.concatenate([jnp.where(head == at, value, zero) for at in range(GROUP_HEADS)], axis=1)


def attend_kernel(place, qt_ref, k_ref, vt_ref, out_ref, log_ref):
    blocks, _, width = qt_ref.shape
    rows = k_ref.shape[1]
    member = place[0]

    def one_query_block(block, _):
        queries = by_head(qt_ref[block ^ member])

        def one_key_block(key_block, carried):
            top, total, accs = carried
            slot = key_block ^ member
            at = pl.multiple_of(slot * rows, rows)
            scores = dot(k_ref[slot], queries)
            new_top = jnp.maximum(top, jnp.max(scores, axis=0, keepdims=True))
            weights = jnp.exp(scores - new_top)
            fading = jnp.exp(top - new_top)
            total = total * fading + jnp.sum(weights, axis=0, keepdims=True)
            low = weights.astype(bf16)
            kept = []
            for head in range(GROUP_HEADS):
                lanes = slice(head * width, (head + 1) * width)
                values = vt_ref[head * HD : (head + 1) * HD, pl.ds(at, rows)]
                kept.append(accs[head] * fading[:, lanes] + dot(values, low[:, lanes]))
            return new_top, total, tuple(kept)

        start_state = (
            jnp.full((1, GROUP_HEADS * width), NEG_BIG, f32),
            jnp.zeros((1, GROUP_HEADS * width), f32),
            tuple(jnp.zeros((HD, width), f32) for _ in range(GROUP_HEADS)),
        )
        top, total, accs = loop(0, block + 1, one_key_block, start_state)
        for head in range(GROUP_HEADS):
            lanes = slice(head * width, (head + 1) * width)
            out_ref[block, head * HD : (head + 1) * HD, :] = (accs[head] / total[:, lanes]).astype(bf16)
        log_ref[block] = top + jnp.log(total)
        return 0

    loop(0, blocks, one_query_block, 0)


def attend_back_kernel(
    place, qt_ref, k_ref, v_ref, kt_ref, gt_ref, out_ref, log_ref, dq_ref, dkv_ref, sum_ref, dk_acc, dv_acc, dq_acc, delta_ref
):
    blocks, _, width = qt_ref.shape
    rows = k_ref.shape[1]
    member = place[0]

    def prepare(block, _):
        products = gt_ref[block].astype(f32) * out_ref[block].astype(f32)
        for head in range(GROUP_HEADS):
            delta_ref[block, :, head * width : (head + 1) * width] = jnp.sum(
                products[head * HD : (head + 1) * HD], axis=0, keepdims=True
            )
        return 0

    lax.fori_loop(0, blocks, prepare, 0)
    dq_acc[...] = jnp.zeros_like(dq_acc)
    sum_ref[...] = jnp.zeros_like(sum_ref)

    def one_key_block(key_block, _):
        slot = key_block ^ member
        at = pl.multiple_of(slot * rows, rows)
        dk_acc[...] = jnp.zeros_like(dk_acc)
        dv_acc[...] = jnp.zeros_like(dv_acc)

        def one_query_block(block, _):
            queries, grads = by_head(qt_ref[block ^ member]), by_head(gt_ref[block])
            prob = jnp.exp(dot(k_ref[slot], queries) - log_ref[block])
            grad_prob = dot(v_ref[slot], grads)
            grad_scores = (prob * (grad_prob - delta_ref[block])).astype(bf16)
            dv_acc[...] += dot_nt(prob.astype(bf16), grads)
            dk_acc[...] += dot_nt(grad_scores, queries)
            for head in range(GROUP_HEADS):
                part = slice(head * HD, (head + 1) * HD)
                lanes = slice(head * width, (head + 1) * width)
                dq_acc[block, part, :] += dot(kt_ref[part, pl.ds(at, rows)], grad_scores[:, lanes])
            return 0

        loop(key_block, blocks, one_query_block, 0)
        dkv_ref[slot] = jnp.concatenate([dk_acc[...], dv_acc[...]], axis=1).astype(bf16)
        sum_ref[1:2, :] += jnp.sum(dv_acc[...], axis=0, keepdims=True)
        return 0

    loop(0, blocks, one_key_block, 0)

    def write(block, _):
        grads = dq_acc[block].T * HEAD_SCALE
        dq_ref[block ^ member] = grads.astype(bf16)
        sum_ref[0:1, :] += jnp.sum(grads, axis=0, keepdims=True)
        return 0

    lax.fori_loop(0, blocks, write, 0)


def middle_kernel(
    place, att_ref, resid_ref, vec_ref, slab0, slab1, slab2, slab3, middle_ref, normed_ref, branch
):
    query_rows = att_ref.shape[2]
    for split in range(att_ref.shape[0] // HEAD_GROUPS):
        total = None
        for distance, slab_ref in enumerate((slab0, slab1, slab2, slab3)):
            part = dot_tn(att_ref[split * HEAD_GROUPS + (distance ^ place[1])], slab_ref[...])
            total = part if total is None else total + part
        branch[split * query_rows : (split + 1) * query_rows, :] = total
    middle = resid_ref[...] + centered(branch[...] + vec_ref[1:2, :])
    middle_ref[...] = middle
    normed_ref[...] = (middle * inverse_rms(middle) * vec_ref[2:3, :]).astype(bf16)


def mlp_kernel(place, *refs):
    normed, grads, slabs = refs[:4], refs[4:8], refs[8:12]
    down_ref, bias_ref = refs[12:14]
    branch_own, branch_far, branch_give, norm_own, norm_far, norm_give = refs[14:20]
    downs, ups, (bias_grad, weight, down_total, up_total) = refs[20:24], refs[24:28], refs[28:]
    rows = normed[0].shape[0]
    shard, wide = slabs[0].shape[0], down_ref.shape[0] // PIECES
    piece = shard // PIECES
    mine, low = place[1], place[3]
    for distance, slab in enumerate(slabs):
        at = pl.multiple_of((distance ^ mine) * shard, shard)
        weight[pl.ds(at, shard), :] = slab[...]
    for tile in range(2):
        blocks = (tile, 2 + tile)
        tokens = jnp.concatenate([normed[at][...] for at in blocks], axis=0)
        grad = jnp.concatenate([grads[at][...] for at in blocks], axis=0)
        hidden = dot(tokens, weight[...]) + bias_ref[...]
        square = hidden * hidden
        bent = jnp.tanh(GELU_A * hidden * (1.0 + GELU_B * square))
        half = 0.5 * (1.0 + bent)
        active = (hidden * half).astype(bf16)
        slope = half + 0.5 * hidden * (1.0 - bent * bent) * (GELU_A * (1.0 + 3.0 * GELU_B * square))
        grad_hidden = (dot_nt(grad, down_ref[...]) * slope).astype(bf16)
        norm, branch = dot_nt(grad_hidden, weight[...]), dot(active, down_ref[...])
        for at in range(2):
            here = slice(at * rows, (at + 1) * rows)
            if tile:
                norm_give[at], branch_give[at] = norm[here].astype(bf16), branch[here].astype(bf16)
            else:
                (norm_own, norm_far)[at][...] = norm[here]
                (branch_own, branch_far)[at][...] = branch[here]
        down, up = dot_tn(active, grad), dot_tn(tokens, grad_hidden)
        bias = jnp.sum(grad_hidden.astype(f32), axis=0, keepdims=True)
        if tile == 0:
            down_total[...], up_total[...], bias_grad[...] = down, up, bias
        else:
            down_total[...] += down
            up_total[...] += up
            bias_grad[...] += bias
    for near, (down_ref, up_ref) in enumerate(zip(downs, ups)):
        for side in range(2):
            at = (side << 2 | near) ^ low
            down_ref[side] = down_total[pl.ds(pl.multiple_of(at * wide, wide), wide), :].astype(bf16)
            for distance in range(4):
                here = pl.multiple_of((distance ^ mine) * shard + at * piece, piece)
                up_ref[side, distance] = up_total[pl.ds(here, piece), :].astype(bf16)


def branch_back_kernel(
    place,
    own_ref,
    core_ref,
    far_ref,
    middle_ref,
    top_ref,
    vec_ref,
    slab0,
    slab1,
    slab2,
    slab3,
    grad_middle_ref,
    grad_branch_ref,
    ga_ref,
    sum_ref,
):
    query_rows = ga_ref.shape[2]
    rows = top_ref.shape[0]
    grad = own_ref[...] + core_ref[0].astype(f32) + far_ref[...].astype(f32)
    middle = middle_ref[...]
    inverse = inverse_rms(middle)
    unit = middle * inverse
    sum_ref[0:1, :] = jnp.sum(grad * unit, axis=0, keepdims=True)
    grad_top = jnp.concatenate([top_ref[...].astype(f32), jnp.zeros((rows, 1), f32)], axis=1)
    grad_middle = grad_top + norm_back(grad * vec_ref[2:3, :], unit, inverse)
    grad_middle_ref[...] = grad_middle
    grad_branch = centered(grad_middle).astype(bf16)
    grad_branch_ref[...] = grad_branch
    for distance, slab_ref in enumerate((slab0, slab1, slab2, slab3)):
        product = dot_nt(slab_ref[...], grad_branch).astype(bf16)
        for split in range(ga_ref.shape[0] // HEAD_GROUPS):
            at = split * HEAD_GROUPS + (distance ^ place[1])
            ga_ref[at] = product[:, split * query_rows : (split + 1) * query_rows]
    sum_ref[1:2, :] = jnp.sum(grad_branch.astype(f32), axis=0, keepdims=True)
    sum_ref[2:3, :] = jnp.sum(centered(grad_top).astype(bf16).astype(f32), axis=0, keepdims=True)


def out_back_kernel(place, att_ref, grad_ref, sum_ref, bias_up_ref, near_ref, far_ref, grad_w):
    query_rows = att_ref.shape[2]
    groups, piece = HEAD_GROUPS, near_ref.shape[2] - EXTRA
    shard = D // groups
    mine, low = place[1], place[3]
    empty = jnp.zeros((1, D - 3 * shard), f32)
    for group in range(groups):
        weight = None
        for split in range(att_ref.shape[0] // groups):
            product = dot(
                att_ref[split * groups + group], grad_ref[split * query_rows : (split + 1) * query_rows, :]
            )
            weight = product if weight is None else weight + product
        lanes = slice(group * shard, (group + 1) * shard)
        grad_w[group * shard : (group + 1) * shard, :] = weight
        row = [sum_ref[at : at + 1, lanes] for at in (1, 0, 2)]
        grad_w[D + group : D + group + 1, :] = jnp.concatenate(row + [empty], axis=1)
    for distance in range(4):
        far, core = distance >> 1, distance & 1
        row = grad_w[pl.ds(D + (distance ^ mine), 1), :]
        up_row = jnp.zeros_like(row) if distance else bias_up_ref[...]
        extra = jnp.concatenate([row, up_row, jnp.zeros((EXTRA - 2, D), f32)], axis=0)
        for near in range(4):
            for side in range(2):
                at = (distance ^ mine) * shard + ((side << 2 | near) ^ low) * piece
                part = grad_w[pl.ds(pl.multiple_of(at, piece), piece), :]
                target = (near_ref, far_ref)[core]
                target[far, near * 2 + side] = jnp.concatenate([part, extra], axis=0).astype(bf16)


def sum_kernel(place, *refs):
    firsts, seconds, targets = refs[:4], refs[4:8], refs[8:]
    wide = firsts[0].shape[1]
    for side, target in enumerate(targets):
        target[:wide, :] = sum(ref[side].astype(f32) for ref in firsts).astype(bf16)
        target[wide:, :] = sum(ref[side].astype(f32) for ref in seconds).astype(bf16)


def arrange_heads(place, q_ref, kv_ref, sum_ref, near_ref, far_ref):
    mine, piece = place[1], near_ref.shape[2] - EXTRA
    shard = 2 * piece
    group = place[0] % HEAD_GROUPS
    for row in range(D // shard):
        relative = row ^ mine
        first = jnp.where(group // 2 == row, sum_ref[0:1, :], 0.0)
        second = jnp.where(2 + group // 2 == row, sum_ref[1:2, :], 0.0)
        extra = jnp.concatenate([first, second, jnp.zeros_like(first)], axis=1)
        extra = jnp.concatenate([extra, jnp.zeros((EXTRA - 1, extra.shape[1]), f32)], axis=0)
        for part in range(2):
            at_row = slice(row * shard + part * piece, row * shard + (part + 1) * piece)
            block = jnp.concatenate([q_ref[at_row, :], kv_ref[at_row, :]], axis=1)
            both = jnp.concatenate([block, extra], axis=0).astype(bf16)
            for core, target in enumerate((near_ref, far_ref)):

                @pl.when((relative & 1) == core)
                def _():
                    target[relative >> 1, part ^ ((place[3] >> 2) & 1)] = both


def project_back_kernel(
    place,
    normed_t_ref,
    query_t_ref,
    dq_ref,
    dkv_ref,
    sum_ref,
    slab0,
    slab1,
    slab2,
    slab3,
    keep_ref,
    give_ref,
    near_ref,
    far_ref,
    wq,
    wkv,
    aq,
    akv,
):
    load_heads(place, (slab0, slab1, slab2, slab3), wq, wkv)
    blocks, query_rows, _ = dq_ref.shape
    rows = dkv_ref.shape[1]
    half = keep_ref.shape[0]
    own = pl.ds(pl.multiple_of(place[2] * query_rows, query_rows), query_rows)
    aq[...] = jnp.zeros_like(aq)
    akv[...] = jnp.zeros_like(akv)
    chunk = min(blocks, max(4, LANES // query_rows))

    def one(at, _):
        start = at * chunk
        dkv = jnp.concatenate([dkv_ref[start + k] for k in range(chunk)], axis=0)
        dq = jnp.concatenate([dq_ref[start + k] for k in range(chunk)], axis=0)
        tokens = pl.ds(pl.multiple_of(start * rows, chunk * rows), chunk * rows)
        queries = pl.ds(pl.multiple_of(start * query_rows, chunk * query_rows), chunk * query_rows)
        akv[...] += dot(normed_t_ref[:, tokens], dkv)
        aq[...] += dot(query_t_ref[:, queries], dq)
        return 0

    loop(0, blocks // chunk, one, 0)
    arrange_heads(place, aq, akv, sum_ref, near_ref, far_ref)

    for core, ref in enumerate((keep_ref, give_ref)):

        def two(at, _, core=core, ref=ref):
            slot = at + core * half
            grad = dot_nt(dkv_ref[slot], wkv[...])
            ref[at] = grad.astype(bf16)
            low = ref[at, own, :].astype(f32)
            ref[at, own, :] = (low + dot_nt(dq_ref[slot], wq[...])).astype(bf16)
            return 0

        loop(0, half, two, 0)


def stream_back_kernel(place, part0, part1, part2, part3, resid_ref, grad_middle_ref, vec_ref, out_ref):
    grad = sum(part[...].astype(f32) for part in (part0, part1, part2, part3))
    resid = resid_ref[...]
    inverse = inverse_rms(resid)
    unit = resid * inverse
    total = grad_middle_ref[...] + norm_back(grad * vec_ref[0:1, :], unit, inverse)
    out_ref[...] = (total - total[:, D - 1 :]).astype(bf16)[:, : D - 1]


def down_out_kernel(place, part0, part1, part2, part3, down_ref, out_ref):
    wide, rows = down_ref.shape[0] // PIECES, out_ref.shape[0] // PIECES
    for near, part in enumerate((part0, part1, part2, part3)):
        for side in range(2):
            at = (side << 2 | near) ^ place[3]
            down_ref[pl.ds(pl.multiple_of(at * wide, wide), wide), :] = part[side, :wide].astype(f32)
            out_ref[pl.ds(pl.multiple_of(at * rows, rows), rows), :] = part[side, wide:].astype(f32)


def up_out_kernel(place, part0, part1, part2, part3, up_ref):
    rows = part0.shape[2]
    for near, part in enumerate((part0, part1, part2, part3)):
        for side in range(2):
            at = pl.multiple_of(((side << 2 | near) ^ place[3]) * rows, rows)
            for slab in range(4):
                col = pl.multiple_of((slab ^ place[1]) * D, LANES)
                up_ref[pl.ds(at, rows), pl.ds(col, D)] = part[side, slab].astype(f32)


def heads_out_kernel(place, part0, part1, part2, part3, weight_ref, out_ref, gain_ref, bias_ref, pieces):
    piece = part0.shape[1] - EXTRA
    mine, low = place[1], place[3]
    for near, part in enumerate((part0, part1, part2, part3)):
        pieces[near] = part[...]
    for part in range(2):
        for group in range(HEAD_GROUPS):
            value = pieces[(group ^ low) & 3, part ^ ((low >> 2) & 1)].astype(f32)
            for kind in range(3):
                start = kind * D + group * GROUP_COLS
                out_ref[part * piece : (part + 1) * piece, start : start + GROUP_COLS] = value[
                    :piece, kind * GROUP_COLS : (kind + 1) * GROUP_COLS
                ]
    gain_ref[...] = jnp.sum(out_ref[...] * weight_ref[...].astype(f32), axis=1, keepdims=True)
    sides = []
    for side in range(2):
        group = ((2 * mine) & 3) + side
        value = pieces[(group ^ low) & 3, 0].astype(f32)[piece : piece + 1]
        sides.append(jnp.where(mine < 2, value[:, :GROUP_COLS], value[:, GROUP_COLS : 2 * GROUP_COLS]))
    bias_ref[...] = jnp.concatenate(sides, axis=1)


def solution(mesh):
    fsdp_count, ctx_count = mesh.shape["fsdp"], mesh.shape["ctx"]
    half = ctx_count // 2
    steps = half.bit_length() - 1
    ctx_steps = steps + 1
    splits = ctx_count // HEAD_GROUPS
    shard = D // fsdp_count

    def send(value, target):
        pairs = []
        for source in range(fsdp_count * ctx_count):
            row, at = target(*divmod(source, ctx_count))
            pairs.append((source, row * ctx_count + at))
        return lax.ppermute(value, AXES, pairs)

    def to_core(value):
        return send(value, lambda row, at: (row ^ 1, at))

    def to_chip_row(value):
        return send(value, lambda row, at: (row ^ 2, at))

    def to_ctx(value, bit):
        return send(value, lambda row, at: (row, at ^ bit))

    def swap_sequences(value):
        return send(
            value, lambda row, at: (row, at) if (row & 1) == at // half else (row ^ 1, at ^ half)
        )

    groups = [
        [(row + core) * ctx_count + side * half + at for core in range(2) for at in range(half)]
        for row in range(0, fsdp_count, 2)
        for side in range(2)
    ]

    def group_all_to_all(value):
        return lax.all_to_all(value, AXES, 0, 0, axis_index_groups=groups, tiled=True)

    def to_fsdp(value, distance):
        return send(value, lambda row, at: (row ^ distance, at))

    def over_fsdp(value):
        far = to_chip_row(value)
        return value, to_core(value), far, to_core(far)

    def to_square(values):
        return tuple(to_ctx(value, near + 1) for near, value in enumerate(values))

    def gather_square(value):
        pair = jnp.stack([value, to_ctx(value, 4)])
        return (pair, *to_square((pair,) * 3))

    def over_rest(value):
        for step in range(3, ctx_steps):
            value = value + to_ctx(value, 1 << step)
        return value

    together = lax.optimization_barrier

    def widened(value):
        width = value.shape[-1]
        return value if width >= LANES else jnp.pad(value, ((0, 0), (0, 0), (0, LANES - width)))

    def local(
        stream_in,
        gain_attn,
        w_qkv,
        bias_qv,
        w_out,
        bias_out,
        gain_mlp,
        w_up,
        bias_up,
        w_down,
        bias_down,
        grad_out,
    ):
        rows = stream_in.shape[0]
        query_rows = rows // splits
        width = max(query_rows, LANES)
        fsdp_at, ctx_at = lax.axis_index("fsdp"), lax.axis_index("ctx")
        core, inner = fsdp_at & 1, ctx_at % half
        member = core * half + inner
        head_group = inner % HEAD_GROUPS
        place = jnp.stack([member, fsdp_at, member // HEAD_GROUPS, ctx_at & 7]).astype(jnp.int32)

        hidden = w_down.shape[0]
        stream = swap_sequences(stream_in)
        w_part, *up_sent = call(
            cut_kernel,
            "cut",
            (
                shape((shard, 3 * GROUP_COLS), bf16),
                *(shape((shard, hidden), bf16) for _ in range(fsdp_count)),
            ),
            (place, w_qkv, w_up),
        )
        vectors = jnp.concatenate(
            [
                part.astype(f32).reshape(1, -1)
                for part in (gain_attn, bias_out, gain_mlp, bias_down, bias_qv, bias_up)
            ],
            axis=1,
        )
        far_heads, far_vectors = together((to_chip_row(w_part), to_chip_row(vectors)))
        w_heads = (w_part, to_core(w_part), far_heads, to_core(far_heads))
        vectors = (vectors, to_core(vectors), far_vectors, to_core(far_vectors))
        far_heads, w_out_sent, stream = together((far_heads, w_out, stream))

        resid, unit = call(
            norm_kernel,
            "norm",
            (shape((rows, D), f32), shape((1, rows, D), bf16)),
            (place, stream),
        )
        got = to_square((unit,) * 3)
        *got, out_far = together((*got, to_chip_row(w_out_sent)))
        pieces = [unit, *got]
        for bit in range(2, steps):
            pieces.append(to_ctx(jnp.concatenate(pieces), 1 << bit))
        pieces = pieces + [to_core(piece) for piece in pieces]

        def by_row(values):
            ordered = []
            for row in range(fsdp_count):
                first = jnp.where((fsdp_at ^ row) & 1 == 0, values[0], values[1])
                second = jnp.where((fsdp_at ^ row) & 1 == 0, values[2], values[3])
                ordered.append(jnp.where((fsdp_at ^ row) < 2, first, second))
            return jnp.concatenate(ordered)

        vectors = by_row(vectors)
        vec = vectors[:, :D].reshape(fsdp_count, 4, shard).transpose(1, 0, 2).reshape(4, D)
        bias_heads = vectors[:, D : D + 2 * shard].reshape(2, HEAD_GROUPS, GROUP_COLS)
        bias_heads = lax.dynamic_index_in_dim(bias_heads, head_group, 1, keepdims=False)
        bias_hidden = lax.dynamic_slice_in_dim(vectors[:, D + 2 * shard :], fsdp_at, 1)
        gain = vec[0:1]

        head_weights = [pltpu.VMEM((D, GROUP_COLS), bf16), pltpu.VMEM((D, 2 * GROUP_COLS), bf16)]
        tokens = ctx_count * rows
        projected = (
            shape((ctx_count, rows, GROUP_COLS), bf16),
            shape((ctx_count, rows, GROUP_COLS), bf16),
            shape((GROUP_COLS, tokens), bf16),
            shape((ctx_count, GROUP_COLS, query_rows), bf16),
        )
        work = 5 * tokens * D * GROUP_COLS
        if 4 * tokens * D * 2 < VMEM_LIMIT:
            normed, keys, values, values_t, queries_t = call(
                project_kernel,
                "project",
                (shape((ctx_count, rows, D), bf16), *projected),
                (place, *w_heads, gain, bias_heads, *pieces),
                flops=work,
                scratch=head_weights,
            )
        else:
            normed = (jnp.concatenate(pieces).astype(f32) * gain).astype(bf16)
            block = lambda *dims: pl.BlockSpec((1,) + dims, lambda at: (at, 0, 0))
            whole = lambda *dims: pl.BlockSpec(dims, lambda at: (0,) * len(dims))
            keys, values, values_t, queries_t = call(
                project_block_kernel,
                "project",
                projected,
                (place, *w_heads, bias_heads, normed),
                flops=work,
                scratch=head_weights,
                grid=(ctx_count,),
                in_specs=[pl.BlockSpec(memory_space=pltpu.SMEM)]
                + [whole(shard, 3 * GROUP_COLS)] * 4
                + [whole(2, GROUP_COLS), block(rows, D)],
                out_specs=(
                    block(rows, GROUP_COLS),
                    block(rows, GROUP_COLS),
                    pl.BlockSpec((GROUP_COLS, rows), lambda at: (0, at)),
                    block(GROUP_COLS, query_rows),
                ),
            )
        queries_t = widened(queries_t)
        pairs = GROUP_HEADS * query_rows * rows * ctx_count * (ctx_count + 1) // 2
        outs, logs = call(
            attend_kernel,
            "attend",
            (
                shape((ctx_count, GROUP_COLS, width), bf16),
                shape((ctx_count, 1, GROUP_HEADS * width), f32),
            ),
            (place, queries_t, keys, values_t),
            flops=4 * HD * pairs,
            exps=pairs,
        )
        outs, *up_got = together(
            (outs, *(to_fsdp(up_sent[distance], distance) for distance in (1, 2, 3)))
        )
        attended = group_all_to_all(outs[:, :, :query_rows])
        if 4 * tokens * D * 2 < VMEM_LIMIT:
            normed_t, query_t, keys_t = call(
                collect_kernel,
                "collect",
                (
                    shape((D, tokens), bf16),
                    shape((D, ctx_count * query_rows), bf16),
                    shape((GROUP_COLS, tokens), bf16),
                ),
                (place, normed, keys),
            )
        else:
            normed_query = lax.dynamic_index_in_dim(
                normed.reshape(ctx_count, splits, query_rows, D), place[2], 1, keepdims=False
            )
            normed_t, query_t = normed.reshape(tokens, D).T, normed_query.reshape(-1, D).T
            keys_t = keys.reshape(tokens, GROUP_COLS).T
        attended, normed_t, query_t, keys_t = together((attended, normed_t, query_t, keys_t))

        w_out_all = (w_out, to_core(w_out), out_far, to_core(out_far))
        top = swap_sequences(grad_out)
        grad_result = jnp.pad(top.astype(f32), ((0, 0), (0, 1)))
        grad_branch_mlp = centered(grad_result).astype(bf16)
        grads_mlp = over_fsdp(grad_branch_mlp)
        middle, normed_mlp = call(
            middle_kernel,
            "middle",
            (shape((rows, D), f32), shape((rows, D), bf16)),
            (place, attended, resid, vec, *w_out_all),
            flops=2 * rows * D * D,
            scratch=[pltpu.VMEM((rows, D), f32)],
        )
        piece = shard // PIECES
        (
            branch_own,
            branch_far,
            branch_give,
            norm_own,
            norm_far,
            norm_give,
            *both_sums,
            bias_up_sum,
        ) = call(
            mlp_kernel,
            "mlp",
            (
                shape((rows, D), f32),
                shape((rows, D), f32),
                shape((2, rows, D), bf16),
                shape((rows, D), f32),
                shape((rows, D), f32),
                shape((2, rows, D), bf16),
                *(shape((2, hidden // PIECES, D), bf16) for _ in range(4)),
                *(shape((2, fsdp_count, piece, hidden), bf16) for _ in range(4)),
                shape((1, hidden), f32),
            ),
            (
                place,
                *over_fsdp(normed_mlp),
                *grads_mlp,
                up_sent[0],
                *up_got,
                w_down,
                bias_hidden,
            ),
            flops=48 * rows * D * hidden,
            exps=4 * rows * hidden,
            scratch=[
                pltpu.VMEM((D, hidden), bf16),
                pltpu.VMEM((hidden, D), f32),
                pltpu.VMEM((D, hidden), f32),
            ],
        )
        norm_got = to_core(norm_give)
        norm_far_got = to_chip_row((norm_far + norm_got[1]).astype(bf16))
        down_sums, up_sums = both_sums[:4], both_sums[4:]
        norm_far_got, *down_got = together((norm_far_got, *to_square(down_sums[1:])))
        down_keep, down_give = (
            sum((part[side] for part in down_got), start=down_sums[0][side]) for side in range(2)
        )
        grad_middle, grad_branch, grad_attended, row_sums = call(
            branch_back_kernel,
            "branch_back",
            (
                shape((rows, D), f32),
                shape((rows, D), bf16),
                shape((ctx_count, GROUP_COLS, query_rows), bf16),
                shape((8, D), f32),
            ),
            (place, norm_own, norm_got, norm_far_got, middle, top, vec, *w_out_all),
            flops=4 * rows * D * D,
        )
        grads = group_all_to_all(grad_attended)
        out_near, out_give = call(
            out_back_kernel,
            "out_back",
            (shape((2, PIECES, piece + EXTRA, D), bf16), shape((2, PIECES, piece + EXTRA, D), bf16)),
            (place, attended, grad_branch, row_sums, bias_up_sum),
            flops=2 * rows * D * D,
            scratch=[pltpu.VMEM((D + 8, D), f32)],
        )
        out_sum = out_near + to_core(out_give)
        branch_got = to_core(branch_give)
        branch_far_got = to_chip_row((branch_far + branch_got[1]).astype(bf16))
        branch_mlp = branch_own + branch_got[0] + branch_far_got + vec[3:4]
        stream_out = (middle + centered(branch_mlp)).astype(bf16)[:, : D - 1]
        grads, out_sum = together((grads, out_sum))
        out_got = to_chip_row(out_sum[1])
        up_got = to_square(up_sums[1:])
        down_got = to_ctx(down_give, 4)
        dq, dkv, head_sums = call(
            attend_back_kernel,
            "attend_back",
            (
                shape((ctx_count, width, GROUP_COLS), bf16),
                shape((ctx_count, rows, 2 * GROUP_COLS), bf16),
                shape((8, GROUP_COLS), f32),
            ),
            (place, queries_t, keys, values, keys_t, widened(grads), outs, logs),
            flops=10 * HD * pairs,
            exps=pairs,
            scratch=[
                pltpu.VMEM((rows, GROUP_COLS), f32),
                pltpu.VMEM((rows, GROUP_COLS), f32),
                pltpu.VMEM((ctx_count, GROUP_COLS, width), f32),
                pltpu.VMEM((ctx_count, 1, GROUP_HEADS * width), f32),
            ],
        )
        dq = dq[:, :query_rows]
        dq, dkv, out_got, down_got, *up_got = together((dq, dkv, out_got, down_got, *up_got))
        up_keep, up_give = (
            sum((part[side] for part in up_got), start=up_sums[0][side]) for side in range(2)
        )
        out_sums = [
            out_sum[0, 2 * near : 2 * near + 2] + out_got[2 * near : 2 * near + 2] for near in range(4)
        ]
        dq, dkv, up_give, *out_sums = together((dq, dkv, up_give, *out_sums))
        up_got = to_ctx(up_give, 4)
        out_got = to_square(out_sums[1:])

        row_shapes = (shape((half, rows, D), bf16), shape((half, rows, D), bf16))
        head_shapes = tuple(
            shape((2, 2, shard // 2 + EXTRA, 3 * GROUP_COLS), bf16) for _ in range(2)
        )
        if 4 * tokens * D * 2 < VMEM_LIMIT:
            keep_rows, give_rows, head_near, head_give = call(
                project_back_kernel,
                "project_back",
                row_shapes + head_shapes,
                (place, normed_t, query_t, dq, dkv, head_sums, *w_heads),
                flops=2 * work,
                scratch=head_weights
                + [pltpu.VMEM((D, GROUP_COLS), f32), pltpu.VMEM((D, 2 * GROUP_COLS), f32)],
            )
        else:
            weights = by_row(w_heads)
            flat_q, flat_kv = dq.reshape(-1, GROUP_COLS), dkv.reshape(tokens, 2 * GROUP_COLS)
            grad_rows = dot_nt(flat_kv, weights[:, GROUP_COLS:]).reshape(
                ctx_count, splits, query_rows, D
            )
            grad_query = dot_nt(flat_q, weights[:, :GROUP_COLS]).reshape(ctx_count, 1, query_rows, D)
            chosen = (jnp.arange(splits) == place[2])[None, :, None, None]
            grad_rows = (grad_rows + jnp.where(chosen, grad_query, 0.0)).astype(bf16)
            grad_rows = grad_rows.reshape(ctx_count, rows, D)
            keep_rows, give_rows = grad_rows[:half], grad_rows[half:]
            head_near, head_give = call(
                arrange_heads,
                "arrange_heads",
                head_shapes,
                (place, dot(query_t, flat_q), dot(normed_t, flat_kv), head_sums),
            )
        keep_rows, up_got, *out_got = together((keep_rows, up_got, *out_got))
        head_got, rows_got = together((to_core(head_give), to_core(give_rows)))
        head_sum = head_near + head_got
        head_got = to_chip_row(head_sum[1])
        if steps == 2:
            parts = [keep_rows[slot] + rows_got[slot] for slot in range(4)]
        else:
            both = keep_rows + rows_got
            for bit in reversed(range(2, steps)):
                both = both[: 1 << bit] + to_ctx(both[1 << bit :], 1 << bit)
            parts = [both[slot] for slot in range(4)]
        rows_got = to_square(parts[1:])
        out_keep, out_give = (
            sum((part[side] for part in out_got), start=out_sums[0][side]) for side in range(2)
        )
        out_got = to_ctx(out_give, 4)
        down, up_rows = over_rest(down_keep + down_got), over_rest(up_keep + up_got)
        up_got = [to_fsdp(up_rows[distance], distance) for distance in (1, 2, 3)]

        head_got, out_got, *up_got = together((head_got, out_got, *up_got))
        head_sum = head_sum[0] + head_got
        head_got = to_ctx(head_sum[1], 4)
        ups = jnp.stack([up_rows[0], *up_got])
        up_got = to_ctx(ups, 4)
        out_rows = over_rest(out_keep + out_got)
        sums = out_rows[piece:].astype(f32)
        downs = jnp.concatenate([down, out_rows[:piece]])
        down_got = to_ctx(downs, 4)

        *rows_got, head_got, up_got, down_got = together((*rows_got, head_got, up_got, down_got))
        (grad_stream,) = call(
            stream_back_kernel,
            "stream_back",
            (shape((rows, D - 1), bf16),),
            (place, parts[0], *rows_got, resid, grad_middle, vec),
        )
        grad_stream = swap_sequences(grad_stream)
        heads = over_rest(head_sum[0] + head_got)
        head_got = to_ctx(heads, 4)
        downs = jnp.stack([downs, down_got])
        downs = (downs, *to_square((downs,) * 3))
        ups = jnp.stack([ups, up_got])
        ups = (ups, *to_square((ups,) * 3))
        heads = jnp.stack([heads, head_got])
        heads = (heads, *to_square((heads,) * 3))
        grad_w_qkv, grad_gain_attn, grad_bias_qv = call(
            heads_out_kernel,
            "heads_out",
            (
                shape((shard, 3 * D), f32),
                shape((shard, 1), f32),
                shape((1, 2 * shard), f32),
            ),
            (place, *heads, w_qkv),
            scratch=[pltpu.VMEM((4, 2, shard // 2 + EXTRA, 3 * GROUP_COLS), bf16)],
        )
        grad_w_down, grad_w_out = call(
            down_out_kernel,
            "down_out",
            (shape((hidden, D), f32), shape((shard, D), f32)),
            (place, *downs),
        )
        (grad_w_up,) = call(
            up_out_kernel, "up_out", (shape((shard, fsdp_count * hidden), f32),), (place, *ups)
        )

        return (
            swap_sequences(stream_out),
            grad_stream.astype(f32),
            grad_gain_attn.reshape(-1) / gain_attn.astype(f32),
            grad_w_qkv,
            grad_bias_qv.reshape(-1),
            grad_w_out,
            sums[0, :shard],
            sums[0, shard : 2 * shard],
            grad_w_up,
            sums[1],
            grad_w_down,
            sums[0, 2 * shard : 3 * shard],
        )

    rows_spec, matrix_spec, vector_spec = P(AXES, None), P("fsdp", None), P("fsdp")
    return jax.shard_map(
        local,
        mesh=mesh,
        in_specs=(
            rows_spec,
            vector_spec,
            matrix_spec,
            vector_spec,
            matrix_spec,
            vector_spec,
            vector_spec,
            matrix_spec,
            vector_spec,
            matrix_spec,
            vector_spec,
            rows_spec,
        ),
        out_specs=(
            rows_spec,
            rows_spec,
            vector_spec,
            matrix_spec,
            vector_spec,
            matrix_spec,
            vector_spec,
            vector_spec,
            matrix_spec,
            vector_spec,
            matrix_spec,
            vector_spec,
        ),
        check_vma=False,
    )
```

```python
import jax
import jax.numpy as jnp
from jax import lax
from jax.experimental import pallas as pl
from jax.experimental.pallas import tpu as pltpu
from jax.sharding import PartitionSpec as P

D = 768
H = 12
HD = 64
HEAD_GROUPS = 4
GROUP_HEADS = H // HEAD_GROUPS
GROUP_COLS = GROUP_HEADS * HD
HEAD_SCALE = HD ** (-0.5)
NORM_EPS = 1e-05
NEG_BIG = -1e30
GELU_A = 0.7978845608028654
GELU_B = 0.044715
LANES = 128
PIECES = 8
EXTRA = 8
LONG = 10**11
AXES = ("fsdp", "ctx")
VMEM_LIMIT = 120 << 19
UNROLL_BLOCKS = 8

f32 = jnp.float32
bf16 = jnp.bfloat16


def dot(left, right):
    return lax.dot_general(left, right, (((1,), (0,)), ((), ())), preferred_element_type=f32)


def dot_tn(left, right):
    return lax.dot_general(left, right, (((0,), (0,)), ((), ())), preferred_element_type=f32)


def dot_nt(left, right):
    return lax.dot_general(left, right, (((1,), (1,)), ((), ())), preferred_element_type=f32)


def centered(branch):
    return branch - jnp.mean(branch, axis=1, keepdims=True)


def inverse_rms(stream):
    return lax.rsqrt(jnp.mean(stream * stream, axis=1, keepdims=True) + NORM_EPS)


def norm_back(grad, unit, inverse):
    return inverse * (grad - unit * jnp.mean(grad * unit, axis=1, keepdims=True))


def slab_at(relative):
    return ((relative & 1) << 1) | (relative >> 1)


def loop(start, stop, body, carried):
    if isinstance(start, int) and isinstance(stop, int) and stop - start <= UNROLL_BLOCKS:
        for at in range(start, stop):
            carried = body(at, carried)
        return carried
    return lax.fori_loop(start, stop, body, carried)


def call(body, name, outs, args, flops=0, exps=0, scratch=(), **grid):
    moved = sum(x.size * x.dtype.itemsize for x in tuple(args) + tuple(outs))
    specs = dict(
        in_specs=[pl.BlockSpec(memory_space=pltpu.SMEM)]
        + [pl.BlockSpec(memory_space=pltpu.VMEM)] * (len(args) - 1),
        out_specs=tuple(pl.BlockSpec(memory_space=pltpu.VMEM) for _ in outs),
    )
    specs.update(grid)
    return pl.pallas_call(
        body,
        out_shape=tuple(outs),
        scratch_shapes=list(scratch),
        compiler_params=pltpu.CompilerParams(vmem_limit_bytes=VMEM_LIMIT),
        cost_estimate=pl.CostEstimate(flops=flops, bytes_accessed=moved, transcendentals=exps),
        name=name,
        **specs,
    )(*args)


def shape(dims, kind):
    return jax.ShapeDtypeStruct(tuple(dims), kind)


def norm_kernel(place, x_ref, resid_ref, unit_ref):
    x = x_ref[...].astype(f32)
    resid_ref[:, : D - 1] = x
    resid_ref[:, D - 1 :] = -jnp.sum(x, axis=1, keepdims=True)
    resid = resid_ref[...]
    unit_ref[0] = (resid * inverse_rms(resid)).astype(bf16)


def cut_kernel(place, qkv_ref, up_ref, heads_ref, *slabs):
    group = place[0] % HEAD_GROUPS
    for at in range(HEAD_GROUPS):

        @pl.when(group == at)
        def _():
            for kind in range(3):
                start = kind * D + at * GROUP_COLS
                heads_ref[:, kind * GROUP_COLS : (kind + 1) * GROUP_COLS] = qkv_ref[
                    :, start : start + GROUP_COLS
                ]

    hidden = slabs[0].shape[1]
    for distance, slab in enumerate(slabs):
        at = pl.multiple_of((distance ^ place[1]) * hidden, LANES)
        slab[...] = up_ref[:, pl.ds(at, hidden)]


def load_heads(place, slab_refs, wq, wkv):
    shard = slab_refs[0].shape[0]
    for distance, slab_ref in enumerate(slab_refs):
        at = pl.ds(pl.multiple_of((distance ^ place[1]) * shard, shard), shard)
        wq[at, :] = slab_ref[:, :GROUP_COLS]
        wkv[at, :] = slab_ref[:, GROUP_COLS:]


def project(place, normed_ref, slots, bias_ref, k_ref, v_ref, q_ref, qt_ref, wq, wkv):
    rows, query_rows = normed_ref.shape[1], qt_ref.shape[2]
    own = pl.ds(pl.multiple_of(place[2] * query_rows, query_rows), query_rows)
    for start in range(0, slots, 2):
        pair = range(start, min(start + 2, slots))
        normed = jnp.concatenate([normed_ref[slot] for slot in pair], axis=0)
        both = dot(normed, wkv[...])
        keys, values = both[:, :GROUP_COLS], both[:, GROUP_COLS:] + bias_ref[1:2, :]
        mine = jnp.concatenate([normed_ref[slot, own, :] for slot in pair], axis=0)
        queries = (dot(mine, wq[...]) + bias_ref[0:1, :]) * HEAD_SCALE
        for at, slot in enumerate(pair):
            here = slice(at * rows, (at + 1) * rows)
            k_ref[slot] = keys[here].astype(bf16)
            v_ref[slot] = values[here].astype(bf16)
            query = queries[at * query_rows : (at + 1) * query_rows]
            q_ref[slot], qt_ref[slot] = query.astype(bf16), query.T.astype(bf16)


def project_kernel(place, *refs):
    slabs, (gain_ref, bias_ref) = refs[:4], refs[4:6]
    pieces = refs[6:-7]
    normed_ref, k_ref, v_ref, q_ref, qt_ref, wq, wkv = refs[-7:]
    load_heads(place, slabs, wq, wkv)
    gain = gain_ref[...]
    slot = 0
    for ref in pieces:
        for at in range(ref.shape[0]):
            normed_ref[slot] = (ref[at].astype(f32) * gain).astype(bf16)
            slot += 1
    project(place, normed_ref, slot, bias_ref, k_ref, v_ref, q_ref, qt_ref, wq, wkv)


def project_block_kernel(place, *refs):
    slabs, bias_ref, normed_ref = refs[:4], refs[4], refs[5]
    k_ref, v_ref, q_ref, qt_ref, wq, wkv = refs[6:]

    @pl.when(pl.program_id(0) == 0)
    def _():
        load_heads(place, slabs, wq, wkv)

    slots = normed_ref.shape[0]
    project(place, normed_ref, slots, bias_ref, k_ref, v_ref, q_ref, qt_ref, wq, wkv)


def collect_kernel(place, normed_ref, normed_t_ref, query_t_ref):
    blocks, rows, _ = normed_ref.shape
    query_rows = query_t_ref.shape[1] // blocks
    own = pl.ds(pl.multiple_of(place[2] * query_rows, query_rows), query_rows)
    for slot in range(blocks):
        normed_t_ref[:, slot * rows : (slot + 1) * rows] = normed_ref[slot].T
        query_t_ref[:, slot * query_rows : (slot + 1) * query_rows] = normed_ref[slot, own, :].T


def by_head(value):
    head = lax.broadcasted_iota(jnp.int32, value.shape, 0) // HD
    zero = jnp.zeros_like(value)
    return jnp.concatenate([jnp.where(head == at, value, zero) for at in range(GROUP_HEADS)], axis=1)


def by_head_rows(value):
    head = lax.broadcasted_iota(jnp.int32, value.shape, 1) // HD
    zero = jnp.zeros_like(value)
    return jnp.concatenate([jnp.where(head == at, value, zero) for at in range(GROUP_HEADS)], axis=0)


def lane_halves(value, join):
    return join(value[:, :LANES], value[:, LANES:])


def attend_kernel(place, q_ref, k_ref, v_ref, out_ref, log_ref, score_ref):
    blocks, width, _ = q_ref.shape
    member = place[0]

    def one_query_block(block, _):
        queries = by_head_rows(q_ref[block ^ member])

        def one_score(key_block, top):
            scores = dot_nt(queries, k_ref[key_block ^ member])
            score_ref[key_block] = scores
            return jnp.maximum(top, lane_halves(scores, jnp.maximum))

        top = loop(0, block + 1, one_score, jnp.full((GROUP_HEADS * width, LANES), NEG_BIG, f32))
        top = jnp.max(top, axis=1, keepdims=True)

        def one_value(key_block, carried):
            total, acc = carried
            weights = jnp.exp(score_ref[key_block] - top)
            total = total + lane_halves(weights, jnp.add)
            return total, acc + dot(weights.astype(bf16), v_ref[key_block ^ member])

        start_state = (
            jnp.zeros((GROUP_HEADS * width, LANES), f32),
            jnp.zeros((GROUP_HEADS * width, GROUP_COLS), f32),
        )
        total, acc = loop(0, block + 1, one_value, start_state)
        total = jnp.sum(total, axis=1, keepdims=True)
        acc = acc / total
        log_sums = jnp.broadcast_to(top + jnp.log(total), (GROUP_HEADS * width, LANES))
        for head in range(GROUP_HEADS):
            here = slice(head * width, (head + 1) * width)
            cols = slice(head * HD, (head + 1) * HD)
            out_ref[block, cols, :] = acc[here, :].T[cols].astype(bf16)
            log_ref[block, :, here] = log_sums[here].T[:1]
        return 0

    loop(0, blocks, one_query_block, 0)


def attend_back_kernel(
    place, qt_ref, k_ref, v_ref, gt_ref, out_ref, log_ref, dq_ref, dkv_ref, sum_ref, dk_acc, dv_acc, dq_acc, delta_ref
):
    blocks, _, width = qt_ref.shape
    member = place[0]

    def prepare(block, _):
        products = gt_ref[block].astype(f32) * out_ref[block].astype(f32)
        for head in range(GROUP_HEADS):
            delta_ref[block, :, head * width : (head + 1) * width] = jnp.sum(
                products[head * HD : (head + 1) * HD], axis=0, keepdims=True
            )
        return 0

    lax.fori_loop(0, blocks, prepare, 0)
    dq_acc[...] = jnp.zeros_like(dq_acc)
    sum_ref[...] = jnp.zeros_like(sum_ref)

    head_at = lax.broadcasted_iota(jnp.int32, (width, GROUP_COLS), 1) // HD

    def one_key_block(key_block, _):
        slot = key_block ^ member
        dk_acc[...] = jnp.zeros_like(dk_acc)
        dv_acc[...] = jnp.zeros_like(dv_acc)

        def one_query_block(block, _):
            queries, grads = by_head(qt_ref[block ^ member]), by_head(gt_ref[block])
            prob = jnp.exp(dot(k_ref[slot], queries) - log_ref[block])
            grad_prob = dot(v_ref[slot], grads)
            grad_scores = (prob * (grad_prob - delta_ref[block])).astype(bf16)
            dv_acc[...] += dot_nt(prob.astype(bf16), grads)
            dk_acc[...] += dot_nt(grad_scores, queries)
            every = dot_tn(grad_scores, k_ref[slot])
            grad = jnp.zeros((width, GROUP_COLS), f32)
            for head in range(GROUP_HEADS):
                grad = jnp.where(head_at == head, every[head * width : (head + 1) * width], grad)
            dq_acc[block] += grad
            return 0

        loop(key_block, blocks, one_query_block, 0)
        dkv_ref[slot] = jnp.concatenate([dk_acc[...], dv_acc[...]], axis=1).astype(bf16)
        sum_ref[1:2, :] += jnp.sum(dv_acc[...], axis=0, keepdims=True)
        return 0

    loop(0, blocks, one_key_block, 0)

    def write(block, _):
        grads = dq_acc[block] * HEAD_SCALE
        dq_ref[block ^ member] = grads.astype(bf16)
        sum_ref[0:1, :] += jnp.sum(grads, axis=0, keepdims=True)
        return 0

    lax.fori_loop(0, blocks, write, 0)


def middle_kernel(
    place, att_ref, resid_ref, vec_ref, slab0, slab1, slab2, slab3, middle_ref, normed_ref, branch
):
    query_rows = att_ref.shape[2]
    for split in range(att_ref.shape[0] // HEAD_GROUPS):
        total = None
        for distance, slab_ref in enumerate((slab0, slab1, slab2, slab3)):
            part = dot_tn(att_ref[split * HEAD_GROUPS + (distance ^ place[1])], slab_ref[...])
            total = part if total is None else total + part
        branch[split * query_rows : (split + 1) * query_rows, :] = total
    middle = resid_ref[...] + centered(branch[...] + vec_ref[1:2, :])
    middle_ref[...] = middle
    normed_ref[...] = (middle * inverse_rms(middle) * vec_ref[2:3, :]).astype(bf16)


def mlp_kernel(place, *refs):
    normed, grads, slabs, (down_ref, bias_ref) = refs[:4], refs[4:8], refs[8:12], refs[12:14]
    norm_own, norm_far, norm_give, active_ref, hidden_ref, bias_grad, weight = refs[14:]
    rows, shard = normed[0].shape[0], slabs[0].shape[0]
    for distance, slab in enumerate(slabs):
        at = pl.multiple_of((distance ^ place[1]) * shard, shard)
        weight[pl.ds(at, shard), :] = slab[...]
    for tile in range(2):
        blocks = (tile, 2 + tile)
        tokens = jnp.concatenate([normed[at][...] for at in blocks], axis=0)
        grad = jnp.concatenate([grads[at][...] for at in blocks], axis=0)
        hidden = dot(tokens, weight[...]) + bias_ref[...]
        square = hidden * hidden
        bent = jnp.tanh(GELU_A * hidden * (1.0 + GELU_B * square))
        half = 0.5 * (1.0 + bent)
        active_ref[tile] = (hidden * half).astype(bf16)
        slope = half + 0.5 * hidden * (1.0 - bent * bent) * (GELU_A * (1.0 + 3.0 * GELU_B * square))
        grad_hidden = (dot_nt(grad, down_ref[...]) * slope).astype(bf16)
        hidden_ref[tile] = grad_hidden
        norm = dot_nt(grad_hidden, weight[...])
        bias = jnp.sum(grad_hidden.astype(f32), axis=0, keepdims=True)
        if tile:
            norm_give[0], norm_give[1] = norm[:rows].astype(bf16), norm[rows:].astype(bf16)
            bias_grad[...] += bias
        else:
            norm_own[...], norm_far[...] = norm[:rows], norm[rows:]
            bias_grad[...] = bias


def mlp_back_kernel(place, *refs):
    normed, grads, (active_ref, hidden_ref, down_ref) = refs[:4], refs[4:8], refs[8:11]
    branch_own, branch_far, branch_give = refs[11:14]
    pieces, (down_total, up_total) = refs[14:18], refs[18:]
    rows = normed[0].shape[0]
    wide = down_ref.shape[0] // PIECES
    piece = (pieces[0].shape[1] - wide) // 4
    shard = piece * PIECES
    mine, low = place[1], place[3]
    for tile in range(2):
        blocks = (tile, 2 + tile)
        tokens = jnp.concatenate([normed[at][...] for at in blocks], axis=0)
        grad = jnp.concatenate([grads[at][...] for at in blocks], axis=0)
        down, up = dot_tn(active_ref[tile], grad), dot_tn(tokens, hidden_ref[tile])
        branch = dot(active_ref[tile], down_ref[...])
        if tile:
            down_total[...] += down
            up_total[...] += up
            branch_give[0], branch_give[1] = branch[:rows].astype(bf16), branch[rows:].astype(bf16)
        else:
            down_total[...], up_total[...] = down, up
            branch_own[...], branch_far[...] = branch[:rows], branch[rows:]
    for near, target in enumerate(pieces):
        for side in range(2):
            at = (side << 2 | near) ^ low
            target[side, :wide] = down_total[pl.ds(pl.multiple_of(at * wide, wide), wide), :].astype(bf16)
            for distance in range(4):
                here = pl.multiple_of((distance ^ mine) * shard + at * piece, piece)
                start = wide + distance * piece
                target[side, start : start + piece] = up_total[pl.ds(here, piece), :].astype(bf16)


def branch_back_kernel(
    place,
    own_ref,
    core_ref,
    far_ref,
    middle_ref,
    top_ref,
    vec_ref,
    slab0,
    slab1,
    slab2,
    slab3,
    grad_middle_ref,
    grad_branch_ref,
    ga_ref,
    sum_ref,
):
    query_rows = ga_ref.shape[2]
    rows = top_ref.shape[0]
    grad = own_ref[...] + core_ref[0].astype(f32) + far_ref[...].astype(f32)
    middle = middle_ref[...]
    inverse = inverse_rms(middle)
    unit = middle * inverse
    sum_ref[0:1, :] = jnp.sum(grad * unit, axis=0, keepdims=True)
    grad_top = jnp.concatenate([top_ref[...].astype(f32), jnp.zeros((rows, 1), f32)], axis=1)
    grad_middle = grad_top + norm_back(grad * vec_ref[2:3, :], unit, inverse)
    grad_middle_ref[...] = grad_middle
    grad_branch = centered(grad_middle).astype(bf16)
    grad_branch_ref[...] = grad_branch
    for distance, slab_ref in enumerate((slab0, slab1, slab2, slab3)):
        product = dot_nt(slab_ref[...], grad_branch).astype(bf16)
        for split in range(ga_ref.shape[0] // HEAD_GROUPS):
            at = split * HEAD_GROUPS + (distance ^ place[1])
            ga_ref[at] = product[:, split * query_rows : (split + 1) * query_rows]
    sum_ref[1:2, :] = jnp.sum(grad_branch.astype(f32), axis=0, keepdims=True)
    sum_ref[2:3, :] = jnp.sum(centered(grad_top).astype(bf16).astype(f32), axis=0, keepdims=True)


def out_back_kernel(place, att_ref, grad_ref, sum_ref, bias_up_ref, near_ref, far_ref, grad_w):
    query_rows = att_ref.shape[2]
    groups, piece = HEAD_GROUPS, near_ref.shape[2] - EXTRA
    shard = D // groups
    mine, low = place[1], place[3]
    empty = jnp.zeros((1, D - 3 * shard), f32)
    for group in range(groups):
        weight = None
        for split in range(att_ref.shape[0] // groups):
            product = dot(
                att_ref[split * groups + group], grad_ref[split * query_rows : (split + 1) * query_rows, :]
            )
            weight = product if weight is None else weight + product
        lanes = slice(group * shard, (group + 1) * shard)
        grad_w[group * shard : (group + 1) * shard, :] = weight
        row = [sum_ref[at : at + 1, lanes] for at in (1, 0, 2)]
        grad_w[D + group : D + group + 1, :] = jnp.concatenate(row + [empty], axis=1)
    for distance in range(4):
        far, core = distance >> 1, distance & 1
        row = grad_w[pl.ds(D + (distance ^ mine), 1), :]
        up_row = jnp.zeros_like(row) if distance else bias_up_ref[...]
        extra = jnp.concatenate([row, up_row, jnp.zeros((EXTRA - 2, D), f32)], axis=0)

        def one(index, _, distance=distance, extra=extra):
            at = (distance ^ mine) * shard + (((index & 1) << 2 | index >> 1) ^ low) * piece
            part = grad_w[pl.ds(pl.multiple_of(at, piece), piece), :]
            target = (near_ref, far_ref)[distance & 1]
            target[distance >> 1, index] = jnp.concatenate([part, extra], axis=0).astype(bf16)
            return 0

        lax.fori_loop(0, PIECES, one, 0)


def sum_kernel(place, part0, part1, part2, part3, down_ref, up_ref):
    parts, wide = (part0, part1, part2, part3), down_ref.shape[1]
    down_ref[...] = sum(part[:, :wide].astype(f32) for part in parts).astype(bf16)
    up_ref[...] = sum(part[:, wide:].astype(f32) for part in parts).astype(bf16)


def heads_back_kernel(place, normed_t_ref, query_t_ref, dq_ref, dkv_ref, sum_ref, near_ref, far_ref, aq, akv):
    blocks, query_rows, _ = dq_ref.shape
    rows = dkv_ref.shape[1]
    chunk = min(blocks, 4)
    for start in range(0, blocks, chunk):
        dkv = jnp.concatenate([dkv_ref[start + at] for at in range(chunk)], axis=0)
        dq = jnp.concatenate([dq_ref[start + at] for at in range(chunk)], axis=0)
        kv = dot(normed_t_ref[:, start * rows : (start + chunk) * rows], dkv)
        q = dot(query_t_ref[:, start * query_rows : (start + chunk) * query_rows], dq)
        if start:
            akv[...] += kv
            aq[...] += q
        else:
            akv[...], aq[...] = kv, q
    arrange_heads(place, aq, akv, sum_ref, near_ref, far_ref)


def arrange_heads(place, q_ref, kv_ref, sum_ref, near_ref, far_ref):
    mine, piece = place[1], near_ref.shape[2] - EXTRA
    shard = 2 * piece
    group = place[0] % HEAD_GROUPS
    for row in range(D // shard):
        relative = row ^ mine
        first = jnp.where(group // 2 == row, sum_ref[0:1, :], 0.0)
        second = jnp.where(2 + group // 2 == row, sum_ref[1:2, :], 0.0)
        extra = jnp.concatenate([first, second, jnp.zeros_like(first)], axis=1)
        extra = jnp.concatenate([extra, jnp.zeros((EXTRA - 1, extra.shape[1]), f32)], axis=0)
        for part in range(2):
            at_row = slice(row * shard + part * piece, row * shard + (part + 1) * piece)
            block = jnp.concatenate([q_ref[at_row, :], kv_ref[at_row, :]], axis=1)
            both = jnp.concatenate([block, extra], axis=0).astype(bf16)
            for core, target in enumerate((near_ref, far_ref)):

                @pl.when((relative & 1) == core)
                def _():
                    target[relative >> 1, part ^ ((place[3] >> 2) & 1)] = both


def rows_back_kernel(place, dq_ref, dkv_ref, slab0, slab1, slab2, slab3, keep_ref, give_ref, wq, wkv):
    load_heads(place, (slab0, slab1, slab2, slab3), wq, wkv)
    query_rows, half = dq_ref.shape[1], keep_ref.shape[0]
    own = pl.ds(pl.multiple_of(place[2] * query_rows, query_rows), query_rows)
    for core, ref in ((1, give_ref), (0, keep_ref)):

        def one(at, _, core=core, ref=ref):
            slot = at + core * half
            ref[at] = dot_nt(dkv_ref[slot], wkv[...]).astype(bf16)
            low = ref[at, own, :].astype(f32)
            ref[at, own, :] = (low + dot_nt(dq_ref[slot], wq[...])).astype(bf16)
            return 0

        loop(0, half, one, 0)


def stream_back_kernel(place, part0, part1, part2, part3, resid_ref, grad_middle_ref, vec_ref, out_ref):
    grad = sum(part[...].astype(f32) for part in (part0, part1, part2, part3))
    resid = resid_ref[...]
    inverse = inverse_rms(resid)
    unit = resid * inverse
    total = grad_middle_ref[...] + norm_back(grad * vec_ref[0:1, :], unit, inverse)
    out_ref[...] = (total - total[:, D - 1 :]).astype(bf16)[:, : D - 1]


def down_out_kernel(place, part0, part1, part2, part3, out_ref):
    wide = part0.shape[1]
    for near, part in enumerate((part0, part1, part2, part3)):
        for side in range(2):
            at = pl.multiple_of(((side << 2 | near) ^ place[3]) * wide, wide)
            out_ref[pl.ds(at, wide), :] = part[side].astype(f32)


def up_out_kernel(place, part0, part1, part2, part3, up_ref, out_ref):
    rows = out_ref.shape[0] // PIECES
    for near, part in enumerate((part0, part1, part2, part3)):
        for side in range(2):
            at = pl.multiple_of(((side << 2 | near) ^ place[3]) * rows, rows)
            for slab in range(4):
                col = pl.multiple_of((slab ^ place[1]) * D, LANES)
                value = part[side, slab * rows : (slab + 1) * rows]
                up_ref[pl.ds(at, rows), pl.ds(col, D)] = value.astype(f32)
            out_ref[pl.ds(at, rows), :] = part[side, 4 * rows :].astype(f32)


def heads_out_kernel(place, part0, part1, part2, part3, weight_ref, out_ref, gain_ref, bias_ref, pieces):
    piece = part0.shape[1] - EXTRA
    mine, low = place[1], place[3]
    for near, part in enumerate((part0, part1, part2, part3)):
        pieces[near] = part[...]
    for part in range(2):
        for group in range(HEAD_GROUPS):
            value = pieces[(group ^ low) & 3, part ^ ((low >> 2) & 1)].astype(f32)
            for kind in range(3):
                start = kind * D + group * GROUP_COLS
                out_ref[part * piece : (part + 1) * piece, start : start + GROUP_COLS] = value[
                    :piece, kind * GROUP_COLS : (kind + 1) * GROUP_COLS
                ]
    gain_ref[...] = jnp.sum(out_ref[...] * weight_ref[...].astype(f32), axis=1, keepdims=True)
    sides = []
    for side in range(2):
        group = ((2 * mine) & 3) + side
        value = pieces[(group ^ low) & 3, 0].astype(f32)[piece : piece + 1]
        sides.append(jnp.where(mine < 2, value[:, :GROUP_COLS], value[:, GROUP_COLS : 2 * GROUP_COLS]))
    bias_ref[...] = jnp.concatenate(sides, axis=1)


def solution(mesh):
    fsdp_count, ctx_count = mesh.shape["fsdp"], mesh.shape["ctx"]
    half = ctx_count // 2
    steps = half.bit_length() - 1
    ctx_steps = steps + 1
    splits = ctx_count // HEAD_GROUPS
    shard = D // fsdp_count

    def send(value, target):
        pairs = []
        for source in range(fsdp_count * ctx_count):
            row, at = target(*divmod(source, ctx_count))
            pairs.append((source, row * ctx_count + at))
        return lax.ppermute(value, AXES, pairs)

    def to_core(value):
        return send(value, lambda row, at: (row ^ 1, at))

    def to_chip_row(value):
        return send(value, lambda row, at: (row ^ 2, at))

    def to_ctx(value, bit):
        return send(value, lambda row, at: (row, at ^ bit))

    def swap_sequences(value):
        return send(
            value, lambda row, at: (row, at) if (row & 1) == at // half else (row ^ 1, at ^ half)
        )

    groups = [
        [(row + core) * ctx_count + side * half + at for core in range(2) for at in range(half)]
        for row in range(0, fsdp_count, 2)
        for side in range(2)
    ]

    def group_all_to_all(value):
        return lax.all_to_all(value, AXES, 0, 0, axis_index_groups=groups, tiled=True)

    def to_fsdp(value, distance):
        return send(value, lambda row, at: (row ^ distance, at))

    def over_fsdp(value):
        far = to_chip_row(value)
        return value, to_core(value), far, to_core(far)

    def to_square(values):
        return tuple(to_ctx(value, near + 1) for near, value in enumerate(values))

    def gather_square(value):
        pair = jnp.stack([value, to_ctx(value, 4)])
        return (pair, *to_square((pair,) * 3))

    def over_rest(value):
        for step in range(3, ctx_steps):
            value = value + to_ctx(value, 1 << step)
        return value

    together = lax.optimization_barrier

    def widened(value):
        width = value.shape[-1]
        return value if width >= LANES else jnp.pad(value, ((0, 0), (0, 0), (0, LANES - width)))

    def local(
        stream_in,
        gain_attn,
        w_qkv,
        bias_qv,
        w_out,
        bias_out,
        gain_mlp,
        w_up,
        bias_up,
        w_down,
        bias_down,
        grad_out,
    ):
        rows = stream_in.shape[0]
        query_rows = rows // splits
        width = max(query_rows, LANES)
        fsdp_at, ctx_at = lax.axis_index("fsdp"), lax.axis_index("ctx")
        core, inner = fsdp_at & 1, ctx_at % half
        member = core * half + inner
        head_group = inner % HEAD_GROUPS
        place = jnp.stack([member, fsdp_at, member // HEAD_GROUPS, ctx_at & 7]).astype(jnp.int32)

        hidden = w_down.shape[0]
        stream = swap_sequences(stream_in)
        w_part, *up_sent = call(
            cut_kernel,
            "cut",
            (
                shape((shard, 3 * GROUP_COLS), bf16),
                *(shape((shard, hidden), bf16) for _ in range(fsdp_count)),
            ),
            (place, w_qkv, w_up),
        )
        vectors = jnp.concatenate(
            [
                part.astype(f32).reshape(1, -1)
                for part in (gain_attn, bias_out, gain_mlp, bias_down, bias_qv, bias_up)
            ],
            axis=1,
        )
        far_heads, far_vectors = together((to_chip_row(w_part), to_chip_row(vectors)))
        w_heads = (w_part, to_core(w_part), far_heads, to_core(far_heads))
        vectors = (vectors, to_core(vectors), far_vectors, to_core(far_vectors))
        far_heads, w_out_sent, stream = together((far_heads, w_out, stream))

        resid, unit = call(
            norm_kernel,
            "norm",
            (shape((rows, D), f32), shape((1, rows, D), bf16)),
            (place, stream),
        )
        got = to_square((unit,) * 3)
        *got, out_far = together((*got, to_chip_row(w_out_sent)))
        pieces = [unit, *got]
        for bit in range(2, steps):
            pieces.append(to_ctx(jnp.concatenate(pieces), 1 << bit))
        pieces = pieces + [to_core(piece) for piece in pieces]

        def by_row(values):
            ordered = []
            for row in range(fsdp_count):
                first = jnp.where((fsdp_at ^ row) & 1 == 0, values[0], values[1])
                second = jnp.where((fsdp_at ^ row) & 1 == 0, values[2], values[3])
                ordered.append(jnp.where((fsdp_at ^ row) < 2, first, second))
            return jnp.concatenate(ordered)

        vectors = by_row(vectors)
        vec = vectors[:, :D].reshape(fsdp_count, 4, shard).transpose(1, 0, 2).reshape(4, D)
        bias_heads = vectors[:, D : D + 2 * shard].reshape(2, HEAD_GROUPS, GROUP_COLS)
        bias_heads = lax.dynamic_index_in_dim(bias_heads, head_group, 1, keepdims=False)
        bias_hidden = lax.dynamic_slice_in_dim(vectors[:, D + 2 * shard :], fsdp_at, 1)
        gain = vec[0:1]

        head_weights = [pltpu.VMEM((D, GROUP_COLS), bf16), pltpu.VMEM((D, 2 * GROUP_COLS), bf16)]
        tokens = ctx_count * rows
        projected = (
            shape((ctx_count, rows, GROUP_COLS), bf16),
            shape((ctx_count, rows, GROUP_COLS), bf16),
            shape((ctx_count, query_rows, GROUP_COLS), bf16),
            shape((ctx_count, GROUP_COLS, query_rows), bf16),
        )
        work = 5 * tokens * D * GROUP_COLS
        if 4 * tokens * D * 2 < VMEM_LIMIT:
            normed, keys, values, queries, queries_t = call(
                project_kernel,
                "project",
                (shape((ctx_count, rows, D), bf16), *projected),
                (place, *w_heads, gain, bias_heads, *pieces),
                flops=work,
                scratch=head_weights,
            )
        else:
            normed = (jnp.concatenate(pieces).astype(f32) * gain).astype(bf16)
            block = lambda *dims: pl.BlockSpec((1,) + dims, lambda at: (at, 0, 0))
            whole = lambda *dims: pl.BlockSpec(dims, lambda at: (0,) * len(dims))
            keys, values, queries, queries_t = call(
                project_block_kernel,
                "project",
                projected,
                (place, *w_heads, bias_heads, normed),
                flops=work,
                scratch=head_weights,
                grid=(ctx_count,),
                in_specs=[pl.BlockSpec(memory_space=pltpu.SMEM)]
                + [whole(shard, 3 * GROUP_COLS)] * 4
                + [whole(2, GROUP_COLS), block(rows, D)],
                out_specs=(
                    block(rows, GROUP_COLS),
                    block(rows, GROUP_COLS),
                    block(query_rows, GROUP_COLS),
                    block(GROUP_COLS, query_rows),
                ),
            )
        queries_t = widened(queries_t)
        queries = jnp.pad(queries, ((0, 0), (0, width - query_rows), (0, 0)))
        pairs = GROUP_HEADS * query_rows * rows * ctx_count * (ctx_count + 1) // 2
        outs, logs = call(
            attend_kernel,
            "attend",
            (
                shape((ctx_count, GROUP_COLS, width), bf16),
                shape((ctx_count, 1, GROUP_HEADS * width), f32),
            ),
            (place, queries, keys, values),
            flops=4 * HD * pairs,
            exps=pairs,
            scratch=[pltpu.VMEM((ctx_count, GROUP_HEADS * width, rows), f32)],
        )
        outs, *up_got = together(
            (outs, *(to_fsdp(up_sent[distance], distance) for distance in (1, 2, 3)))
        )
        attended = group_all_to_all(outs[:, :, :query_rows])
        w_out_all = (w_out, to_core(w_out), out_far, to_core(out_far))
        top = swap_sequences(grad_out)
        grad_result = jnp.pad(top.astype(f32), ((0, 0), (0, 1)))
        grad_branch_mlp = centered(grad_result).astype(bf16)
        grads_mlp = over_fsdp(grad_branch_mlp)
        middle, normed_mlp = call(
            middle_kernel,
            "middle",
            (shape((rows, D), f32), shape((rows, D), bf16)),
            (place, attended, resid, vec, *w_out_all),
            flops=2 * rows * D * D,
            scratch=[pltpu.VMEM((rows, D), f32)],
        )
        piece = shard // PIECES
        normed_mlp, normed = together((normed_mlp, normed))
        if 4 * tokens * D * 2 < VMEM_LIMIT:
            normed_t, query_t = call(
                collect_kernel,
                "collect",
                (
                    shape((D, tokens), bf16),
                    shape((D, ctx_count * query_rows), bf16),
                ),
                (place, normed),
            )
        else:
            normed_query = lax.dynamic_index_in_dim(
                normed.reshape(ctx_count, splits, query_rows, D), place[2], 1, keepdims=False
            )
            normed_t, query_t = normed.reshape(tokens, D).T, normed_query.reshape(-1, D).T
        normed_all = over_fsdp(normed_mlp)
        far_normed, normed_t, query_t = together((normed_all[2], normed_t, query_t))
        normed_all = (normed_all[0], normed_all[1], far_normed, to_core(far_normed))
        norm_own, norm_far, norm_give, active, grad_hidden, bias_up_sum = call(
            mlp_kernel,
            "mlp",
            (
                shape((rows, D), f32),
                shape((rows, D), f32),
                shape((2, rows, D), bf16),
                shape((2, 2 * rows, hidden), bf16),
                shape((2, 2 * rows, hidden), bf16),
                shape((1, hidden), f32),
            ),
            (place, *normed_all, *grads_mlp, up_sent[0], *up_got, w_down, bias_hidden),
            flops=24 * rows * D * hidden,
            exps=4 * rows * hidden,
            scratch=[pltpu.VMEM((D, hidden), bf16)],
        )
        norm_got = to_core(norm_give)
        norm_far_got = to_chip_row((norm_far + norm_got[1]).astype(bf16))
        norm_sent, active, grad_hidden = together((norm_got, active, grad_hidden))
        branch_own, branch_far, branch_give, *both_sums = call(
            mlp_back_kernel,
            "mlp_back",
            (
                shape((rows, D), f32),
                shape((rows, D), f32),
                shape((2, rows, D), bf16),
                *(shape((2, hidden // PIECES + 4 * piece, D), bf16) for _ in range(4)),
            ),
            (place, *normed_all, *grads_mlp, active, grad_hidden, w_down),
            flops=LONG,
            scratch=[pltpu.VMEM((hidden, D), f32), pltpu.VMEM((D, hidden), f32)],
        )
        norm_far_got, branch_own, branch_far, branch_give, *both_sums = together(
            (norm_far_got, branch_own, branch_far, branch_give, *both_sums)
        )
        grad_middle, grad_branch, grad_attended, row_sums = call(
            branch_back_kernel,
            "branch_back",
            (
                shape((rows, D), f32),
                shape((rows, D), bf16),
                shape((ctx_count, GROUP_COLS, query_rows), bf16),
                shape((8, D), f32),
            ),
            (place, norm_own, norm_got, norm_far_got, middle, top, vec, *w_out_all),
            flops=4 * rows * D * D,
        )
        grads = group_all_to_all(grad_attended)
        out_near, out_give = call(
            out_back_kernel,
            "out_back",
            (shape((2, PIECES, piece + EXTRA, D), bf16), shape((2, PIECES, piece + EXTRA, D), bf16)),
            (place, attended, grad_branch, row_sums, bias_up_sum),
            flops=2 * rows * D * D,
            scratch=[pltpu.VMEM((D + 8, D), f32)],
        )
        out_sum = out_near + to_core(out_give)
        branch_got = to_core(branch_give)
        branch_far_got = to_chip_row((branch_far + branch_got[1]).astype(bf16))
        branch_mlp = branch_own + branch_got[0] + branch_far_got + vec[3:4]
        stream_out = (middle + centered(branch_mlp)).astype(bf16)[:, : D - 1]
        grads, out_sum, stream_out = together((grads, out_sum, stream_out))
        stream_out = swap_sequences(stream_out)
        out_got = to_chip_row(out_sum[1])
        both_got = to_square(both_sums[1:])
        dq, dkv, head_sums = call(
            attend_back_kernel,
            "attend_back",
            (
                shape((ctx_count, width, GROUP_COLS), bf16),
                shape((ctx_count, rows, 2 * GROUP_COLS), bf16),
                shape((8, GROUP_COLS), f32),
            ),
            (place, queries_t, keys, values, widened(grads), outs, logs),
            flops=10 * HD * pairs,
            exps=pairs,
            scratch=[
                pltpu.VMEM((rows, GROUP_COLS), f32),
                pltpu.VMEM((rows, GROUP_COLS), f32),
                pltpu.VMEM((ctx_count, width, GROUP_COLS), f32),
                pltpu.VMEM((ctx_count, 1, GROUP_HEADS * width), f32),
            ],
        )
        dq = dq[:, :query_rows]
        dq, dkv, out_got = together((dq, dkv, out_got))

        head_shapes = tuple(
            shape((2, 2, shard // 2 + EXTRA, 3 * GROUP_COLS), bf16) for _ in range(2)
        )
        if 4 * tokens * D * 2 < VMEM_LIMIT:
            head_near, head_give = call(
                heads_back_kernel,
                "heads_back",
                head_shapes,
                (place, normed_t, query_t, dq, dkv, head_sums),
                flops=work,
                scratch=[pltpu.VMEM((D, GROUP_COLS), f32), pltpu.VMEM((D, 2 * GROUP_COLS), f32)],
            )
        else:
            flat_q, flat_kv = dq.reshape(-1, GROUP_COLS), dkv.reshape(tokens, 2 * GROUP_COLS)
            head_near, head_give = call(
                arrange_heads,
                "arrange_heads",
                head_shapes,
                (place, dot(query_t, flat_q), dot(normed_t, flat_kv), head_sums),
            )
        head_near, head_give, stream_out, out_got, *both_got = together(
            (head_near, head_give, stream_out, out_got, *both_got)
        )
        down_sum, up_sum = call(
            sum_kernel,
            "sum",
            (
                shape((2, hidden // PIECES, D), bf16),
                shape((2, fsdp_count * piece, hidden), bf16),
            ),
            (place, both_sums[0], *both_got),
        )
        out_sums = [
            out_sum[0, 2 * near : 2 * near + 2] + out_got[2 * near : 2 * near + 2] for near in range(4)
        ]
        head_sum = head_near + to_core(head_give)
        dq, head_near, head_give, down_sum, up_sum, *out_sums = together(
            (dq, head_sum[0], head_sum[1], down_sum, up_sum, *out_sums)
        )
        head_got = to_chip_row(head_give)
        down_got, up_got = to_ctx(down_sum, 4), to_ctx(up_sum, 4)
        out_got = to_square(out_sums[1:])

        row_shapes = (shape((half, rows, D), bf16), shape((half, rows, D), bf16))
        if 4 * tokens * D * 2 < VMEM_LIMIT:
            keep_rows, give_rows = call(
                rows_back_kernel,
                "rows_back",
                row_shapes,
                (place, dq, dkv, *w_heads),
                flops=work,
                scratch=head_weights,
            )
        else:
            weights = by_row(w_heads)
            flat_q, flat_kv = dq.reshape(-1, GROUP_COLS), dkv.reshape(tokens, 2 * GROUP_COLS)
            grad_rows = dot_nt(flat_kv, weights[:, GROUP_COLS:]).reshape(
                ctx_count, splits, query_rows, D
            )
            grad_query = dot_nt(flat_q, weights[:, :GROUP_COLS]).reshape(ctx_count, 1, query_rows, D)
            chosen = (jnp.arange(splits) == place[2])[None, :, None, None]
            grad_rows = (grad_rows + jnp.where(chosen, grad_query, 0.0)).astype(bf16)
            grad_rows = grad_rows.reshape(ctx_count, rows, D)
            keep_rows, give_rows = grad_rows[:half], grad_rows[half:]
        keep_rows, give_rows, head_got, *out_got = together(
            (keep_rows, give_rows, head_got, *out_got)
        )

        def both_sides(own, other):
            return over_rest(jnp.stack([own[0] + other[1], own[1] + other[0]]))

        rows_got = to_core(give_rows)
        head_sum = head_near + head_got
        out_sum = sum(out_got, start=out_sums[0])
        rows_got, head_sum, out_sum = together((rows_got, head_sum, out_sum))
        head_got, out_got = to_ctx(head_sum, 4), to_ctx(out_sum, 4)
        if steps == 2:
            parts = [keep_rows[slot] + rows_got[slot] for slot in range(4)]
        else:
            both = keep_rows + rows_got
            for bit in reversed(range(2, steps)):
                both = both[: 1 << bit] + to_ctx(both[1 << bit :], 1 << bit)
            parts = [both[slot] for slot in range(4)]
        rows_got = to_square(parts[1:])
        up_got, down_got, *rows_got = together((up_got, down_got, *rows_got))
        up_sum = both_sides(up_sum, up_got)
        ups = [up_sum[:, distance * piece : (distance + 1) * piece] for distance in range(fsdp_count)]
        ups = [ups[0]] + [to_fsdp(ups[distance], distance) for distance in (1, 2, 3)]
        downs = both_sides(down_sum, down_got)
        downs = (downs, *to_square((downs,) * 3))
        *ups, head_got, out_got = together((*ups, head_got, out_got))
        outs = both_sides(out_sum, out_got)
        sums = outs[0, piece:].astype(f32)
        ups = jnp.concatenate([*ups, outs[:, :piece]], axis=1)
        ups = (ups, *to_square((ups,) * 3))
        heads = both_sides(head_sum, head_got)
        heads = (heads, *to_square((heads,) * 3))
        (grad_stream,) = call(
            stream_back_kernel,
            "stream_back",
            (shape((rows, D - 1), bf16),),
            (place, parts[0], *rows_got, resid, grad_middle, vec),
        )
        grad_stream = swap_sequences(grad_stream)
        (grad_w_down,) = call(down_out_kernel, "down_out", (shape((hidden, D), f32),), (place, *downs))
        grad_w_up, grad_w_out = call(
            up_out_kernel,
            "up_out",
            (shape((shard, fsdp_count * hidden), f32), shape((shard, D), f32)),
            (place, *ups),
        )
        grad_w_qkv, grad_gain_attn, grad_bias_qv = call(
            heads_out_kernel,
            "heads_out",
            (
                shape((shard, 3 * D), f32),
                shape((shard, 1), f32),
                shape((1, 2 * shard), f32),
            ),
            (place, *heads, w_qkv),
            scratch=[pltpu.VMEM((4, 2, shard // 2 + EXTRA, 3 * GROUP_COLS), bf16)],
        )
        return (
            stream_out,
            grad_stream.astype(f32),
            grad_gain_attn.reshape(-1) / gain_attn.astype(f32),
            grad_w_qkv,
            grad_bias_qv.reshape(-1),
            grad_w_out,
            sums[0, :shard],
            sums[0, shard : 2 * shard],
            grad_w_up,
            sums[1],
            grad_w_down,
            sums[0, 2 * shard : 3 * shard],
        )

    rows_spec, matrix_spec, vector_spec = P(AXES, None), P("fsdp", None), P("fsdp")
    return jax.shard_map(
        local,
        mesh=mesh,
        in_specs=(
            rows_spec,
            vector_spec,
            matrix_spec,
            vector_spec,
            matrix_spec,
            vector_spec,
            vector_spec,
            matrix_spec,
            vector_spec,
            matrix_spec,
            vector_spec,
            rows_spec,
        ),
        out_specs=(
            rows_spec,
            rows_spec,
            vector_spec,
            matrix_spec,
            vector_spec,
            matrix_spec,
            vector_spec,
            vector_spec,
            matrix_spec,
            vector_spec,
            matrix_spec,
            vector_spec,
        ),
        check_vma=False,
    )
```

```python
import jax
import jax.numpy as jnp
from jax import lax
from jax.experimental import pallas as pl
from jax.experimental.pallas import tpu as pltpu
from jax.sharding import PartitionSpec as P

D = 768
H = 12
HD = 64
HEAD_GROUPS = 4
GROUP_HEADS = H // HEAD_GROUPS
GROUP_COLS = GROUP_HEADS * HD
HEAD_SCALE = HD ** (-0.5)
NORM_EPS = 1e-05
NEG_BIG = -1e30
GELU_A = 0.7978845608028654
GELU_B = 0.044715
LANES = 128
PIECES = 8
EXTRA = 8
LONG = 10**11
AXES = ("fsdp", "ctx")
VMEM_LIMIT = 120 << 19
UNROLL_BLOCKS = 8

f32 = jnp.float32
bf16 = jnp.bfloat16


def dot(left, right):
    return lax.dot_general(left, right, (((1,), (0,)), ((), ())), preferred_element_type=f32)


def dot_tn(left, right):
    return lax.dot_general(left, right, (((0,), (0,)), ((), ())), preferred_element_type=f32)


def dot_nt(left, right):
    return lax.dot_general(left, right, (((1,), (1,)), ((), ())), preferred_element_type=f32)


def centered(branch):
    return branch - jnp.mean(branch, axis=1, keepdims=True)


def inverse_rms(stream):
    return lax.rsqrt(jnp.mean(stream * stream, axis=1, keepdims=True) + NORM_EPS)


def norm_back(grad, unit, inverse):
    return inverse * (grad - unit * jnp.mean(grad * unit, axis=1, keepdims=True))


def slab_at(relative):
    return ((relative & 1) << 1) | (relative >> 1)


def loop(start, stop, body, carried):
    if isinstance(start, int) and isinstance(stop, int) and stop - start <= UNROLL_BLOCKS:
        for at in range(start, stop):
            carried = body(at, carried)
        return carried
    return lax.fori_loop(start, stop, body, carried)


def call(body, name, outs, args, flops=0, exps=0, scratch=(), **grid):
    moved = sum(x.size * x.dtype.itemsize for x in tuple(args) + tuple(outs))
    specs = dict(
        in_specs=[pl.BlockSpec(memory_space=pltpu.SMEM)]
        + [pl.BlockSpec(memory_space=pltpu.VMEM)] * (len(args) - 1),
        out_specs=tuple(pl.BlockSpec(memory_space=pltpu.VMEM) for _ in outs),
    )
    specs.update(grid)
    return pl.pallas_call(
        body,
        out_shape=tuple(outs),
        scratch_shapes=list(scratch),
        compiler_params=pltpu.CompilerParams(vmem_limit_bytes=VMEM_LIMIT),
        cost_estimate=pl.CostEstimate(flops=flops, bytes_accessed=moved, transcendentals=exps),
        name=name,
        **specs,
    )(*args)


def shape(dims, kind):
    return jax.ShapeDtypeStruct(tuple(dims), kind)


def norm_kernel(place, x_ref, resid_ref, unit_ref):
    x = x_ref[...].astype(f32)
    resid_ref[:, : D - 1] = x
    resid_ref[:, D - 1 :] = -jnp.sum(x, axis=1, keepdims=True)
    resid = resid_ref[...]
    unit_ref[0] = (resid * inverse_rms(resid)).astype(bf16)


def cut_kernel(place, qkv_ref, up_ref, heads_ref, *slabs):
    group = place[0] % HEAD_GROUPS
    for at in range(HEAD_GROUPS):

        @pl.when(group == at)
        def _():
            for kind in range(3):
                start = kind * D + at * GROUP_COLS
                heads_ref[:, kind * GROUP_COLS : (kind + 1) * GROUP_COLS] = qkv_ref[
                    :, start : start + GROUP_COLS
                ]

    hidden = slabs[0].shape[1]
    for distance, slab in enumerate(slabs):
        at = pl.multiple_of((distance ^ place[1]) * hidden, LANES)
        slab[...] = up_ref[:, pl.ds(at, hidden)]


def load_heads(place, slab_refs, wq, wkv):
    shard = slab_refs[0].shape[0]
    for distance, slab_ref in enumerate(slab_refs):
        at = pl.ds(pl.multiple_of((distance ^ place[1]) * shard, shard), shard)
        wq[at, :] = slab_ref[:, :GROUP_COLS]
        wkv[at, :] = slab_ref[:, GROUP_COLS:]


def project(place, normed_ref, slots, bias_ref, k_ref, v_ref, q_ref, qt_ref, wq, wkv):
    rows, query_rows = normed_ref.shape[1], qt_ref.shape[2]
    own = pl.ds(pl.multiple_of(place[2] * query_rows, query_rows), query_rows)
    for start in range(0, slots, 2):
        pair = range(start, min(start + 2, slots))
        normed = jnp.concatenate([normed_ref[slot] for slot in pair], axis=0)
        both = dot(normed, wkv[...])
        keys, values = both[:, :GROUP_COLS], both[:, GROUP_COLS:] + bias_ref[1:2, :]
        mine = jnp.concatenate([normed_ref[slot, own, :] for slot in pair], axis=0)
        queries = (dot(mine, wq[...]) + bias_ref[0:1, :]) * HEAD_SCALE
        for at, slot in enumerate(pair):
            here = slice(at * rows, (at + 1) * rows)
            k_ref[slot] = keys[here].astype(bf16)
            v_ref[slot] = values[here].astype(bf16)
            query = queries[at * query_rows : (at + 1) * query_rows]
            q_ref[slot], qt_ref[slot] = query.astype(bf16), query.T.astype(bf16)


def project_kernel(place, *refs):
    slabs, (gain_ref, bias_ref) = refs[:4], refs[4:6]
    pieces = refs[6:-7]
    k_ref, v_ref, q_ref, qt_ref, wq, wkv, normed_ref = refs[-7:]
    load_heads(place, slabs, wq, wkv)
    gain = gain_ref[...]
    slot = 0
    for ref in pieces:
        for at in range(ref.shape[0]):
            normed_ref[slot] = (ref[at].astype(f32) * gain).astype(bf16)
            slot += 1
    project(place, normed_ref, slot, bias_ref, k_ref, v_ref, q_ref, qt_ref, wq, wkv)


def project_block_kernel(place, *refs):
    slabs, bias_ref, normed_ref = refs[:4], refs[4], refs[5]
    k_ref, v_ref, q_ref, qt_ref, wq, wkv = refs[6:]

    @pl.when(pl.program_id(0) == 0)
    def _():
        load_heads(place, slabs, wq, wkv)

    slots = normed_ref.shape[0]
    project(place, normed_ref, slots, bias_ref, k_ref, v_ref, q_ref, qt_ref, wq, wkv)


def collect_kernel(place, gain_ref, *refs):
    pieces, (normed_t_ref, query_t_ref, normed_ref) = refs[:-3], refs[-3:]
    blocks, rows, _ = normed_ref.shape
    query_rows = query_t_ref.shape[1] // blocks
    own = pl.ds(pl.multiple_of(place[2] * query_rows, query_rows), query_rows)
    gain, slot = gain_ref[...], 0
    for ref in pieces:
        for at in range(ref.shape[0]):
            normed_ref[slot] = (ref[at].astype(f32) * gain).astype(bf16)
            normed_t_ref[:, slot * rows : (slot + 1) * rows] = normed_ref[slot].T
            mine = normed_ref[slot, own, :].T
            query_t_ref[:, slot * query_rows : (slot + 1) * query_rows] = mine
            slot += 1


def by_head(value):
    head = lax.broadcasted_iota(jnp.int32, value.shape, 0) // HD
    zero = jnp.zeros_like(value)
    return jnp.concatenate([jnp.where(head == at, value, zero) for at in range(GROUP_HEADS)], axis=1)


def by_head_rows(value):
    head = lax.broadcasted_iota(jnp.int32, value.shape, 1) // HD
    zero = jnp.zeros_like(value)
    return jnp.concatenate([jnp.where(head == at, value, zero) for at in range(GROUP_HEADS)], axis=0)


def lane_halves(value, join):
    return join(value[:, :LANES], value[:, LANES:])


def attend_kernel(place, q_ref, k_ref, v_ref, out_ref, log_ref, score_ref):
    blocks, width, _ = q_ref.shape
    member = place[0]

    def one_query_block(block, _):
        queries = by_head_rows(q_ref[block ^ member])

        def one_score(key_block, top):
            scores = dot_nt(queries, k_ref[key_block ^ member])
            score_ref[key_block] = scores
            return jnp.maximum(top, lane_halves(scores, jnp.maximum))

        top = loop(0, block + 1, one_score, jnp.full((GROUP_HEADS * width, LANES), NEG_BIG, f32))
        top = jnp.max(top, axis=1, keepdims=True)

        def one_value(key_block, carried):
            total, acc = carried
            weights = jnp.exp(score_ref[key_block] - top)
            total = total + lane_halves(weights, jnp.add)
            return total, acc + dot(weights.astype(bf16), v_ref[key_block ^ member])

        start_state = (
            jnp.zeros((GROUP_HEADS * width, LANES), f32),
            jnp.zeros((GROUP_HEADS * width, GROUP_COLS), f32),
        )
        total, acc = loop(0, block + 1, one_value, start_state)
        total = jnp.sum(total, axis=1, keepdims=True)
        acc = acc / total
        log_sums = jnp.broadcast_to(top + jnp.log(total), (GROUP_HEADS * width, LANES))
        for head in range(GROUP_HEADS):
            here = slice(head * width, (head + 1) * width)
            cols = slice(head * HD, (head + 1) * HD)
            out_ref[block, cols, :] = acc[here, :].T[cols].astype(bf16)
            log_ref[block, :, here] = log_sums[here].T[:1]
        return 0

    loop(0, blocks, one_query_block, 0)


def attend_back_kernel(
    place, qt_ref, k_ref, v_ref, gt_ref, out_ref, log_ref, dq_ref, dkv_ref, sum_ref, dk_acc, dv_acc, dq_acc, delta_ref
):
    blocks, _, width = qt_ref.shape
    member = place[0]

    def prepare(block, _):
        products = gt_ref[block].astype(f32) * out_ref[block].astype(f32)
        for head in range(GROUP_HEADS):
            delta_ref[block, :, head * width : (head + 1) * width] = jnp.sum(
                products[head * HD : (head + 1) * HD], axis=0, keepdims=True
            )
        return 0

    lax.fori_loop(0, blocks, prepare, 0)
    dq_acc[...] = jnp.zeros_like(dq_acc)
    sum_ref[...] = jnp.zeros_like(sum_ref)

    head_at = lax.broadcasted_iota(jnp.int32, (width, GROUP_COLS), 1) // HD

    def one_key_block(key_block, _):
        slot = key_block ^ member
        dk_acc[...] = jnp.zeros_like(dk_acc)
        dv_acc[...] = jnp.zeros_like(dv_acc)

        def one_query_block(block, _):
            queries, grads = by_head(qt_ref[block ^ member]), by_head(gt_ref[block])
            prob = jnp.exp(dot(k_ref[slot], queries) - log_ref[block])
            grad_prob = dot(v_ref[slot], grads)
            grad_scores = (prob * (grad_prob - delta_ref[block])).astype(bf16)
            dv_acc[...] += dot_nt(prob.astype(bf16), grads)
            dk_acc[...] += dot_nt(grad_scores, queries)
            every = dot_tn(grad_scores, k_ref[slot])
            grad = jnp.zeros((width, GROUP_COLS), f32)
            for head in range(GROUP_HEADS):
                grad = jnp.where(head_at == head, every[head * width : (head + 1) * width], grad)
            dq_acc[block] += grad
            return 0

        loop(key_block, blocks, one_query_block, 0)
        dkv_ref[slot] = jnp.concatenate([dk_acc[...], dv_acc[...]], axis=1).astype(bf16)
        sum_ref[1:2, :] += jnp.sum(dv_acc[...], axis=0, keepdims=True)
        return 0

    loop(0, blocks, one_key_block, 0)

    def write(block, _):
        grads = dq_acc[block] * HEAD_SCALE
        dq_ref[block ^ member] = grads.astype(bf16)
        sum_ref[0:1, :] += jnp.sum(grads, axis=0, keepdims=True)
        return 0

    lax.fori_loop(0, blocks, write, 0)


def middle_kernel(
    place, att_ref, resid_ref, vec_ref, slab0, slab1, slab2, slab3, middle_ref, normed_ref, branch
):
    query_rows = att_ref.shape[2]
    for split in range(att_ref.shape[0] // HEAD_GROUPS):
        total = None
        for distance, slab_ref in enumerate((slab0, slab1, slab2, slab3)):
            part = dot_tn(att_ref[split * HEAD_GROUPS + (distance ^ place[1])], slab_ref[...])
            total = part if total is None else total + part
        branch[split * query_rows : (split + 1) * query_rows, :] = total
    middle = resid_ref[...] + centered(branch[...] + vec_ref[1:2, :])
    middle_ref[...] = middle
    normed_ref[...] = (middle * inverse_rms(middle) * vec_ref[2:3, :]).astype(bf16)


def mlp_kernel(place, *refs):
    normed, grads, slabs, (down_ref, bias_ref) = refs[:4], refs[4:8], refs[8:12], refs[12:14]
    norm_own, norm_far, norm_give, active_ref, hidden_ref, bias_grad, weight = refs[14:]
    rows, shard = normed[0].shape[0], slabs[0].shape[0]
    for distance, slab in enumerate(slabs):
        at = pl.multiple_of((distance ^ place[1]) * shard, shard)
        weight[pl.ds(at, shard), :] = slab[...]
    for tile in range(2):
        blocks = (tile, 2 + tile)
        tokens = jnp.concatenate([normed[at][...] for at in blocks], axis=0)
        grad = jnp.concatenate([grads[at][...] for at in blocks], axis=0)
        hidden = dot(tokens, weight[...]) + bias_ref[...]
        square = hidden * hidden
        bent = jnp.tanh(GELU_A * hidden * (1.0 + GELU_B * square))
        half = 0.5 * (1.0 + bent)
        active_ref[tile] = (hidden * half).astype(bf16)
        slope = half + 0.5 * hidden * (1.0 - bent * bent) * (GELU_A * (1.0 + 3.0 * GELU_B * square))
        grad_hidden = (dot_nt(grad, down_ref[...]) * slope).astype(bf16)
        hidden_ref[tile] = grad_hidden
        norm = dot_nt(grad_hidden, weight[...])
        bias = jnp.sum(grad_hidden.astype(f32), axis=0, keepdims=True)
        if tile:
            norm_give[0], norm_give[1] = norm[:rows].astype(bf16), norm[rows:].astype(bf16)
            bias_grad[...] += bias
        else:
            norm_own[...], norm_far[...] = norm[:rows], norm[rows:]
            bias_grad[...] = bias


def mlp_back_kernel(place, *refs):
    normed, grads, (active_ref, hidden_ref, down_ref) = refs[:4], refs[4:8], refs[8:11]
    branch_own, branch_far, branch_give = refs[11:14]
    pieces, (down_total, up_total) = refs[14:18], refs[18:]
    rows = normed[0].shape[0]
    wide = down_ref.shape[0] // PIECES
    piece = (pieces[0].shape[1] - wide) // 4
    shard = piece * PIECES
    mine, low = place[1], place[3]
    for tile in range(2):
        blocks = (tile, 2 + tile)
        tokens = jnp.concatenate([normed[at][...] for at in blocks], axis=0)
        grad = jnp.concatenate([grads[at][...] for at in blocks], axis=0)
        down, up = dot_tn(active_ref[tile], grad), dot_tn(tokens, hidden_ref[tile])
        branch = dot(active_ref[tile], down_ref[...])
        if tile:
            down_total[...] += down
            up_total[...] += up
            branch_give[0], branch_give[1] = branch[:rows].astype(bf16), branch[rows:].astype(bf16)
        else:
            down_total[...], up_total[...] = down, up
            branch_own[...], branch_far[...] = branch[:rows], branch[rows:]
    for near, target in enumerate(pieces):
        for side in range(2):
            at = (side << 2 | near) ^ low
            target[side, :wide] = down_total[pl.ds(pl.multiple_of(at * wide, wide), wide), :].astype(bf16)
            for distance in range(4):
                here = pl.multiple_of((distance ^ mine) * shard + at * piece, piece)
                start = wide + distance * piece
                target[side, start : start + piece] = up_total[pl.ds(here, piece), :].astype(bf16)


def branch_back_kernel(
    place,
    own_ref,
    core_ref,
    far_ref,
    middle_ref,
    top_ref,
    vec_ref,
    slab0,
    slab1,
    slab2,
    slab3,
    grad_middle_ref,
    grad_branch_ref,
    ga_ref,
    sum_ref,
):
    query_rows = ga_ref.shape[2]
    rows = top_ref.shape[0]
    grad = own_ref[...] + core_ref[0].astype(f32) + far_ref[...].astype(f32)
    middle = middle_ref[...]
    inverse = inverse_rms(middle)
    unit = middle * inverse
    sum_ref[0:1, :] = jnp.sum(grad * unit, axis=0, keepdims=True)
    grad_top = jnp.concatenate([top_ref[...].astype(f32), jnp.zeros((rows, 1), f32)], axis=1)
    grad_middle = grad_top + norm_back(grad * vec_ref[2:3, :], unit, inverse)
    grad_middle_ref[...] = grad_middle
    grad_branch = centered(grad_middle).astype(bf16)
    grad_branch_ref[...] = grad_branch
    for distance, slab_ref in enumerate((slab0, slab1, slab2, slab3)):
        product = dot_nt(slab_ref[...], grad_branch).astype(bf16)
        for split in range(ga_ref.shape[0] // HEAD_GROUPS):
            at = split * HEAD_GROUPS + (distance ^ place[1])
            ga_ref[at] = product[:, split * query_rows : (split + 1) * query_rows]
    sum_ref[1:2, :] = jnp.sum(grad_branch.astype(f32), axis=0, keepdims=True)
    sum_ref[2:3, :] = jnp.sum(centered(grad_top).astype(bf16).astype(f32), axis=0, keepdims=True)


def out_back_kernel(place, att_ref, grad_ref, sum_ref, bias_up_ref, near_ref, far_ref, grad_w):
    query_rows = att_ref.shape[2]
    groups, piece = HEAD_GROUPS, near_ref.shape[2] - EXTRA
    shard = D // groups
    mine, low = place[1], place[3]
    empty = jnp.zeros((1, D - 3 * shard), f32)
    for group in range(groups):
        weight = None
        for split in range(att_ref.shape[0] // groups):
            product = dot(
                att_ref[split * groups + group], grad_ref[split * query_rows : (split + 1) * query_rows, :]
            )
            weight = product if weight is None else weight + product
        lanes = slice(group * shard, (group + 1) * shard)
        grad_w[group * shard : (group + 1) * shard, :] = weight
        row = [sum_ref[at : at + 1, lanes] for at in (1, 0, 2)]
        grad_w[D + group : D + group + 1, :] = jnp.concatenate(row + [empty], axis=1)
    for distance in range(4):
        far, core = distance >> 1, distance & 1
        row = grad_w[pl.ds(D + (distance ^ mine), 1), :]
        up_row = jnp.zeros_like(row) if distance else bias_up_ref[...]
        extra = jnp.concatenate([row, up_row, jnp.zeros((EXTRA - 2, D), f32)], axis=0)

        def one(index, _, distance=distance, extra=extra):
            at = (distance ^ mine) * shard + (((index & 1) << 2 | index >> 1) ^ low) * piece
            part = grad_w[pl.ds(pl.multiple_of(at, piece), piece), :]
            target = (near_ref, far_ref)[distance & 1]
            target[distance >> 1, index] = jnp.concatenate([part, extra], axis=0).astype(bf16)
            return 0

        lax.fori_loop(0, PIECES, one, 0)


def sum_kernel(place, part0, part1, part2, part3, out_ref):
    out_ref[...] = sum(part[...].astype(f32) for part in (part0, part1, part2, part3)).astype(bf16)


def heads_back_kernel(place, normed_t_ref, query_t_ref, dq_ref, dkv_ref, sum_ref, near_ref, far_ref, aq, akv):
    blocks, query_rows, _ = dq_ref.shape
    rows = dkv_ref.shape[1]
    chunk = min(blocks, 4)
    for start in range(0, blocks, chunk):
        dkv = jnp.concatenate([dkv_ref[start + at] for at in range(chunk)], axis=0)
        dq = jnp.concatenate([dq_ref[start + at] for at in range(chunk)], axis=0)
        kv = dot(normed_t_ref[:, start * rows : (start + chunk) * rows], dkv)
        q = dot(query_t_ref[:, start * query_rows : (start + chunk) * query_rows], dq)
        if start:
            akv[...] += kv
            aq[...] += q
        else:
            akv[...], aq[...] = kv, q
    arrange_heads(place, aq, akv, sum_ref, near_ref, far_ref)


def arrange_heads(place, q_ref, kv_ref, sum_ref, near_ref, far_ref):
    mine, piece = place[1], near_ref.shape[2] - EXTRA
    shard = 2 * piece
    group = place[0] % HEAD_GROUPS
    for row in range(D // shard):
        relative = row ^ mine
        first = jnp.where(group // 2 == row, sum_ref[0:1, :], 0.0)
        second = jnp.where(2 + group // 2 == row, sum_ref[1:2, :], 0.0)
        extra = jnp.concatenate([first, second, jnp.zeros_like(first)], axis=1)
        extra = jnp.concatenate([extra, jnp.zeros((EXTRA - 1, extra.shape[1]), f32)], axis=0)
        for part in range(2):
            at_row = slice(row * shard + part * piece, row * shard + (part + 1) * piece)
            block = jnp.concatenate([q_ref[at_row, :], kv_ref[at_row, :]], axis=1)
            both = jnp.concatenate([block, extra], axis=0).astype(bf16)
            for core, target in enumerate((near_ref, far_ref)):

                @pl.when((relative & 1) == core)
                def _():
                    target[relative >> 1, part ^ ((place[3] >> 2) & 1)] = both


def rows_back_kernel(place, dq_ref, dkv_ref, slab0, slab1, slab2, slab3, keep_ref, give_ref, wq, wkv):
    load_heads(place, (slab0, slab1, slab2, slab3), wq, wkv)
    query_rows, half = dq_ref.shape[1], keep_ref.shape[0]
    own = pl.ds(pl.multiple_of(place[2] * query_rows, query_rows), query_rows)
    for core, ref in ((1, give_ref), (0, keep_ref)):

        def one(at, _, core=core, ref=ref):
            slot = at + core * half
            ref[at] = dot_nt(dkv_ref[slot], wkv[...]).astype(bf16)
            low = ref[at, own, :].astype(f32)
            ref[at, own, :] = (low + dot_nt(dq_ref[slot], wq[...])).astype(bf16)
            return 0

        loop(0, half, one, 0)


def by_near(own, got, pair, first):
    return ((0, own), (first, got), (3 - first, pair.at[0]), (3, pair.at[1]))


UP_FIRST, DOWN_FIRST, HEADS_FIRST = 1, 2, 2


def stream_back_kernel(place, near_ref, far_ref, last_ref, resid_ref, grad_middle_ref, vec_ref, out_ref):
    grad = near_ref[0].astype(f32) + far_ref[0].astype(f32) + last_ref[...].astype(f32)
    resid = resid_ref[...]
    inverse = inverse_rms(resid)
    unit = resid * inverse
    total = grad_middle_ref[...] + norm_back(grad * vec_ref[0:1, :], unit, inverse)
    out_ref[...] = (total - total[:, D - 1 :]).astype(bf16)[:, : D - 1]


def down_out_kernel(place, own, got, pair, out_ref):
    wide = own.shape[1]
    for near, part in by_near(own, got, pair, DOWN_FIRST):
        for side in range(2):
            at = pl.multiple_of(((side << 2 | near) ^ place[3]) * wide, wide)
            out_ref[pl.ds(at, wide), :] = part[side].astype(f32)


def up_out_kernel(place, own, got, pair, up_ref, out_ref):
    rows = out_ref.shape[0] // PIECES
    for near, part in by_near(own, got, pair, UP_FIRST):
        for side in range(2):
            at = pl.multiple_of(((side << 2 | near) ^ place[3]) * rows, rows)
            for slab in range(4):
                col = pl.multiple_of((slab ^ place[1]) * D, LANES)
                value = part[side, slab * rows : (slab + 1) * rows]
                up_ref[pl.ds(at, rows), pl.ds(col, D)] = value.astype(f32)
            out_ref[pl.ds(at, rows), :] = part[side, 4 * rows :].astype(f32)


def heads_out_kernel(place, own, got, pair, weight_ref, out_ref, gain_ref, bias_ref, pieces):
    piece = own.shape[1] - EXTRA
    mine, low = place[1], place[3]
    for near, part in by_near(own, got, pair, HEADS_FIRST):
        pieces[near] = part[...]
    for part in range(2):
        for group in range(HEAD_GROUPS):
            value = pieces[(group ^ low) & 3, part ^ ((low >> 2) & 1)].astype(f32)
            for kind in range(3):
                start = kind * D + group * GROUP_COLS
                out_ref[part * piece : (part + 1) * piece, start : start + GROUP_COLS] = value[
                    :piece, kind * GROUP_COLS : (kind + 1) * GROUP_COLS
                ]
    gain_ref[...] = jnp.sum(out_ref[...] * weight_ref[...].astype(f32), axis=1, keepdims=True)
    sides = []
    for side in range(2):
        group = ((2 * mine) & 3) + side
        value = pieces[(group ^ low) & 3, 0].astype(f32)[piece : piece + 1]
        sides.append(jnp.where(mine < 2, value[:, :GROUP_COLS], value[:, GROUP_COLS : 2 * GROUP_COLS]))
    bias_ref[...] = jnp.concatenate(sides, axis=1)


def solution(mesh):
    fsdp_count, ctx_count = mesh.shape["fsdp"], mesh.shape["ctx"]
    half = ctx_count // 2
    steps = half.bit_length() - 1
    ctx_steps = steps + 1
    splits = ctx_count // HEAD_GROUPS
    shard = D // fsdp_count

    def send(value, target):
        pairs = []
        for source in range(fsdp_count * ctx_count):
            row, at = target(*divmod(source, ctx_count))
            pairs.append((source, row * ctx_count + at))
        return lax.ppermute(value, AXES, pairs)

    def to_core(value):
        return send(value, lambda row, at: (row ^ 1, at))

    def to_chip_row(value):
        return send(value, lambda row, at: (row ^ 2, at))

    def to_ctx(value, bit):
        return send(value, lambda row, at: (row, at ^ bit))

    def swap_sequences(value):
        return send(
            value, lambda row, at: (row, at) if (row & 1) == at // half else (row ^ 1, at ^ half)
        )

    groups = [
        [(row + core) * ctx_count + side * half + at for core in range(2) for at in range(half)]
        for row in range(0, fsdp_count, 2)
        for side in range(2)
    ]

    def group_all_to_all(value):
        return lax.all_to_all(value, AXES, 0, 0, axis_index_groups=groups, tiled=True)

    def to_fsdp(value, distance):
        return send(value, lambda row, at: (row ^ distance, at))

    def over_fsdp(value):
        far = to_chip_row(value)
        return value, to_core(value), far, to_core(far)

    def to_square(values):
        return tuple(to_ctx(value, near + 1) for near, value in enumerate(values))

    def over_rest(value):
        for step in range(3, ctx_steps):
            value = value + to_ctx(value, 1 << step)
        return value

    def gather_square(value, first):
        got = to_ctx(value, first)
        return value, got, to_ctx(jnp.stack([value, got]), 3 - first)

    together = lax.optimization_barrier

    def widened(value):
        width = value.shape[-1]
        return value if width >= LANES else jnp.pad(value, ((0, 0), (0, 0), (0, LANES - width)))

    def local(
        stream_in,
        gain_attn,
        w_qkv,
        bias_qv,
        w_out,
        bias_out,
        gain_mlp,
        w_up,
        bias_up,
        w_down,
        bias_down,
        grad_out,
    ):
        rows = stream_in.shape[0]
        query_rows = rows // splits
        width = max(query_rows, LANES)
        fsdp_at, ctx_at = lax.axis_index("fsdp"), lax.axis_index("ctx")
        core, inner = fsdp_at & 1, ctx_at % half
        member = core * half + inner
        head_group = inner % HEAD_GROUPS
        place = jnp.stack([member, fsdp_at, member // HEAD_GROUPS, ctx_at & 7]).astype(jnp.int32)

        hidden = w_down.shape[0]
        stream = swap_sequences(stream_in)
        w_part, *up_sent = call(
            cut_kernel,
            "cut",
            (
                shape((shard, 3 * GROUP_COLS), bf16),
                *(shape((shard, hidden), bf16) for _ in range(fsdp_count)),
            ),
            (place, w_qkv, w_up),
        )
        vectors = jnp.concatenate(
            [
                part.astype(f32).reshape(1, -1)
                for part in (gain_attn, bias_out, gain_mlp, bias_down, bias_qv, bias_up)
            ],
            axis=1,
        )
        far_heads, far_vectors = together((to_chip_row(w_part), to_chip_row(vectors)))
        w_heads = (w_part, to_core(w_part), far_heads, to_core(far_heads))
        vectors = (vectors, to_core(vectors), far_vectors, to_core(far_vectors))
        far_heads, w_out_sent, stream = together((far_heads, w_out, stream))

        resid, unit = call(
            norm_kernel,
            "norm",
            (shape((rows, D), f32), shape((1, rows, D), bf16)),
            (place, stream),
        )
        got = to_square((unit,) * 3)
        *got, out_far = together((*got, to_chip_row(w_out_sent)))
        pieces = [unit, *got]
        for bit in range(2, steps):
            pieces.append(to_ctx(jnp.concatenate(pieces), 1 << bit))
        pieces = pieces + [to_core(piece) for piece in pieces]

        def by_row(values):
            ordered = []
            for row in range(fsdp_count):
                first = jnp.where((fsdp_at ^ row) & 1 == 0, values[0], values[1])
                second = jnp.where((fsdp_at ^ row) & 1 == 0, values[2], values[3])
                ordered.append(jnp.where((fsdp_at ^ row) < 2, first, second))
            return jnp.concatenate(ordered)

        vectors = by_row(vectors)
        vec = vectors[:, :D].reshape(fsdp_count, 4, shard).transpose(1, 0, 2).reshape(4, D)
        bias_heads = vectors[:, D : D + 2 * shard].reshape(2, HEAD_GROUPS, GROUP_COLS)
        bias_heads = lax.dynamic_index_in_dim(bias_heads, head_group, 1, keepdims=False)
        bias_hidden = lax.dynamic_slice_in_dim(vectors[:, D + 2 * shard :], fsdp_at, 1)
        gain = vec[0:1]

        head_weights = [pltpu.VMEM((D, GROUP_COLS), bf16), pltpu.VMEM((D, 2 * GROUP_COLS), bf16)]
        tokens = ctx_count * rows
        projected = (
            shape((ctx_count, rows, GROUP_COLS), bf16),
            shape((ctx_count, rows, GROUP_COLS), bf16),
            shape((ctx_count, query_rows, GROUP_COLS), bf16),
            shape((ctx_count, GROUP_COLS, query_rows), bf16),
        )
        work = 5 * tokens * D * GROUP_COLS
        if 4 * tokens * D * 2 < VMEM_LIMIT:
            keys, values, queries, queries_t = call(
                project_kernel,
                "project",
                projected,
                (place, *w_heads, gain, bias_heads, *pieces),
                flops=work,
                scratch=head_weights + [pltpu.VMEM((ctx_count, rows, D), bf16)],
            )
        else:
            normed = (jnp.concatenate(pieces).astype(f32) * gain).astype(bf16)
            block = lambda *dims: pl.BlockSpec((1,) + dims, lambda at: (at, 0, 0))
            whole = lambda *dims: pl.BlockSpec(dims, lambda at: (0,) * len(dims))
            keys, values, queries, queries_t = call(
                project_block_kernel,
                "project",
                projected,
                (place, *w_heads, bias_heads, normed),
                flops=work,
                scratch=head_weights,
                grid=(ctx_count,),
                in_specs=[pl.BlockSpec(memory_space=pltpu.SMEM)]
                + [whole(shard, 3 * GROUP_COLS)] * 4
                + [whole(2, GROUP_COLS), block(rows, D)],
                out_specs=(
                    block(rows, GROUP_COLS),
                    block(rows, GROUP_COLS),
                    block(query_rows, GROUP_COLS),
                    block(GROUP_COLS, query_rows),
                ),
            )
        queries_t = widened(queries_t)
        queries = jnp.pad(queries, ((0, 0), (0, width - query_rows), (0, 0)))
        pairs = GROUP_HEADS * query_rows * rows * ctx_count * (ctx_count + 1) // 2
        outs, logs = call(
            attend_kernel,
            "attend",
            (
                shape((ctx_count, GROUP_COLS, width), bf16),
                shape((ctx_count, 1, GROUP_HEADS * width), f32),
            ),
            (place, queries, keys, values),
            flops=4 * HD * pairs,
            exps=pairs,
            scratch=[pltpu.VMEM((ctx_count, GROUP_HEADS * width, rows), f32)],
        )
        outs, *up_got = together(
            (outs, *(to_fsdp(up_sent[distance], distance) for distance in (1, 2, 3)))
        )
        attended = group_all_to_all(outs[:, :, :query_rows])
        w_out_all = (w_out, to_core(w_out), out_far, to_core(out_far))
        top = swap_sequences(grad_out)
        grad_result = jnp.pad(top.astype(f32), ((0, 0), (0, 1)))
        grad_branch_mlp = centered(grad_result).astype(bf16)
        grads_mlp = over_fsdp(grad_branch_mlp)
        middle, normed_mlp = call(
            middle_kernel,
            "middle",
            (shape((rows, D), f32), shape((rows, D), bf16)),
            (place, attended, resid, vec, *w_out_all),
            flops=2 * rows * D * D,
            scratch=[pltpu.VMEM((rows, D), f32)],
        )
        piece = shard // PIECES
        normed_mlp, *late_pieces = together((normed_mlp, *pieces))
        if 4 * tokens * D * 2 < VMEM_LIMIT:
            normed_t, query_t = call(
                collect_kernel,
                "collect",
                (
                    shape((D, tokens), bf16),
                    shape((D, ctx_count * query_rows), bf16),
                ),
                (place, gain, *late_pieces),
                scratch=[pltpu.VMEM((ctx_count, rows, D), bf16)],
            )
        else:
            normed = (jnp.concatenate(late_pieces).astype(f32) * gain).astype(bf16)
            normed_query = lax.dynamic_index_in_dim(
                normed.reshape(ctx_count, splits, query_rows, D), place[2], 1, keepdims=False
            )
            normed_t, query_t = normed.reshape(tokens, D).T, normed_query.reshape(-1, D).T
        normed_all = over_fsdp(normed_mlp)
        far_normed, normed_t, query_t = together((normed_all[2], normed_t, query_t))
        normed_all = (normed_all[0], normed_all[1], far_normed, to_core(far_normed))
        norm_own, norm_far, norm_give, active, grad_hidden, bias_up_sum = call(
            mlp_kernel,
            "mlp",
            (
                shape((rows, D), f32),
                shape((rows, D), f32),
                shape((2, rows, D), bf16),
                shape((2, 2 * rows, hidden), bf16),
                shape((2, 2 * rows, hidden), bf16),
                shape((1, hidden), f32),
            ),
            (place, *normed_all, *grads_mlp, up_sent[0], *up_got, w_down, bias_hidden),
            flops=24 * rows * D * hidden,
            exps=4 * rows * hidden,
            scratch=[pltpu.VMEM((D, hidden), bf16)],
        )
        norm_got = to_core(norm_give)
        norm_far_got = to_chip_row((norm_far + norm_got[1]).astype(bf16))
        norm_sent, active, grad_hidden = together((norm_got, active, grad_hidden))
        branch_own, branch_far, branch_give, *both_sums = call(
            mlp_back_kernel,
            "mlp_back",
            (
                shape((rows, D), f32),
                shape((rows, D), f32),
                shape((2, rows, D), bf16),
                *(shape((2, hidden // PIECES + 4 * piece, D), bf16) for _ in range(4)),
            ),
            (place, *normed_all, *grads_mlp, active, grad_hidden, w_down),
            flops=LONG,
            scratch=[pltpu.VMEM((hidden, D), f32), pltpu.VMEM((D, hidden), f32)],
        )
        norm_far_got, branch_own, branch_far, branch_give, *both_sums = together(
            (norm_far_got, branch_own, branch_far, branch_give, *both_sums)
        )
        grad_middle, grad_branch, grad_attended, row_sums = call(
            branch_back_kernel,
            "branch_back",
            (
                shape((rows, D), f32),
                shape((rows, D), bf16),
                shape((ctx_count, GROUP_COLS, query_rows), bf16),
                shape((8, D), f32),
            ),
            (place, norm_own, norm_got, norm_far_got, middle, top, vec, *w_out_all),
            flops=4 * rows * D * D,
        )
        grads = group_all_to_all(grad_attended)
        out_near, out_give = call(
            out_back_kernel,
            "out_back",
            (shape((2, PIECES, piece + EXTRA, D), bf16), shape((2, PIECES, piece + EXTRA, D), bf16)),
            (place, attended, grad_branch, row_sums, bias_up_sum),
            flops=2 * rows * D * D,
            scratch=[pltpu.VMEM((D + 8, D), f32)],
        )
        out_sum = out_near + to_core(out_give)
        grads, out_sum = together((grads, out_sum))
        out_got = to_chip_row(out_sum[1])
        both_got = to_square(both_sums[1:])
        dq, dkv, head_sums = call(
            attend_back_kernel,
            "attend_back",
            (
                shape((ctx_count, width, GROUP_COLS), bf16),
                shape((ctx_count, rows, 2 * GROUP_COLS), bf16),
                shape((8, GROUP_COLS), f32),
            ),
            (place, queries_t, keys, values, widened(grads), outs, logs),
            flops=10 * HD * pairs,
            exps=pairs,
            scratch=[
                pltpu.VMEM((rows, GROUP_COLS), f32),
                pltpu.VMEM((rows, GROUP_COLS), f32),
                pltpu.VMEM((ctx_count, width, GROUP_COLS), f32),
                pltpu.VMEM((ctx_count, 1, GROUP_HEADS * width), f32),
            ],
        )
        dq = dq[:, :query_rows]
        dq, dkv, out_got = together((dq, dkv, out_got))

        head_shapes = tuple(
            shape((2, 2, shard // 2 + EXTRA, 3 * GROUP_COLS), bf16) for _ in range(2)
        )
        if 4 * tokens * D * 2 < VMEM_LIMIT:
            head_near, head_give = call(
                heads_back_kernel,
                "heads_back",
                head_shapes,
                (place, normed_t, query_t, dq, dkv, head_sums),
                flops=work,
                scratch=[pltpu.VMEM((D, GROUP_COLS), f32), pltpu.VMEM((D, 2 * GROUP_COLS), f32)],
            )
        else:
            flat_q, flat_kv = dq.reshape(-1, GROUP_COLS), dkv.reshape(tokens, 2 * GROUP_COLS)
            head_near, head_give = call(
                arrange_heads,
                "arrange_heads",
                head_shapes,
                (place, dot(query_t, flat_q), dot(normed_t, flat_kv), head_sums),
            )
        head_near, head_give, out_got, *both_got = together(
            (head_near, head_give, out_got, *both_got)
        )
        wide = hidden // PIECES
        (both_sum,) = call(
            sum_kernel,
            "sum",
            (shape((2, wide + fsdp_count * piece, D), bf16),),
            (place, both_sums[0], *both_got),
        )
        out_sums = [
            out_sum[0, 2 * near : 2 * near + 2] + out_got[2 * near : 2 * near + 2] for near in range(4)
        ]
        head_sum = head_near + to_core(head_give)
        dq, head_near, head_give, both_sum, *out_sums = together(
            (dq, head_sum[0], head_sum[1], both_sum, *out_sums)
        )
        head_got = to_chip_row(head_give)
        both_got = to_ctx(both_sum, 4)
        out_got = to_square(out_sums[1:])

        row_shapes = (shape((half, rows, D), bf16), shape((half, rows, D), bf16))
        if 4 * tokens * D * 2 < VMEM_LIMIT:
            keep_rows, give_rows = call(
                rows_back_kernel,
                "rows_back",
                row_shapes,
                (place, dq, dkv, *w_heads),
                flops=work,
                scratch=head_weights,
            )
        else:
            weights = by_row(w_heads)
            flat_q, flat_kv = dq.reshape(-1, GROUP_COLS), dkv.reshape(tokens, 2 * GROUP_COLS)
            grad_rows = dot_nt(flat_kv, weights[:, GROUP_COLS:]).reshape(
                ctx_count, splits, query_rows, D
            )
            grad_query = dot_nt(flat_q, weights[:, :GROUP_COLS]).reshape(ctx_count, 1, query_rows, D)
            chosen = (jnp.arange(splits) == place[2])[None, :, None, None]
            grad_rows = (grad_rows + jnp.where(chosen, grad_query, 0.0)).astype(bf16)
            grad_rows = grad_rows.reshape(ctx_count, rows, D)
            keep_rows, give_rows = grad_rows[:half], grad_rows[half:]
        keep_rows, give_rows, head_got, both_got, *out_got = together(
            (keep_rows, give_rows, head_got, both_got, *out_got)
        )

        def both_sides(own, other):
            return over_rest(jnp.stack([own[0] + other[1], own[1] + other[0]]))

        rows_got = to_core(give_rows)
        head_sum = head_near + head_got
        out_sum = sum(out_got, start=out_sums[0])
        rows_got, head_sum, out_sum, both_got = together((rows_got, head_sum, out_sum, both_got))
        head_got, out_got = to_ctx(head_sum, 4), to_ctx(out_sum, 4)
        up_sum = both_sides(both_sum[:, wide:], both_got[:, wide:])
        ups = [up_sum[:, distance * piece : (distance + 1) * piece] for distance in range(fsdp_count)]
        ups = [ups[0]] + [to_fsdp(ups[distance], distance) for distance in (1, 2, 3)]
        keep_rows, both_got, branch_give, *ups = together((keep_rows, both_got, branch_give, *ups))
        if steps == 2:
            near_rows, far_rows = (keep_rows[at::2] + rows_got[at::2] for at in range(2))
        else:
            both = keep_rows + rows_got
            for bit in reversed(range(2, steps)):
                both = both[: 1 << bit] + to_ctx(both[1 << bit :], 1 << bit)
            near_rows, far_rows = both[0::2], both[1::2]
        far_got = to_ctx(far_rows, 1)
        last_got = to_ctx(near_rows[1] + far_got[1], 2)
        downs = both_sides(both_sum[:, :wide], both_got[:, :wide])
        downs = gather_square(downs, DOWN_FIRST)
        branch_got = to_core(branch_give)
        branch_far_got = to_chip_row((branch_far + branch_got[1]).astype(bf16))
        head_got, out_got = together((head_got, out_got))
        branch_mlp = branch_own + branch_got[0] + branch_far_got + vec[3:4]
        stream_out = (middle + centered(branch_mlp)).astype(bf16)[:, : D - 1]
        stream_out = swap_sequences(stream_out)
        outs = both_sides(out_sum, out_got)
        sums = outs[0, piece:].astype(f32)
        ups = jnp.concatenate([*ups, outs[:, :piece]], axis=1)
        ups = gather_square(ups, UP_FIRST)
        heads = both_sides(head_sum, head_got)
        heads = gather_square(heads, HEADS_FIRST)
        (grad_stream,) = call(
            stream_back_kernel,
            "stream_back",
            (shape((rows, D - 1), bf16),),
            (place, near_rows, far_got, last_got, resid, grad_middle, vec),
        )
        grad_stream = swap_sequences(grad_stream)
        (grad_w_down,) = call(down_out_kernel, "down_out", (shape((hidden, D), f32),), (place, *downs))
        grad_w_up, grad_w_out = call(
            up_out_kernel,
            "up_out",
            (shape((shard, fsdp_count * hidden), f32), shape((shard, D), f32)),
            (place, *ups),
        )
        grad_w_qkv, grad_gain_attn, grad_bias_qv = call(
            heads_out_kernel,
            "heads_out",
            (
                shape((shard, 3 * D), f32),
                shape((shard, 1), f32),
                shape((1, 2 * shard), f32),
            ),
            (place, *heads, w_qkv),
            scratch=[pltpu.VMEM((4, 2, shard // 2 + EXTRA, 3 * GROUP_COLS), bf16)],
        )
        return (
            stream_out,
            grad_stream.astype(f32),
            grad_gain_attn.reshape(-1) / gain_attn.astype(f32),
            grad_w_qkv,
            grad_bias_qv.reshape(-1),
            grad_w_out,
            sums[0, :shard],
            sums[0, shard : 2 * shard],
            grad_w_up,
            sums[1],
            grad_w_down,
            sums[0, 2 * shard : 3 * shard],
        )

    rows_spec, matrix_spec, vector_spec = P(AXES, None), P("fsdp", None), P("fsdp")
    return jax.shard_map(
        local,
        mesh=mesh,
        in_specs=(
            rows_spec,
            vector_spec,
            matrix_spec,
            vector_spec,
            matrix_spec,
            vector_spec,
            vector_spec,
            matrix_spec,
            vector_spec,
            matrix_spec,
            vector_spec,
            rows_spec,
        ),
        out_specs=(
            rows_spec,
            rows_spec,
            vector_spec,
            matrix_spec,
            vector_spec,
            matrix_spec,
            vector_spec,
            vector_spec,
            matrix_spec,
            vector_spec,
            matrix_spec,
            vector_spec,
        ),
        check_vma=False,
    )
```

```python
import jax
import jax.numpy as jnp
from jax import lax
from jax.experimental import pallas as pl
from jax.experimental.pallas import tpu as pltpu
from jax.sharding import PartitionSpec as P

D = 768
H = 12
HD = 64
HEAD_GROUPS = 4
GROUP_HEADS = H // HEAD_GROUPS
GROUP_COLS = GROUP_HEADS * HD
HEAD_SCALE = HD ** (-0.5)
NORM_EPS = 1e-05
NEG_BIG = -1e30
GELU_A = 0.7978845608028654
GELU_B = 0.044715
LANES = 128
PIECES = 8
EXTRA = 8
LONG = 10**11
AXES = ("fsdp", "ctx")
VMEM_LIMIT = 120 << 19
UNROLL_BLOCKS = 8

f32 = jnp.float32
bf16 = jnp.bfloat16


def dot(left, right):
    return lax.dot_general(left, right, (((1,), (0,)), ((), ())), preferred_element_type=f32)


def dot_tn(left, right):
    return lax.dot_general(left, right, (((0,), (0,)), ((), ())), preferred_element_type=f32)


def dot_nt(left, right):
    return lax.dot_general(left, right, (((1,), (1,)), ((), ())), preferred_element_type=f32)


def centered(branch):
    return branch - jnp.mean(branch, axis=1, keepdims=True)


def inverse_rms(stream):
    return lax.rsqrt(jnp.mean(stream * stream, axis=1, keepdims=True) + NORM_EPS)


def norm_back(grad, unit, inverse):
    return inverse * (grad - unit * jnp.mean(grad * unit, axis=1, keepdims=True))


def slab_at(relative):
    return ((relative & 1) << 1) | (relative >> 1)


def loop(start, stop, body, carried):
    if isinstance(start, int) and isinstance(stop, int) and stop - start <= UNROLL_BLOCKS:
        for at in range(start, stop):
            carried = body(at, carried)
        return carried
    return lax.fori_loop(start, stop, body, carried)


def call(body, name, outs, args, flops=0, exps=0, scratch=(), **grid):
    moved = sum(x.size * x.dtype.itemsize for x in tuple(args) + tuple(outs))
    specs = dict(
        in_specs=[pl.BlockSpec(memory_space=pltpu.SMEM)]
        + [pl.BlockSpec(memory_space=pltpu.VMEM)] * (len(args) - 1),
        out_specs=tuple(pl.BlockSpec(memory_space=pltpu.VMEM) for _ in outs),
    )
    specs.update(grid)
    return pl.pallas_call(
        body,
        out_shape=tuple(outs),
        scratch_shapes=list(scratch),
        compiler_params=pltpu.CompilerParams(vmem_limit_bytes=VMEM_LIMIT),
        cost_estimate=pl.CostEstimate(flops=flops, bytes_accessed=moved, transcendentals=exps),
        name=name,
        **specs,
    )(*args)


def shape(dims, kind):
    return jax.ShapeDtypeStruct(tuple(dims), kind)


def norm_kernel(place, x_ref, resid_ref, unit_ref):
    x = x_ref[...].astype(f32)
    resid_ref[:, : D - 1] = x
    resid_ref[:, D - 1 :] = -jnp.sum(x, axis=1, keepdims=True)
    resid = resid_ref[...]
    unit_ref[0] = (resid * inverse_rms(resid)).astype(bf16)


def cut_kernel(place, qkv_ref, up_ref, heads_ref, *slabs):
    group = place[0] % HEAD_GROUPS
    for at in range(HEAD_GROUPS):

        @pl.when(group == at)
        def _():
            for kind in range(3):
                start = kind * D + at * GROUP_COLS
                heads_ref[:, kind * GROUP_COLS : (kind + 1) * GROUP_COLS] = qkv_ref[
                    :, start : start + GROUP_COLS
                ]

    hidden = slabs[0].shape[1]
    for distance, slab in enumerate(slabs):
        at = pl.multiple_of((distance ^ place[1]) * hidden, LANES)
        slab[...] = up_ref[:, pl.ds(at, hidden)]


def load_heads(place, slab_refs, wq, wkv):
    shard = slab_refs[0].shape[0]
    for distance, slab_ref in enumerate(slab_refs):
        at = pl.ds(pl.multiple_of((distance ^ place[1]) * shard, shard), shard)
        wq[at, :] = slab_ref[:, :GROUP_COLS]
        wkv[at, :] = slab_ref[:, GROUP_COLS:]


def project(place, normed_ref, slots, bias_ref, k_ref, v_ref, q_ref, qt_ref, wq, wkv):
    rows, query_rows = normed_ref.shape[1], qt_ref.shape[2]
    own = pl.ds(pl.multiple_of(place[2] * query_rows, query_rows), query_rows)
    for start in range(0, slots, 2):
        pair = range(start, min(start + 2, slots))
        normed = jnp.concatenate([normed_ref[slot] for slot in pair], axis=0)
        both = dot(normed, wkv[...])
        keys, values = both[:, :GROUP_COLS], both[:, GROUP_COLS:] + bias_ref[1:2, :]
        mine = jnp.concatenate([normed_ref[slot, own, :] for slot in pair], axis=0)
        queries = (dot(mine, wq[...]) + bias_ref[0:1, :]) * HEAD_SCALE
        for at, slot in enumerate(pair):
            here = slice(at * rows, (at + 1) * rows)
            k_ref[slot] = keys[here].astype(bf16)
            v_ref[slot] = values[here].astype(bf16)
            query = queries[at * query_rows : (at + 1) * query_rows]
            q_ref[slot], qt_ref[slot] = query.astype(bf16), query.T.astype(bf16)


def project_kernel(place, *refs):
    slabs, (gain_ref, bias_ref) = refs[:4], refs[4:6]
    pieces = refs[6:-7]
    k_ref, v_ref, q_ref, qt_ref, wq, wkv, normed_ref = refs[-7:]
    load_heads(place, slabs, wq, wkv)
    gain = gain_ref[0:1, :]
    slot = 0
    for ref in pieces:
        for at in range(ref.shape[0]):
            normed_ref[slot] = (ref[at].astype(f32) * gain).astype(bf16)
            slot += 1
    project(place, normed_ref, slot, bias_ref, k_ref, v_ref, q_ref, qt_ref, wq, wkv)


def project_block_kernel(place, *refs):
    slabs, bias_ref, normed_ref = refs[:4], refs[4], refs[5]
    k_ref, v_ref, q_ref, qt_ref, wq, wkv = refs[6:]

    @pl.when(pl.program_id(0) == 0)
    def _():
        load_heads(place, slabs, wq, wkv)

    slots = normed_ref.shape[0]
    project(place, normed_ref, slots, bias_ref, k_ref, v_ref, q_ref, qt_ref, wq, wkv)


def collect_kernel(place, gain_ref, *refs):
    pieces, (normed_t_ref, query_t_ref, normed_ref) = refs[:-3], refs[-3:]
    blocks, rows, _ = normed_ref.shape
    query_rows = query_t_ref.shape[1] // blocks
    own = pl.ds(pl.multiple_of(place[2] * query_rows, query_rows), query_rows)
    gain, slot = gain_ref[0:1, :], 0
    for ref in pieces:
        for at in range(ref.shape[0]):
            normed_ref[slot] = (ref[at].astype(f32) * gain).astype(bf16)
            normed_t_ref[:, slot * rows : (slot + 1) * rows] = normed_ref[slot].T
            mine = normed_ref[slot, own, :].T
            query_t_ref[:, slot * query_rows : (slot + 1) * query_rows] = mine
            slot += 1


def by_head(value):
    head = lax.broadcasted_iota(jnp.int32, value.shape, 0) // HD
    zero = jnp.zeros_like(value)
    return jnp.concatenate([jnp.where(head == at, value, zero) for at in range(GROUP_HEADS)], axis=1)


def by_head_rows(value):
    head = lax.broadcasted_iota(jnp.int32, value.shape, 1) // HD
    zero = jnp.zeros_like(value)
    return jnp.concatenate([jnp.where(head == at, value, zero) for at in range(GROUP_HEADS)], axis=0)


def lane_halves(value, join):
    return join(value[:, :LANES], value[:, LANES:])


def attend_kernel(place, q_ref, k_ref, v_ref, out_ref, log_ref, score_ref):
    blocks, width, _ = q_ref.shape
    member = place[0]

    def one_query_block(block, _):
        queries = by_head_rows(q_ref[block ^ member])

        def one_score(key_block, top):
            scores = dot_nt(queries, k_ref[key_block ^ member])
            score_ref[key_block] = scores
            return jnp.maximum(top, lane_halves(scores, jnp.maximum))

        top = loop(0, block + 1, one_score, jnp.full((GROUP_HEADS * width, LANES), NEG_BIG, f32))
        top = jnp.max(top, axis=1, keepdims=True)

        def one_value(key_block, carried):
            total, acc = carried
            weights = jnp.exp(score_ref[key_block] - top)
            total = total + lane_halves(weights, jnp.add)
            return total, acc + dot(weights.astype(bf16), v_ref[key_block ^ member])

        start_state = (
            jnp.zeros((GROUP_HEADS * width, LANES), f32),
            jnp.zeros((GROUP_HEADS * width, GROUP_COLS), f32),
        )
        total, acc = loop(0, block + 1, one_value, start_state)
        total = jnp.sum(total, axis=1, keepdims=True)
        acc = acc / total
        log_sums = jnp.broadcast_to(top + jnp.log(total), (GROUP_HEADS * width, LANES))
        for head in range(GROUP_HEADS):
            here = slice(head * width, (head + 1) * width)
            cols = slice(head * HD, (head + 1) * HD)
            out_ref[block, cols, :] = acc[here, :].T[cols].astype(bf16)
            log_ref[block, :, here] = log_sums[here].T[:1]
        return 0

    loop(0, blocks, one_query_block, 0)


def attend_back_kernel(
    place, qt_ref, k_ref, v_ref, gt_ref, out_ref, log_ref, dq_ref, dkv_ref, sum_ref, dk_acc, dv_acc, dq_acc, delta_ref
):
    blocks, _, width = qt_ref.shape
    member = place[0]

    def prepare(block, _):
        products = gt_ref[block].astype(f32) * out_ref[block].astype(f32)
        for head in range(GROUP_HEADS):
            delta_ref[block, :, head * width : (head + 1) * width] = jnp.sum(
                products[head * HD : (head + 1) * HD], axis=0, keepdims=True
            )
        return 0

    lax.fori_loop(0, blocks, prepare, 0)
    dq_acc[...] = jnp.zeros_like(dq_acc)
    sum_ref[...] = jnp.zeros_like(sum_ref)

    head_at = lax.broadcasted_iota(jnp.int32, (width, GROUP_COLS), 1) // HD

    def one_key_block(key_block, _):
        slot = key_block ^ member
        dk_acc[...] = jnp.zeros_like(dk_acc)
        dv_acc[...] = jnp.zeros_like(dv_acc)

        def one_query_block(block, _):
            queries, grads = by_head(qt_ref[block ^ member]), by_head(gt_ref[block])
            prob = jnp.exp(dot(k_ref[slot], queries) - log_ref[block])
            grad_prob = dot(v_ref[slot], grads)
            grad_scores = (prob * (grad_prob - delta_ref[block])).astype(bf16)
            dv_acc[...] += dot_nt(prob.astype(bf16), grads)
            dk_acc[...] += dot_nt(grad_scores, queries)
            every = dot_tn(grad_scores, k_ref[slot])
            grad = jnp.zeros((width, GROUP_COLS), f32)
            for head in range(GROUP_HEADS):
                grad = jnp.where(head_at == head, every[head * width : (head + 1) * width], grad)
            dq_acc[block] += grad
            return 0

        loop(key_block, blocks, one_query_block, 0)
        dkv_ref[slot] = jnp.concatenate([dk_acc[...], dv_acc[...]], axis=1).astype(bf16)
        sum_ref[1:2, :] += jnp.sum(dv_acc[...], axis=0, keepdims=True)
        return 0

    loop(0, blocks, one_key_block, 0)

    def write(block, _):
        grads = dq_acc[block] * HEAD_SCALE
        dq_ref[block ^ member] = grads.astype(bf16)
        sum_ref[0:1, :] += jnp.sum(grads, axis=0, keepdims=True)
        return 0

    lax.fori_loop(0, blocks, write, 0)


def middle_kernel(
    place, att_ref, resid_ref, vec_ref, slab0, slab1, slab2, slab3, middle_ref, normed_ref, branch
):
    query_rows = att_ref.shape[2]
    for split in range(att_ref.shape[0] // HEAD_GROUPS):
        total = None
        for distance, slab_ref in enumerate((slab0, slab1, slab2, slab3)):
            part = dot_tn(att_ref[split * HEAD_GROUPS + (distance ^ place[1])], slab_ref[...])
            total = part if total is None else total + part
        branch[split * query_rows : (split + 1) * query_rows, :] = total
    middle = resid_ref[...] + centered(branch[...] + vec_ref[1:2, :])
    middle_ref[...] = middle
    normed_ref[...] = (middle * inverse_rms(middle) * vec_ref[2:3, :]).astype(bf16)


def mlp_kernel(place, *refs):
    normed, grads, slabs, (down_ref, bias_ref) = refs[:4], refs[4:8], refs[8:12], refs[12:14]
    norm_own, norm_far, norm_give, active_ref, hidden_ref, bias_grad, weight = refs[14:]
    rows, shard = normed[0].shape[0], slabs[0].shape[0]
    for distance, slab in enumerate(slabs):
        at = pl.multiple_of((distance ^ place[1]) * shard, shard)
        weight[pl.ds(at, shard), :] = slab[...]
    for tile in range(2):
        blocks = (tile, 2 + tile)
        tokens = jnp.concatenate([normed[at][...] for at in blocks], axis=0)
        grad = jnp.concatenate([grads[at][...] for at in blocks], axis=0)
        hidden = dot(tokens, weight[...]) + bias_ref[...]
        square = hidden * hidden
        bent = jnp.tanh(GELU_A * hidden * (1.0 + GELU_B * square))
        half = 0.5 * (1.0 + bent)
        active_ref[tile] = (hidden * half).astype(bf16)
        slope = half + 0.5 * hidden * (1.0 - bent * bent) * (GELU_A * (1.0 + 3.0 * GELU_B * square))
        grad_hidden = (dot_nt(grad, down_ref[...]) * slope).astype(bf16)
        hidden_ref[tile] = grad_hidden
        norm = dot_nt(grad_hidden, weight[...])
        bias = jnp.sum(grad_hidden.astype(f32), axis=0, keepdims=True)
        if tile:
            norm_give[0], norm_give[1] = norm[:rows].astype(bf16), norm[rows:].astype(bf16)
            bias_grad[...] += bias
        else:
            norm_own[...], norm_far[...] = norm[:rows], norm[rows:]
            bias_grad[...] = bias


def mlp_back_kernel(place, *refs):
    normed, grads, (active_ref, hidden_ref, down_ref) = refs[:4], refs[4:8], refs[8:11]
    branch_own, branch_far, branch_give = refs[11:14]
    pieces, (down_total, up_total) = refs[14:18], refs[18:]
    rows = normed[0].shape[0]
    wide = down_ref.shape[0] // PIECES
    piece = (pieces[0].shape[1] - wide) // 4
    shard = piece * PIECES
    mine, low = place[1], place[3]
    for tile in range(2):
        blocks = (tile, 2 + tile)
        tokens = jnp.concatenate([normed[at][...] for at in blocks], axis=0)
        grad = jnp.concatenate([grads[at][...] for at in blocks], axis=0)
        down, up = dot_tn(active_ref[tile], grad), dot_tn(tokens, hidden_ref[tile])
        branch = dot(active_ref[tile], down_ref[...])
        if tile:
            down_total[...] += down
            up_total[...] += up
            branch_give[0], branch_give[1] = branch[:rows].astype(bf16), branch[rows:].astype(bf16)
        else:
            down_total[...], up_total[...] = down, up
            branch_own[...], branch_far[...] = branch[:rows], branch[rows:]
    for near, target in enumerate(pieces):
        for side in range(2):
            at = (side << 2 | near) ^ low
            target[side, :wide] = down_total[pl.ds(pl.multiple_of(at * wide, wide), wide), :].astype(bf16)
            for distance in range(4):
                here = pl.multiple_of((distance ^ mine) * shard + at * piece, piece)
                start = wide + distance * piece
                target[side, start : start + piece] = up_total[pl.ds(here, piece), :].astype(bf16)


def branch_back_kernel(
    place,
    own_ref,
    core_ref,
    far_ref,
    middle_ref,
    top_ref,
    vec_ref,
    slab0,
    slab1,
    slab2,
    slab3,
    grad_middle_ref,
    grad_branch_ref,
    ga_ref,
    sum_ref,
):
    query_rows = ga_ref.shape[2]
    rows = top_ref.shape[0]
    grad = own_ref[...] + core_ref[0].astype(f32) + far_ref[...].astype(f32)
    middle = middle_ref[...]
    inverse = inverse_rms(middle)
    unit = middle * inverse
    sum_ref[0:1, :] = jnp.sum(grad * unit, axis=0, keepdims=True)
    grad_top = jnp.concatenate([top_ref[...].astype(f32), jnp.zeros((rows, 1), f32)], axis=1)
    grad_middle = grad_top + norm_back(grad * vec_ref[2:3, :], unit, inverse)
    grad_middle_ref[...] = grad_middle
    grad_branch = centered(grad_middle).astype(bf16)
    grad_branch_ref[...] = grad_branch
    for distance, slab_ref in enumerate((slab0, slab1, slab2, slab3)):
        product = dot_nt(slab_ref[...], grad_branch).astype(bf16)
        for split in range(ga_ref.shape[0] // HEAD_GROUPS):
            at = split * HEAD_GROUPS + (distance ^ place[1])
            ga_ref[at] = product[:, split * query_rows : (split + 1) * query_rows]
    sum_ref[1:2, :] = jnp.sum(grad_branch.astype(f32), axis=0, keepdims=True)
    sum_ref[2:3, :] = jnp.sum(centered(grad_top).astype(bf16).astype(f32), axis=0, keepdims=True)


def out_back_kernel(place, att_ref, grad_ref, sum_ref, bias_up_ref, near_ref, far_ref, grad_w):
    query_rows = att_ref.shape[2]
    groups, piece = HEAD_GROUPS, near_ref.shape[2] - EXTRA
    shard = D // groups
    mine, low = place[1], place[3]
    empty = jnp.zeros((1, D - 3 * shard), f32)
    for group in range(groups):
        weight = None
        for split in range(att_ref.shape[0] // groups):
            product = dot(
                att_ref[split * groups + group], grad_ref[split * query_rows : (split + 1) * query_rows, :]
            )
            weight = product if weight is None else weight + product
        lanes = slice(group * shard, (group + 1) * shard)
        grad_w[group * shard : (group + 1) * shard, :] = weight
        row = [sum_ref[at : at + 1, lanes] for at in (1, 0, 2)]
        grad_w[D + group : D + group + 1, :] = jnp.concatenate(row + [empty], axis=1)
    for distance in range(4):
        far, core = distance >> 1, distance & 1
        row = grad_w[pl.ds(D + (distance ^ mine), 1), :]
        up_row = jnp.zeros_like(row) if distance else bias_up_ref[...]
        extra = jnp.concatenate([row, up_row, jnp.zeros((EXTRA - 2, D), f32)], axis=0)

        def one(index, _, distance=distance, extra=extra):
            at = (distance ^ mine) * shard + (((index & 1) << 2 | index >> 1) ^ low) * piece
            part = grad_w[pl.ds(pl.multiple_of(at, piece), piece), :]
            target = (near_ref, far_ref)[distance & 1]
            target[distance >> 1, index] = jnp.concatenate([part, extra], axis=0).astype(bf16)
            return 0

        lax.fori_loop(0, PIECES, one, 0)


def sum_kernel(place, part0, part1, part2, part3, out_ref):
    out_ref[...] = sum(part[...].astype(f32) for part in (part0, part1, part2, part3)).astype(bf16)


def heads_back_kernel(place, normed_t_ref, query_t_ref, dq_ref, dkv_ref, sum_ref, near_ref, far_ref, aq, akv):
    blocks, query_rows, _ = dq_ref.shape
    rows = dkv_ref.shape[1]
    chunk = min(blocks, 4)
    for start in range(0, blocks, chunk):
        dkv = jnp.concatenate([dkv_ref[start + at] for at in range(chunk)], axis=0)
        dq = jnp.concatenate([dq_ref[start + at] for at in range(chunk)], axis=0)
        kv = dot(normed_t_ref[:, start * rows : (start + chunk) * rows], dkv)
        q = dot(query_t_ref[:, start * query_rows : (start + chunk) * query_rows], dq)
        if start:
            akv[...] += kv
            aq[...] += q
        else:
            akv[...], aq[...] = kv, q
    arrange_heads(place, aq, akv, sum_ref, near_ref, far_ref)


def arrange_heads(place, q_ref, kv_ref, sum_ref, near_ref, far_ref):
    mine, piece = place[1], near_ref.shape[2] - EXTRA
    shard = 2 * piece
    group = place[0] % HEAD_GROUPS
    for row in range(D // shard):
        relative = row ^ mine
        first = jnp.where(group // 2 == row, sum_ref[0:1, :], 0.0)
        second = jnp.where(2 + group // 2 == row, sum_ref[1:2, :], 0.0)
        extra = jnp.concatenate([first, second, jnp.zeros_like(first)], axis=1)
        extra = jnp.concatenate([extra, jnp.zeros((EXTRA - 1, extra.shape[1]), f32)], axis=0)
        for part in range(2):
            at_row = slice(row * shard + part * piece, row * shard + (part + 1) * piece)
            block = jnp.concatenate([q_ref[at_row, :], kv_ref[at_row, :]], axis=1)
            both = jnp.concatenate([block, extra], axis=0).astype(bf16)
            for core, target in enumerate((near_ref, far_ref)):

                @pl.when((relative & 1) == core)
                def _():
                    target[relative >> 1, part ^ ((place[3] >> 2) & 1)] = both


def rows_back_kernel(place, dq_ref, dkv_ref, slab0, slab1, slab2, slab3, keep_ref, give_ref, wq, wkv):
    load_heads(place, (slab0, slab1, slab2, slab3), wq, wkv)
    query_rows, half = dq_ref.shape[1], keep_ref.shape[0]
    own = pl.ds(pl.multiple_of(place[2] * query_rows, query_rows), query_rows)
    for core, ref in ((1, give_ref), (0, keep_ref)):

        def one(at, _, core=core, ref=ref):
            slot = at + core * half
            ref[at] = dot_nt(dkv_ref[slot], wkv[...]).astype(bf16)
            low = ref[at, own, :].astype(f32)
            ref[at, own, :] = (low + dot_nt(dq_ref[slot], wq[...])).astype(bf16)
            return 0

        loop(0, half, one, 0)


def by_near(own, got, pair, first):
    return ((0, own), (first, got), (3 - first, pair.at[0]), (3, pair.at[1]))


UP_FIRST, DOWN_FIRST, HEADS_FIRST = 1, 2, 2


def stream_back_kernel(place, near_ref, far_ref, last_ref, resid_ref, grad_middle_ref, vec_ref, out_ref):
    grad = near_ref[0].astype(f32) + far_ref[0].astype(f32) + last_ref[...].astype(f32)
    resid = resid_ref[...]
    inverse = inverse_rms(resid)
    unit = resid * inverse
    total = grad_middle_ref[...] + norm_back(grad * vec_ref[0:1, :], unit, inverse)
    out_ref[...] = (total - total[:, D - 1 :]).astype(bf16)[:, : D - 1]


def down_out_kernel(place, own, got, pair, out_ref):
    wide = own.shape[1]
    for near, part in by_near(own, got, pair, DOWN_FIRST):
        for side in range(2):
            at = pl.multiple_of(((side << 2 | near) ^ place[3]) * wide, wide)
            out_ref[pl.ds(at, wide), :] = part[side].astype(f32)


def up_out_kernel(place, own, got, pair, up_ref, out_ref):
    rows = out_ref.shape[0] // PIECES
    for near, part in by_near(own, got, pair, UP_FIRST):
        for side in range(2):
            at = pl.multiple_of(((side << 2 | near) ^ place[3]) * rows, rows)
            for slab in range(4):
                col = pl.multiple_of((slab ^ place[1]) * D, LANES)
                value = part[side, slab * rows : (slab + 1) * rows]
                up_ref[pl.ds(at, rows), pl.ds(col, D)] = value.astype(f32)
            out_ref[pl.ds(at, rows), :] = part[side, 4 * rows :].astype(f32)


def heads_out_kernel(place, own, got, pair, weight_ref, out_ref, gain_ref, bias_ref, pieces):
    piece = own.shape[1] - EXTRA
    mine, low = place[1], place[3]
    for near, part in by_near(own, got, pair, HEADS_FIRST):
        pieces[near] = part[...]
    for part in range(2):
        for group in range(HEAD_GROUPS):
            value = pieces[(group ^ low) & 3, part ^ ((low >> 2) & 1)].astype(f32)
            for kind in range(3):
                start = kind * D + group * GROUP_COLS
                out_ref[part * piece : (part + 1) * piece, start : start + GROUP_COLS] = value[
                    :piece, kind * GROUP_COLS : (kind + 1) * GROUP_COLS
                ]
    gain_ref[...] = jnp.sum(out_ref[...] * weight_ref[...].astype(f32), axis=1, keepdims=True)
    sides = []
    for side in range(2):
        group = ((2 * mine) & 3) + side
        value = pieces[(group ^ low) & 3, 0].astype(f32)[piece : piece + 1]
        sides.append(jnp.where(mine < 2, value[:, :GROUP_COLS], value[:, GROUP_COLS : 2 * GROUP_COLS]))
    bias_ref[...] = jnp.concatenate(sides, axis=1)


def solution(mesh):
    fsdp_count, ctx_count = mesh.shape["fsdp"], mesh.shape["ctx"]
    half = ctx_count // 2
    steps = half.bit_length() - 1
    ctx_steps = steps + 1
    splits = ctx_count // HEAD_GROUPS
    shard = D // fsdp_count

    def send(value, target):
        pairs = []
        for source in range(fsdp_count * ctx_count):
            row, at = target(*divmod(source, ctx_count))
            pairs.append((source, row * ctx_count + at))
        return lax.ppermute(value, AXES, pairs)

    def to_core(value):
        return send(value, lambda row, at: (row ^ 1, at))

    def to_chip_row(value):
        return send(value, lambda row, at: (row ^ 2, at))

    def to_ctx(value, bit):
        return send(value, lambda row, at: (row, at ^ bit))

    def swap_sequences(value):
        return send(
            value, lambda row, at: (row, at) if (row & 1) == at // half else (row ^ 1, at ^ half)
        )

    groups = [
        [(row + core) * ctx_count + side * half + at for core in range(2) for at in range(half)]
        for row in range(0, fsdp_count, 2)
        for side in range(2)
    ]

    def group_all_to_all(value):
        return lax.all_to_all(value, AXES, 0, 0, axis_index_groups=groups, tiled=True)

    def to_fsdp(value, distance):
        return send(value, lambda row, at: (row ^ distance, at))

    def over_fsdp(value):
        far = to_chip_row(value)
        return value, to_core(value), far, to_core(far)

    def to_square(values):
        return tuple(to_ctx(value, near + 1) for near, value in enumerate(values))

    def over_rest(value):
        for step in range(3, ctx_steps):
            value = value + to_ctx(value, 1 << step)
        return value

    def gather_square(value, first):
        got = to_ctx(value, first)
        return value, got, to_ctx(jnp.stack([value, got]), 3 - first)

    together = lax.optimization_barrier

    def widened(value):
        width = value.shape[-1]
        return value if width >= LANES else jnp.pad(value, ((0, 0), (0, 0), (0, LANES - width)))

    def local(
        stream_in,
        gain_attn,
        w_qkv,
        bias_qv,
        w_out,
        bias_out,
        gain_mlp,
        w_up,
        bias_up,
        w_down,
        bias_down,
        grad_out,
    ):
        rows = stream_in.shape[0]
        query_rows = rows // splits
        width = max(query_rows, LANES)
        fsdp_at, ctx_at = lax.axis_index("fsdp"), lax.axis_index("ctx")
        core, inner = fsdp_at & 1, ctx_at % half
        member = core * half + inner
        head_group = inner % HEAD_GROUPS
        place = jnp.stack([member, fsdp_at, member // HEAD_GROUPS, ctx_at & 7]).astype(jnp.int32)

        hidden = w_down.shape[0]
        stream = swap_sequences(stream_in)
        w_part, *up_sent = call(
            cut_kernel,
            "cut",
            (
                shape((shard, 3 * GROUP_COLS), bf16),
                *(shape((shard, hidden), bf16) for _ in range(fsdp_count)),
            ),
            (place, w_qkv, w_up),
        )
        vectors = jnp.concatenate(
            [
                part.astype(f32).reshape(1, -1)
                for part in (gain_attn, bias_out, gain_mlp, bias_down, bias_qv, bias_up)
            ],
            axis=1,
        )
        far_heads, far_vectors = together((to_chip_row(w_part), to_chip_row(vectors)))
        w_heads = (w_part, to_core(w_part), far_heads, to_core(far_heads))
        vectors = (vectors, to_core(vectors), far_vectors, to_core(far_vectors))
        far_heads, w_out_sent, stream = together((far_heads, w_out, stream))

        resid, unit = call(
            norm_kernel,
            "norm",
            (shape((rows, D), f32), shape((1, rows, D), bf16)),
            (place, stream),
        )
        got = to_square((unit,) * 3)
        *got, out_far = together((*got, to_chip_row(w_out_sent)))
        pieces = [unit, *got]
        for bit in range(2, steps):
            pieces.append(to_ctx(jnp.concatenate(pieces), 1 << bit))
        pieces = pieces + [to_core(piece) for piece in pieces]

        def by_row(values):
            ordered = []
            for row in range(fsdp_count):
                first = jnp.where((fsdp_at ^ row) & 1 == 0, values[0], values[1])
                second = jnp.where((fsdp_at ^ row) & 1 == 0, values[2], values[3])
                ordered.append(jnp.where((fsdp_at ^ row) < 2, first, second))
            return jnp.concatenate(ordered)

        vectors = by_row(vectors)
        vec = vectors[:, :D].reshape(fsdp_count, 4, shard).transpose(1, 0, 2).reshape(4, D)
        bias_heads = vectors[:, D : D + 2 * shard].reshape(2, HEAD_GROUPS, GROUP_COLS)
        bias_heads = lax.dynamic_index_in_dim(bias_heads, head_group, 1, keepdims=False)
        bias_hidden = lax.dynamic_slice_in_dim(vectors[:, D + 2 * shard :], fsdp_at, 1)

        head_weights = [pltpu.VMEM((D, GROUP_COLS), bf16), pltpu.VMEM((D, 2 * GROUP_COLS), bf16)]
        tokens = ctx_count * rows
        projected = (
            shape((ctx_count, rows, GROUP_COLS), bf16),
            shape((ctx_count, rows, GROUP_COLS), bf16),
            shape((ctx_count, query_rows, GROUP_COLS), bf16),
            shape((ctx_count, GROUP_COLS, query_rows), bf16),
        )
        work = 5 * tokens * D * GROUP_COLS
        if 4 * tokens * D * 2 < VMEM_LIMIT:
            keys, values, queries, queries_t = call(
                project_kernel,
                "project",
                projected,
                (place, *w_heads, vec, bias_heads, *pieces),
                flops=work,
                scratch=head_weights + [pltpu.VMEM((ctx_count, rows, D), bf16)],
            )
        else:
            normed = (jnp.concatenate(pieces).astype(f32) * vec[0:1]).astype(bf16)
            block = lambda *dims: pl.BlockSpec((1,) + dims, lambda at: (at, 0, 0))
            whole = lambda *dims: pl.BlockSpec(dims, lambda at: (0,) * len(dims))
            keys, values, queries, queries_t = call(
                project_block_kernel,
                "project",
                projected,
                (place, *w_heads, bias_heads, normed),
                flops=work,
                scratch=head_weights,
                grid=(ctx_count,),
                in_specs=[pl.BlockSpec(memory_space=pltpu.SMEM)]
                + [whole(shard, 3 * GROUP_COLS)] * 4
                + [whole(2, GROUP_COLS), block(rows, D)],
                out_specs=(
                    block(rows, GROUP_COLS),
                    block(rows, GROUP_COLS),
                    block(query_rows, GROUP_COLS),
                    block(GROUP_COLS, query_rows),
                ),
            )
        queries_t = widened(queries_t)
        queries = jnp.pad(queries, ((0, 0), (0, width - query_rows), (0, 0)))
        pairs = GROUP_HEADS * query_rows * rows * ctx_count * (ctx_count + 1) // 2
        outs, logs = call(
            attend_kernel,
            "attend",
            (
                shape((ctx_count, GROUP_COLS, width), bf16),
                shape((ctx_count, 1, GROUP_HEADS * width), f32),
            ),
            (place, queries, keys, values),
            flops=4 * HD * pairs,
            exps=pairs,
            scratch=[pltpu.VMEM((ctx_count, GROUP_HEADS * width, rows), f32)],
        )
        outs, *up_got = together(
            (outs, *(to_fsdp(up_sent[distance], distance) for distance in (1, 2, 3)))
        )
        attended = group_all_to_all(outs[:, :, :query_rows])
        w_out_all = (w_out, to_core(w_out), out_far, to_core(out_far))
        top = swap_sequences(grad_out)
        grad_result = jnp.pad(top.astype(f32), ((0, 0), (0, 1)))
        grad_branch_mlp = centered(grad_result).astype(bf16)
        grads_mlp = over_fsdp(grad_branch_mlp)
        middle, normed_mlp = call(
            middle_kernel,
            "middle",
            (shape((rows, D), f32), shape((rows, D), bf16)),
            (place, attended, resid, vec, *w_out_all),
            flops=2 * rows * D * D,
            scratch=[pltpu.VMEM((rows, D), f32)],
        )
        piece = shard // PIECES
        normed_mlp, *late_pieces = together((normed_mlp, *pieces))
        if 4 * tokens * D * 2 < VMEM_LIMIT:
            normed_t, query_t = call(
                collect_kernel,
                "collect",
                (
                    shape((D, tokens), bf16),
                    shape((D, ctx_count * query_rows), bf16),
                ),
                (place, vec, *late_pieces),
                scratch=[pltpu.VMEM((ctx_count, rows, D), bf16)],
            )
        else:
            normed = (jnp.concatenate(late_pieces).astype(f32) * vec[0:1]).astype(bf16)
            normed_query = lax.dynamic_index_in_dim(
                normed.reshape(ctx_count, splits, query_rows, D), place[2], 1, keepdims=False
            )
            normed_t, query_t = normed.reshape(tokens, D).T, normed_query.reshape(-1, D).T
        normed_all = over_fsdp(normed_mlp)
        far_normed, normed_t, query_t = together((normed_all[2], normed_t, query_t))
        normed_all = (normed_all[0], normed_all[1], far_normed, to_core(far_normed))
        norm_own, norm_far, norm_give, active, grad_hidden, bias_up_sum = call(
            mlp_kernel,
            "mlp",
            (
                shape((rows, D), f32),
                shape((rows, D), f32),
                shape((2, rows, D), bf16),
                shape((2, 2 * rows, hidden), bf16),
                shape((2, 2 * rows, hidden), bf16),
                shape((1, hidden), f32),
            ),
            (place, *normed_all, *grads_mlp, up_sent[0], *up_got, w_down, bias_hidden),
            flops=24 * rows * D * hidden,
            exps=4 * rows * hidden,
            scratch=[pltpu.VMEM((D, hidden), bf16)],
        )
        norm_got = to_core(norm_give)
        norm_far_got = to_chip_row((norm_far + norm_got[1]).astype(bf16))
        norm_sent, active, grad_hidden = together((norm_got, active, grad_hidden))
        branch_own, branch_far, branch_give, *both_sums = call(
            mlp_back_kernel,
            "mlp_back",
            (
                shape((rows, D), f32),
                shape((rows, D), f32),
                shape((2, rows, D), bf16),
                *(shape((2, hidden // PIECES + 4 * piece, D), bf16) for _ in range(4)),
            ),
            (place, *normed_all, *grads_mlp, active, grad_hidden, w_down),
            flops=LONG,
            scratch=[pltpu.VMEM((hidden, D), f32), pltpu.VMEM((D, hidden), f32)],
        )
        norm_far_got, branch_own, branch_far, branch_give, *both_sums = together(
            (norm_far_got, branch_own, branch_far, branch_give, *both_sums)
        )
        grad_middle, grad_branch, grad_attended, row_sums = call(
            branch_back_kernel,
            "branch_back",
            (
                shape((rows, D), f32),
                shape((rows, D), bf16),
                shape((ctx_count, GROUP_COLS, query_rows), bf16),
                shape((8, D), f32),
            ),
            (place, norm_own, norm_got, norm_far_got, middle, top, vec, *w_out_all),
            flops=4 * rows * D * D,
        )
        grads = group_all_to_all(grad_attended)
        out_near, out_give = call(
            out_back_kernel,
            "out_back",
            (shape((2, PIECES, piece + EXTRA, D), bf16), shape((2, PIECES, piece + EXTRA, D), bf16)),
            (place, attended, grad_branch, row_sums, bias_up_sum),
            flops=2 * rows * D * D,
            scratch=[pltpu.VMEM((D + 8, D), f32)],
        )
        grads, out_near = together((grads, out_near))
        out_sum = out_near + to_core(out_give)
        grads, out_sum = together((grads, out_sum))
        out_got = to_chip_row(out_sum[1])
        both_got = to_square(both_sums[1:])
        dq, dkv, head_sums = call(
            attend_back_kernel,
            "attend_back",
            (
                shape((ctx_count, width, GROUP_COLS), bf16),
                shape((ctx_count, rows, 2 * GROUP_COLS), bf16),
                shape((8, GROUP_COLS), f32),
            ),
            (place, queries_t, keys, values, widened(grads), outs, logs),
            flops=10 * HD * pairs,
            exps=pairs,
            scratch=[
                pltpu.VMEM((rows, GROUP_COLS), f32),
                pltpu.VMEM((rows, GROUP_COLS), f32),
                pltpu.VMEM((ctx_count, width, GROUP_COLS), f32),
                pltpu.VMEM((ctx_count, 1, GROUP_HEADS * width), f32),
            ],
        )
        dq = dq[:, :query_rows]
        dq, dkv, out_got = together((dq, dkv, out_got))

        head_shapes = tuple(
            shape((2, 2, shard // 2 + EXTRA, 3 * GROUP_COLS), bf16) for _ in range(2)
        )
        if 4 * tokens * D * 2 < VMEM_LIMIT:
            head_near, head_give = call(
                heads_back_kernel,
                "heads_back",
                head_shapes,
                (place, normed_t, query_t, dq, dkv, head_sums),
                flops=work,
                scratch=[pltpu.VMEM((D, GROUP_COLS), f32), pltpu.VMEM((D, 2 * GROUP_COLS), f32)],
            )
        else:
            flat_q, flat_kv = dq.reshape(-1, GROUP_COLS), dkv.reshape(tokens, 2 * GROUP_COLS)
            head_near, head_give = call(
                arrange_heads,
                "arrange_heads",
                head_shapes,
                (place, dot(query_t, flat_q), dot(normed_t, flat_kv), head_sums),
            )
        head_near, head_give, out_got, *both_got = together(
            (head_near, head_give, out_got, *both_got)
        )
        wide = hidden // PIECES
        (both_sum,) = call(
            sum_kernel,
            "sum",
            (shape((2, wide + fsdp_count * piece, D), bf16),),
            (place, both_sums[0], *both_got),
        )
        out_sums = [
            out_sum[0, 2 * near : 2 * near + 2] + out_got[2 * near : 2 * near + 2] for near in range(4)
        ]
        head_sum = head_near + to_core(head_give)
        dq, head_near, head_give, both_sum, *out_sums = together(
            (dq, head_sum[0], head_sum[1], both_sum, *out_sums)
        )
        head_got = to_chip_row(head_give)
        both_got = to_ctx(both_sum, 4)
        out_got = to_square(out_sums[1:])

        row_shapes = (shape((half, rows, D), bf16), shape((half, rows, D), bf16))
        if 4 * tokens * D * 2 < VMEM_LIMIT:
            keep_rows, give_rows = call(
                rows_back_kernel,
                "rows_back",
                row_shapes,
                (place, dq, dkv, *w_heads),
                flops=work,
                scratch=head_weights,
            )
        else:
            weights = by_row(w_heads)
            flat_q, flat_kv = dq.reshape(-1, GROUP_COLS), dkv.reshape(tokens, 2 * GROUP_COLS)
            grad_rows = dot_nt(flat_kv, weights[:, GROUP_COLS:]).reshape(
                ctx_count, splits, query_rows, D
            )
            grad_query = dot_nt(flat_q, weights[:, :GROUP_COLS]).reshape(ctx_count, 1, query_rows, D)
            chosen = (jnp.arange(splits) == place[2])[None, :, None, None]
            grad_rows = (grad_rows + jnp.where(chosen, grad_query, 0.0)).astype(bf16)
            grad_rows = grad_rows.reshape(ctx_count, rows, D)
            keep_rows, give_rows = grad_rows[:half], grad_rows[half:]
        keep_rows, give_rows, head_got, both_got, *out_got = together(
            (keep_rows, give_rows, head_got, both_got, *out_got)
        )

        def both_sides(own, other):
            return over_rest(jnp.stack([own[0] + other[1], own[1] + other[0]]))

        rows_got = to_core(give_rows)
        head_sum = head_near + head_got
        out_sum = sum(out_got, start=out_sums[0])
        rows_got, head_sum, out_sum, both_got = together((rows_got, head_sum, out_sum, both_got))
        head_got, out_got = to_ctx(head_sum, 4), to_ctx(out_sum, 4)
        up_sum = both_sides(both_sum[:, wide:], both_got[:, wide:])
        ups = [up_sum[:, distance * piece : (distance + 1) * piece] for distance in range(fsdp_count)]
        ups = [ups[0]] + [to_fsdp(ups[distance], distance) for distance in (1, 2, 3)]
        keep_rows, both_got, branch_give, *ups = together((keep_rows, both_got, branch_give, *ups))
        if steps == 2:
            near_rows, far_rows = (keep_rows[at::2] + rows_got[at::2] for at in range(2))
        else:
            both = keep_rows + rows_got
            for bit in reversed(range(2, steps)):
                both = both[: 1 << bit] + to_ctx(both[1 << bit :], 1 << bit)
            near_rows, far_rows = both[0::2], both[1::2]
        far_got = to_ctx(far_rows, 1)
        last_got = to_ctx(near_rows[1] + far_got[1], 2)
        downs = both_sides(both_sum[:, :wide], both_got[:, :wide])
        downs = gather_square(downs, DOWN_FIRST)
        branch_got = to_core(branch_give)
        branch_far_got = to_chip_row((branch_far + branch_got[1]).astype(bf16))
        head_got, out_got = together((head_got, out_got))
        branch_mlp = branch_own + branch_got[0] + branch_far_got + vec[3:4]
        stream_out = (middle + centered(branch_mlp)).astype(bf16)[:, : D - 1]
        stream_out = swap_sequences(stream_out)
        outs = both_sides(out_sum, out_got)
        sums = outs[0, piece:].astype(f32)
        ups = jnp.concatenate([*ups, outs[:, :piece]], axis=1)
        ups = gather_square(ups, UP_FIRST)
        heads = both_sides(head_sum, head_got)
        heads = gather_square(heads, HEADS_FIRST)
        (grad_stream,) = call(
            stream_back_kernel,
            "stream_back",
            (shape((rows, D - 1), bf16),),
            (place, near_rows, far_got, last_got, resid, grad_middle, vec),
        )
        grad_stream = swap_sequences(grad_stream)
        (grad_w_down,) = call(down_out_kernel, "down_out", (shape((hidden, D), f32),), (place, *downs))
        grad_w_down, *heads = together((grad_w_down, *heads))
        grad_w_qkv, grad_gain_attn, grad_bias_qv = call(
            heads_out_kernel,
            "heads_out",
            (
                shape((shard, 3 * D), f32),
                shape((shard, 1), f32),
                shape((1, 2 * shard), f32),
            ),
            (place, *heads, w_qkv),
            scratch=[pltpu.VMEM((4, 2, shard // 2 + EXTRA, 3 * GROUP_COLS), bf16)],
        )
        grad_w_up, grad_w_out = call(
            up_out_kernel,
            "up_out",
            (shape((shard, fsdp_count * hidden), f32), shape((shard, D), f32)),
            (place, *ups),
        )

        return (
            stream_out,
            grad_stream.astype(f32),
            grad_gain_attn.reshape(-1) / gain_attn.astype(f32),
            grad_w_qkv,
            grad_bias_qv.reshape(-1),
            grad_w_out,
            sums[0, :shard],
            sums[0, shard : 2 * shard],
            grad_w_up,
            sums[1],
            grad_w_down,
            sums[0, 2 * shard : 3 * shard],
        )

    rows_spec, matrix_spec, vector_spec = P(AXES, None), P("fsdp", None), P("fsdp")
    return jax.shard_map(
        local,
        mesh=mesh,
        in_specs=(
            rows_spec,
            vector_spec,
            matrix_spec,
            vector_spec,
            matrix_spec,
            vector_spec,
            vector_spec,
            matrix_spec,
            vector_spec,
            matrix_spec,
            vector_spec,
            rows_spec,
        ),
        out_specs=(
            rows_spec,
            rows_spec,
            vector_spec,
            matrix_spec,
            vector_spec,
            matrix_spec,
            vector_spec,
            vector_spec,
            matrix_spec,
            vector_spec,
            matrix_spec,
            vector_spec,
        ),
        check_vma=False,
    )
```

```python
import jax
import jax.numpy as jnp
from jax import lax
from jax.experimental import pallas as pl
from jax.experimental.pallas import tpu as pltpu
from jax.sharding import PartitionSpec as P

D = 768
H = 12
HD = 64
HEAD_GROUPS = 4
GROUP_HEADS = H // HEAD_GROUPS
GROUP_COLS = GROUP_HEADS * HD
HEAD_SCALE = HD ** (-0.5)
NORM_EPS = 1e-05
NEG_BIG = -1e30
GELU_A = 0.7978845608028654
GELU_B = 0.044715
LANES = 128
PIECES = 8
EXTRA = 8
LONG = 10**11
AXES = ("fsdp", "ctx")
VMEM_LIMIT = 120 << 19
UNROLL_BLOCKS = 8

f32 = jnp.float32
bf16 = jnp.bfloat16


def dot(left, right):
    return lax.dot_general(left, right, (((1,), (0,)), ((), ())), preferred_element_type=f32)


def dot_tn(left, right):
    return lax.dot_general(left, right, (((0,), (0,)), ((), ())), preferred_element_type=f32)


def dot_nt(left, right):
    return lax.dot_general(left, right, (((1,), (1,)), ((), ())), preferred_element_type=f32)


def centered(branch):
    return branch - jnp.mean(branch, axis=1, keepdims=True)


def inverse_rms(stream):
    return lax.rsqrt(jnp.mean(stream * stream, axis=1, keepdims=True) + NORM_EPS)


def norm_back(grad, unit, inverse):
    return inverse * (grad - unit * jnp.mean(grad * unit, axis=1, keepdims=True))


def slab_at(relative):
    return ((relative & 1) << 1) | (relative >> 1)


def loop(start, stop, body, carried):
    if isinstance(start, int) and isinstance(stop, int) and stop - start <= UNROLL_BLOCKS:
        for at in range(start, stop):
            carried = body(at, carried)
        return carried
    return lax.fori_loop(start, stop, body, carried)


def call(body, name, outs, args, flops=0, exps=0, scratch=(), **grid):
    moved = sum(x.size * x.dtype.itemsize for x in tuple(args) + tuple(outs))
    specs = dict(
        in_specs=[pl.BlockSpec(memory_space=pltpu.SMEM)]
        + [pl.BlockSpec(memory_space=pltpu.VMEM)] * (len(args) - 1),
        out_specs=tuple(pl.BlockSpec(memory_space=pltpu.VMEM) for _ in outs),
    )
    specs.update(grid)
    return pl.pallas_call(
        body,
        out_shape=tuple(outs),
        scratch_shapes=list(scratch),
        compiler_params=pltpu.CompilerParams(vmem_limit_bytes=VMEM_LIMIT),
        cost_estimate=pl.CostEstimate(flops=flops, bytes_accessed=moved, transcendentals=exps),
        name=name,
        **specs,
    )(*args)


def shape(dims, kind):
    return jax.ShapeDtypeStruct(tuple(dims), kind)


def norm_kernel(place, x_ref, resid_ref, unit_ref):
    x = x_ref[...].astype(f32)
    resid_ref[:, : D - 1] = x
    resid_ref[:, D - 1 :] = -jnp.sum(x, axis=1, keepdims=True)
    resid = resid_ref[...]
    unit_ref[0] = (resid * inverse_rms(resid)).astype(bf16)


def cut_kernel(place, qkv_ref, up_ref, heads_ref, *slabs):
    group = place[0] % HEAD_GROUPS
    for at in range(HEAD_GROUPS):

        @pl.when(group == at)
        def _():
            for kind in range(3):
                start = kind * D + at * GROUP_COLS
                heads_ref[:, kind * GROUP_COLS : (kind + 1) * GROUP_COLS] = qkv_ref[
                    :, start : start + GROUP_COLS
                ]

    hidden = slabs[0].shape[1]
    for distance, slab in enumerate(slabs):
        at = pl.multiple_of((distance ^ place[1]) * hidden, LANES)
        slab[...] = up_ref[:, pl.ds(at, hidden)]


def load_heads(place, slab_refs, wq, wkv):
    shard = slab_refs[0].shape[0]
    for distance, slab_ref in enumerate(slab_refs):
        at = pl.ds(pl.multiple_of((distance ^ place[1]) * shard, shard), shard)
        wq[at, :] = slab_ref[:, :GROUP_COLS]
        wkv[at, :] = slab_ref[:, GROUP_COLS:]


def project(place, normed_ref, slots, bias_ref, k_ref, v_ref, q_ref, qt_ref, wq, wkv):
    rows, query_rows = normed_ref.shape[1], qt_ref.shape[2]
    own = pl.ds(pl.multiple_of(place[2] * query_rows, query_rows), query_rows)
    for start in range(0, slots, 2):
        pair = range(start, min(start + 2, slots))
        normed = jnp.concatenate([normed_ref[slot] for slot in pair], axis=0)
        both = dot(normed, wkv[...])
        keys, values = both[:, :GROUP_COLS], both[:, GROUP_COLS:] + bias_ref[1:2, :]
        mine = jnp.concatenate([normed_ref[slot, own, :] for slot in pair], axis=0)
        queries = (dot(mine, wq[...]) + bias_ref[0:1, :]) * HEAD_SCALE
        for at, slot in enumerate(pair):
            here = slice(at * rows, (at + 1) * rows)
            k_ref[slot] = keys[here].astype(bf16)
            v_ref[slot] = values[here].astype(bf16)
            query = queries[at * query_rows : (at + 1) * query_rows]
            q_ref[slot], qt_ref[slot] = query.astype(bf16), query.T.astype(bf16)


def project_kernel(place, *refs):
    slabs, (gain_ref, bias_ref) = refs[:4], refs[4:6]
    pieces = refs[6:-7]
    k_ref, v_ref, q_ref, qt_ref, wq, wkv, normed_ref = refs[-7:]
    load_heads(place, slabs, wq, wkv)
    gain = gain_ref[0:1, :]
    slot = 0
    for ref in pieces:
        for at in range(ref.shape[0]):
            normed_ref[slot] = (ref[at].astype(f32) * gain).astype(bf16)
            slot += 1
    project(place, normed_ref, slot, bias_ref, k_ref, v_ref, q_ref, qt_ref, wq, wkv)


def project_block_kernel(place, *refs):
    slabs, bias_ref, normed_ref = refs[:4], refs[4], refs[5]
    k_ref, v_ref, q_ref, qt_ref, wq, wkv = refs[6:]

    @pl.when(pl.program_id(0) == 0)
    def _():
        load_heads(place, slabs, wq, wkv)

    slots = normed_ref.shape[0]
    project(place, normed_ref, slots, bias_ref, k_ref, v_ref, q_ref, qt_ref, wq, wkv)


def collect_kernel(place, gain_ref, *refs):
    pieces, (normed_t_ref, query_t_ref, normed_ref) = refs[:-3], refs[-3:]
    blocks, rows, _ = normed_ref.shape
    query_rows = query_t_ref.shape[1] // blocks
    own = pl.ds(pl.multiple_of(place[2] * query_rows, query_rows), query_rows)
    gain, slot = gain_ref[0:1, :], 0
    for ref in pieces:
        for at in range(ref.shape[0]):
            normed_ref[slot] = (ref[at].astype(f32) * gain).astype(bf16)
            normed_t_ref[:, slot * rows : (slot + 1) * rows] = normed_ref[slot].T
            mine = normed_ref[slot, own, :].T
            query_t_ref[:, slot * query_rows : (slot + 1) * query_rows] = mine
            slot += 1


def by_head(value):
    head = lax.broadcasted_iota(jnp.int32, value.shape, 0) // HD
    zero = jnp.zeros_like(value)
    return jnp.concatenate([jnp.where(head == at, value, zero) for at in range(GROUP_HEADS)], axis=1)


def by_head_rows(value):
    head = lax.broadcasted_iota(jnp.int32, value.shape, 1) // HD
    zero = jnp.zeros_like(value)
    return jnp.concatenate([jnp.where(head == at, value, zero) for at in range(GROUP_HEADS)], axis=0)


def lane_halves(value, join):
    return join(value[:, :LANES], value[:, LANES:])


def attend_kernel(place, q_ref, k_ref, v_ref, out_ref, log_ref, score_ref):
    blocks, width, _ = q_ref.shape
    member = place[0]

    def one_query_block(block, _):
        queries = by_head_rows(q_ref[block ^ member])

        def one_score(key_block, top):
            scores = dot_nt(queries, k_ref[key_block ^ member])
            score_ref[key_block] = scores
            return jnp.maximum(top, lane_halves(scores, jnp.maximum))

        top = loop(0, block + 1, one_score, jnp.full((GROUP_HEADS * width, LANES), NEG_BIG, f32))
        top = jnp.max(top, axis=1, keepdims=True)

        def one_value(key_block, carried):
            total, acc = carried
            weights = jnp.exp(score_ref[key_block] - top)
            total = total + lane_halves(weights, jnp.add)
            return total, acc + dot(weights.astype(bf16), v_ref[key_block ^ member])

        start_state = (
            jnp.zeros((GROUP_HEADS * width, LANES), f32),
            jnp.zeros((GROUP_HEADS * width, GROUP_COLS), f32),
        )
        total, acc = loop(0, block + 1, one_value, start_state)
        total = jnp.sum(total, axis=1, keepdims=True)
        acc = acc / total
        log_sums = jnp.broadcast_to(top + jnp.log(total), (GROUP_HEADS * width, LANES))
        for head in range(GROUP_HEADS):
            here = slice(head * width, (head + 1) * width)
            cols = slice(head * HD, (head + 1) * HD)
            out_ref[block, cols, :] = acc[here, :].T[cols].astype(bf16)
            log_ref[block, :, here] = log_sums[here].T[:1]
        return 0

    loop(0, blocks, one_query_block, 0)


def attend_back_kernel(
    place, qt_ref, k_ref, v_ref, gt_ref, out_ref, log_ref, dq_ref, dkv_ref, sum_ref, dk_acc, dv_acc, dq_acc, delta_ref
):
    blocks, _, width = qt_ref.shape
    member = place[0]

    def prepare(block, _):
        products = gt_ref[block].astype(f32) * out_ref[block].astype(f32)
        for head in range(GROUP_HEADS):
            delta_ref[block, :, head * width : (head + 1) * width] = jnp.sum(
                products[head * HD : (head + 1) * HD], axis=0, keepdims=True
            )
        return 0

    lax.fori_loop(0, blocks, prepare, 0)
    dq_acc[...] = jnp.zeros_like(dq_acc)
    sum_ref[...] = jnp.zeros_like(sum_ref)

    head_at = lax.broadcasted_iota(jnp.int32, (width, GROUP_COLS), 1) // HD

    def one_key_block(key_block, _):
        slot = key_block ^ member
        dk_acc[...] = jnp.zeros_like(dk_acc)
        dv_acc[...] = jnp.zeros_like(dv_acc)

        def one_query_block(block, _):
            queries, grads = by_head(qt_ref[block ^ member]), by_head(gt_ref[block])
            prob = jnp.exp(dot(k_ref[slot], queries) - log_ref[block])
            grad_prob = dot(v_ref[slot], grads)
            grad_scores = (prob * (grad_prob - delta_ref[block])).astype(bf16)
            dv_acc[...] += dot_nt(prob.astype(bf16), grads)
            dk_acc[...] += dot_nt(grad_scores, queries)
            every = dot_tn(grad_scores, k_ref[slot])
            grad = jnp.zeros((width, GROUP_COLS), f32)
            for head in range(GROUP_HEADS):
                grad = jnp.where(head_at == head, every[head * width : (head + 1) * width], grad)
            dq_acc[block] += grad
            return 0

        loop(key_block, blocks, one_query_block, 0)
        dkv_ref[slot] = jnp.concatenate([dk_acc[...], dv_acc[...]], axis=1).astype(bf16)
        sum_ref[1:2, :] += jnp.sum(dv_acc[...], axis=0, keepdims=True)
        return 0

    loop(0, blocks, one_key_block, 0)

    def write(block, _):
        grads = dq_acc[block] * HEAD_SCALE
        dq_ref[block ^ member] = grads.astype(bf16)
        sum_ref[0:1, :] += jnp.sum(grads, axis=0, keepdims=True)
        return 0

    lax.fori_loop(0, blocks, write, 0)


def middle_kernel(
    place, att_ref, resid_ref, vec_ref, slab0, slab1, slab2, slab3, middle_ref, normed_ref, branch
):
    query_rows = att_ref.shape[2]
    for split in range(att_ref.shape[0] // HEAD_GROUPS):
        total = None
        for distance, slab_ref in enumerate((slab0, slab1, slab2, slab3)):
            part = dot_tn(att_ref[split * HEAD_GROUPS + (distance ^ place[1])], slab_ref[...])
            total = part if total is None else total + part
        branch[split * query_rows : (split + 1) * query_rows, :] = total
    middle = resid_ref[...] + centered(branch[...] + vec_ref[1:2, :])
    middle_ref[...] = middle
    normed_ref[...] = (middle * inverse_rms(middle) * vec_ref[2:3, :]).astype(bf16)


def mlp_kernel(place, *refs):
    normed, grads, slabs, (down_ref, bias_ref) = refs[:4], refs[4:8], refs[8:12], refs[12:14]
    norm_own, norm_far, norm_give, active_ref, hidden_ref, bias_grad, weight = refs[14:]
    rows, shard = normed[0].shape[0], slabs[0].shape[0]
    for distance, slab in enumerate(slabs):
        at = pl.multiple_of((distance ^ place[1]) * shard, shard)
        weight[pl.ds(at, shard), :] = slab[...]
    for tile in range(2):
        blocks = (tile, 2 + tile)
        tokens = jnp.concatenate([normed[at][...] for at in blocks], axis=0)
        grad = jnp.concatenate([grads[at][...] for at in blocks], axis=0)
        hidden = dot(tokens, weight[...]) + bias_ref[...]
        square = hidden * hidden
        bent = jnp.tanh(GELU_A * hidden * (1.0 + GELU_B * square))
        half = 0.5 * (1.0 + bent)
        active_ref[tile] = (hidden * half).astype(bf16)
        slope = half + 0.5 * hidden * (1.0 - bent * bent) * (GELU_A * (1.0 + 3.0 * GELU_B * square))
        grad_hidden = (dot_nt(grad, down_ref[...]) * slope).astype(bf16)
        hidden_ref[tile] = grad_hidden
        norm = dot_nt(grad_hidden, weight[...])
        bias = jnp.sum(grad_hidden.astype(f32), axis=0, keepdims=True)
        if tile:
            norm_give[0], norm_give[1] = norm[:rows].astype(bf16), norm[rows:].astype(bf16)
            bias_grad[...] += bias
        else:
            norm_own[...], norm_far[...] = norm[:rows], norm[rows:]
            bias_grad[...] = bias


def mlp_back_kernel(place, *refs):
    normed, grads, (active_ref, hidden_ref, down_ref) = refs[:4], refs[4:8], refs[8:11]
    branch_own, branch_far, branch_give = refs[11:14]
    pieces, (down_total, up_total) = refs[14:18], refs[18:]
    rows = normed[0].shape[0]
    wide = down_ref.shape[0] // PIECES
    piece = (pieces[0].shape[1] - wide) // 4
    shard = piece * PIECES
    mine, low = place[1], place[3]
    for tile in range(2):
        blocks = (tile, 2 + tile)
        tokens = jnp.concatenate([normed[at][...] for at in blocks], axis=0)
        grad = jnp.concatenate([grads[at][...] for at in blocks], axis=0)
        down, up = dot_tn(active_ref[tile], grad), dot_tn(tokens, hidden_ref[tile])
        branch = dot(active_ref[tile], down_ref[...])
        if tile:
            down_total[...] += down
            up_total[...] += up
            branch_give[0], branch_give[1] = branch[:rows].astype(bf16), branch[rows:].astype(bf16)
        else:
            down_total[...], up_total[...] = down, up
            branch_own[...], branch_far[...] = branch[:rows], branch[rows:]
    for near, target in enumerate(pieces):
        for side in range(2):
            at = (side << 2 | near) ^ low
            target[side, :wide] = down_total[pl.ds(pl.multiple_of(at * wide, wide), wide), :].astype(bf16)
            for distance in range(4):
                here = pl.multiple_of((distance ^ mine) * shard + at * piece, piece)
                start = wide + distance * piece
                target[side, start : start + piece] = up_total[pl.ds(here, piece), :].astype(bf16)


def branch_back_kernel(
    place,
    own_ref,
    core_ref,
    far_ref,
    middle_ref,
    top_ref,
    vec_ref,
    slab0,
    slab1,
    slab2,
    slab3,
    grad_middle_ref,
    grad_branch_ref,
    ga_ref,
    sum_ref,
):
    query_rows = ga_ref.shape[2]
    rows = top_ref.shape[0]
    grad = own_ref[...] + core_ref[0].astype(f32) + far_ref[...].astype(f32)
    middle = middle_ref[...]
    inverse = inverse_rms(middle)
    unit = middle * inverse
    sum_ref[0:1, :] = jnp.sum(grad * unit, axis=0, keepdims=True)
    grad_top = jnp.concatenate([top_ref[...].astype(f32), jnp.zeros((rows, 1), f32)], axis=1)
    grad_middle = grad_top + norm_back(grad * vec_ref[2:3, :], unit, inverse)
    grad_middle_ref[...] = grad_middle
    grad_branch = centered(grad_middle).astype(bf16)
    grad_branch_ref[...] = grad_branch
    for distance, slab_ref in enumerate((slab0, slab1, slab2, slab3)):
        product = dot_nt(slab_ref[...], grad_branch).astype(bf16)
        for split in range(ga_ref.shape[0] // HEAD_GROUPS):
            at = split * HEAD_GROUPS + (distance ^ place[1])
            ga_ref[at] = product[:, split * query_rows : (split + 1) * query_rows]
    sum_ref[1:2, :] = jnp.sum(grad_branch.astype(f32), axis=0, keepdims=True)
    sum_ref[2:3, :] = jnp.sum(centered(grad_top).astype(bf16).astype(f32), axis=0, keepdims=True)


def out_back_kernel(place, att_ref, grad_ref, sum_ref, bias_up_ref, near_ref, far_ref, grad_w):
    query_rows = att_ref.shape[2]
    groups, piece = HEAD_GROUPS, near_ref.shape[2] - EXTRA
    shard = D // groups
    mine, low = place[1], place[3]
    empty = jnp.zeros((1, D - 3 * shard), f32)
    for group in range(groups):
        weight = None
        for split in range(att_ref.shape[0] // groups):
            product = dot(
                att_ref[split * groups + group], grad_ref[split * query_rows : (split + 1) * query_rows, :]
            )
            weight = product if weight is None else weight + product
        lanes = slice(group * shard, (group + 1) * shard)
        grad_w[group * shard : (group + 1) * shard, :] = weight
        row = [sum_ref[at : at + 1, lanes] for at in (1, 0, 2)]
        grad_w[D + group : D + group + 1, :] = jnp.concatenate(row + [empty], axis=1)
    for distance in range(4):
        far, core = distance >> 1, distance & 1
        row = grad_w[pl.ds(D + (distance ^ mine), 1), :]
        up_row = jnp.zeros_like(row) if distance else bias_up_ref[...]
        extra = jnp.concatenate([row, up_row, jnp.zeros((EXTRA - 2, D), f32)], axis=0)

        def one(index, _, distance=distance, extra=extra):
            at = (distance ^ mine) * shard + (((index & 1) << 2 | index >> 1) ^ low) * piece
            part = grad_w[pl.ds(pl.multiple_of(at, piece), piece), :]
            target = (near_ref, far_ref)[distance & 1]
            target[distance >> 1, index] = jnp.concatenate([part, extra], axis=0).astype(bf16)
            return 0

        lax.fori_loop(0, PIECES, one, 0)


def sum_kernel(place, part0, part1, part2, part3, out_ref):
    out_ref[...] = sum(part[...].astype(f32) for part in (part0, part1, part2, part3)).astype(bf16)


def heads_back_kernel(place, normed_t_ref, query_t_ref, dq_ref, dkv_ref, sum_ref, near_ref, far_ref, aq, akv):
    blocks, query_rows, _ = dq_ref.shape
    rows = dkv_ref.shape[1]
    chunk = min(blocks, 4)
    for start in range(0, blocks, chunk):
        dkv = jnp.concatenate([dkv_ref[start + at] for at in range(chunk)], axis=0)
        dq = jnp.concatenate([dq_ref[start + at] for at in range(chunk)], axis=0)
        kv = dot(normed_t_ref[:, start * rows : (start + chunk) * rows], dkv)
        q = dot(query_t_ref[:, start * query_rows : (start + chunk) * query_rows], dq)
        if start:
            akv[...] += kv
            aq[...] += q
        else:
            akv[...], aq[...] = kv, q
    arrange_heads(place, aq, akv, sum_ref, near_ref, far_ref)


def arrange_heads(place, q_ref, kv_ref, sum_ref, near_ref, far_ref):
    mine, piece = place[1], near_ref.shape[2] - EXTRA
    shard = 2 * piece
    group = place[0] % HEAD_GROUPS
    for row in range(D // shard):
        relative = row ^ mine
        first = jnp.where(group // 2 == row, sum_ref[0:1, :], 0.0)
        second = jnp.where(2 + group // 2 == row, sum_ref[1:2, :], 0.0)
        extra = jnp.concatenate([first, second, jnp.zeros_like(first)], axis=1)
        extra = jnp.concatenate([extra, jnp.zeros((EXTRA - 1, extra.shape[1]), f32)], axis=0)
        for part in range(2):
            at_row = slice(row * shard + part * piece, row * shard + (part + 1) * piece)
            block = jnp.concatenate([q_ref[at_row, :], kv_ref[at_row, :]], axis=1)
            both = jnp.concatenate([block, extra], axis=0).astype(bf16)
            for core, target in enumerate((near_ref, far_ref)):

                @pl.when((relative & 1) == core)
                def _():
                    target[relative >> 1, part ^ ((place[3] >> 2) & 1)] = both


def rows_back_kernel(place, dq_ref, dkv_ref, slab0, slab1, slab2, slab3, keep_ref, give_ref, wq, wkv):
    load_heads(place, (slab0, slab1, slab2, slab3), wq, wkv)
    query_rows, half = dq_ref.shape[1], keep_ref.shape[0]
    own = pl.ds(pl.multiple_of(place[2] * query_rows, query_rows), query_rows)
    for core, ref in ((1, give_ref), (0, keep_ref)):

        def one(at, _, core=core, ref=ref):
            slot = at + core * half
            ref[at] = dot_nt(dkv_ref[slot], wkv[...]).astype(bf16)
            low = ref[at, own, :].astype(f32)
            ref[at, own, :] = (low + dot_nt(dq_ref[slot], wq[...])).astype(bf16)
            return 0

        loop(0, half, one, 0)


def by_near(own, got, pair, first):
    return ((0, own), (first, got), (3 - first, pair.at[0]), (3, pair.at[1]))


UP_FIRST, DOWN_FIRST, HEADS_FIRST = 1, 2, 2


def stream_back_kernel(place, near_ref, far_ref, last_ref, resid_ref, grad_middle_ref, vec_ref, out_ref):
    grad = near_ref[0].astype(f32) + far_ref[0].astype(f32) + last_ref[...].astype(f32)
    resid = resid_ref[...]
    inverse = inverse_rms(resid)
    unit = resid * inverse
    total = grad_middle_ref[...] + norm_back(grad * vec_ref[0:1, :], unit, inverse)
    out_ref[...] = (total - total[:, D - 1 :]).astype(bf16)[:, : D - 1]


def down_out_kernel(place, own, got, pair, out_ref):
    wide = own.shape[1]
    for near, part in by_near(own, got, pair, DOWN_FIRST):
        for side in range(2):
            at = pl.multiple_of(((side << 2 | near) ^ place[3]) * wide, wide)
            out_ref[pl.ds(at, wide), :] = part[side].astype(f32)


def up_out_kernel(place, own, got, pair, up_ref, out_ref):
    rows = out_ref.shape[0] // PIECES
    for near, part in by_near(own, got, pair, UP_FIRST):
        for side in range(2):
            at = pl.multiple_of(((side << 2 | near) ^ place[3]) * rows, rows)
            for slab in range(4):
                col = pl.multiple_of((slab ^ place[1]) * D, LANES)
                value = part[side, slab * rows : (slab + 1) * rows]
                up_ref[pl.ds(at, rows), pl.ds(col, D)] = value.astype(f32)
            out_ref[pl.ds(at, rows), :] = part[side, 4 * rows :].astype(f32)


def heads_out_kernel(place, own, got, pair, weight_ref, out_ref, gain_ref, bias_ref, pieces):
    piece = own.shape[1] - EXTRA
    mine, low = place[1], place[3]
    for near, part in by_near(own, got, pair, HEADS_FIRST):
        pieces[near] = part[...]
    for part in range(2):
        for group in range(HEAD_GROUPS):
            value = pieces[(group ^ low) & 3, part ^ ((low >> 2) & 1)].astype(f32)
            for kind in range(3):
                start = kind * D + group * GROUP_COLS
                out_ref[part * piece : (part + 1) * piece, start : start + GROUP_COLS] = value[
                    :piece, kind * GROUP_COLS : (kind + 1) * GROUP_COLS
                ]
    gain_ref[...] = jnp.sum(out_ref[...] * weight_ref[...].astype(f32), axis=1, keepdims=True)
    sides = []
    for side in range(2):
        group = ((2 * mine) & 3) + side
        value = pieces[(group ^ low) & 3, 0].astype(f32)[piece : piece + 1]
        sides.append(jnp.where(mine < 2, value[:, :GROUP_COLS], value[:, GROUP_COLS : 2 * GROUP_COLS]))
    bias_ref[...] = jnp.concatenate(sides, axis=1)


def solution(mesh):
    fsdp_count, ctx_count = mesh.shape["fsdp"], mesh.shape["ctx"]
    half = ctx_count // 2
    steps = half.bit_length() - 1
    ctx_steps = steps + 1
    splits = ctx_count // HEAD_GROUPS
    shard = D // fsdp_count

    def send(value, target):
        pairs = []
        for source in range(fsdp_count * ctx_count):
            row, at = target(*divmod(source, ctx_count))
            pairs.append((source, row * ctx_count + at))
        return lax.ppermute(value, AXES, pairs)

    def to_core(value):
        return send(value, lambda row, at: (row ^ 1, at))

    def to_chip_row(value):
        return send(value, lambda row, at: (row ^ 2, at))

    def to_ctx(value, bit):
        return send(value, lambda row, at: (row, at ^ bit))

    def swap_sequences(value):
        return send(
            value, lambda row, at: (row, at) if (row & 1) == at // half else (row ^ 1, at ^ half)
        )

    groups = [
        [(row + core) * ctx_count + side * half + at for core in range(2) for at in range(half)]
        for row in range(0, fsdp_count, 2)
        for side in range(2)
    ]

    def group_all_to_all(value):
        return lax.all_to_all(value, AXES, 0, 0, axis_index_groups=groups, tiled=True)

    def to_fsdp(value, distance):
        return send(value, lambda row, at: (row ^ distance, at))

    def over_fsdp(value):
        far = to_chip_row(value)
        return value, to_core(value), far, to_core(far)

    def to_square(values):
        return tuple(to_ctx(value, near + 1) for near, value in enumerate(values))

    def over_rest(value):
        for step in range(3, ctx_steps):
            value = value + to_ctx(value, 1 << step)
        return value

    def gather_square(value, first):
        got = to_ctx(value, first)
        return value, got, to_ctx(jnp.stack([value, got]), 3 - first)

    together = lax.optimization_barrier

    def widened(value):
        width = value.shape[-1]
        return value if width >= LANES else jnp.pad(value, ((0, 0), (0, 0), (0, LANES - width)))

    def local(
        stream_in,
        gain_attn,
        w_qkv,
        bias_qv,
        w_out,
        bias_out,
        gain_mlp,
        w_up,
        bias_up,
        w_down,
        bias_down,
        grad_out,
    ):
        rows = stream_in.shape[0]
        query_rows = rows // splits
        width = max(query_rows, LANES)
        fsdp_at, ctx_at = lax.axis_index("fsdp"), lax.axis_index("ctx")
        core, inner = fsdp_at & 1, ctx_at % half
        member = core * half + inner
        head_group = inner % HEAD_GROUPS
        place = jnp.stack([member, fsdp_at, member // HEAD_GROUPS, ctx_at & 7]).astype(jnp.int32)

        hidden = w_down.shape[0]
        stream = swap_sequences(stream_in)
        w_part, *up_sent = call(
            cut_kernel,
            "cut",
            (
                shape((shard, 3 * GROUP_COLS), bf16),
                *(shape((shard, hidden), bf16) for _ in range(fsdp_count)),
            ),
            (place, w_qkv, w_up),
        )
        vectors = jnp.concatenate(
            [
                part.astype(f32).reshape(1, -1)
                for part in (gain_attn, bias_out, gain_mlp, bias_down, bias_qv, bias_up)
            ],
            axis=1,
        )
        far_heads, far_vectors = together((to_chip_row(w_part), to_chip_row(vectors)))
        w_heads = (w_part, to_core(w_part), far_heads, to_core(far_heads))
        vectors = (vectors, to_core(vectors), far_vectors, to_core(far_vectors))
        far_heads, w_out_sent, stream = together((far_heads, w_out, stream))

        resid, unit = call(
            norm_kernel,
            "norm",
            (shape((rows, D), f32), shape((1, rows, D), bf16)),
            (place, stream),
        )
        got = to_square((unit,) * 3)
        *got, out_far = together((*got, to_chip_row(w_out_sent)))
        pieces = [unit, *got]
        for bit in range(2, steps):
            pieces.append(to_ctx(jnp.concatenate(pieces), 1 << bit))
        pieces = pieces + [to_core(piece) for piece in pieces]

        def by_row(values):
            ordered = []
            for row in range(fsdp_count):
                first = jnp.where((fsdp_at ^ row) & 1 == 0, values[0], values[1])
                second = jnp.where((fsdp_at ^ row) & 1 == 0, values[2], values[3])
                ordered.append(jnp.where((fsdp_at ^ row) < 2, first, second))
            return jnp.concatenate(ordered)

        vectors = by_row(vectors)
        vec = vectors[:, :D].reshape(fsdp_count, 4, shard).transpose(1, 0, 2).reshape(4, D)
        bias_heads = vectors[:, D : D + 2 * shard].reshape(2, HEAD_GROUPS, GROUP_COLS)
        bias_heads = lax.dynamic_index_in_dim(bias_heads, head_group, 1, keepdims=False)
        bias_hidden = lax.dynamic_slice_in_dim(vectors[:, D + 2 * shard :], fsdp_at, 1)

        head_weights = [pltpu.VMEM((D, GROUP_COLS), bf16), pltpu.VMEM((D, 2 * GROUP_COLS), bf16)]
        tokens = ctx_count * rows
        projected = (
            shape((ctx_count, rows, GROUP_COLS), bf16),
            shape((ctx_count, rows, GROUP_COLS), bf16),
            shape((ctx_count, query_rows, GROUP_COLS), bf16),
            shape((ctx_count, GROUP_COLS, query_rows), bf16),
        )
        work = 5 * tokens * D * GROUP_COLS
        if 4 * tokens * D * 2 < VMEM_LIMIT:
            keys, values, queries, queries_t = call(
                project_kernel,
                "project",
                projected,
                (place, *w_heads, vec, bias_heads, *pieces),
                flops=work,
                scratch=head_weights + [pltpu.VMEM((ctx_count, rows, D), bf16)],
            )
        else:
            normed = (jnp.concatenate(pieces).astype(f32) * vec[0:1]).astype(bf16)
            block = lambda *dims: pl.BlockSpec((1,) + dims, lambda at: (at, 0, 0))
            whole = lambda *dims: pl.BlockSpec(dims, lambda at: (0,) * len(dims))
            keys, values, queries, queries_t = call(
                project_block_kernel,
                "project",
                projected,
                (place, *w_heads, bias_heads, normed),
                flops=work,
                scratch=head_weights,
                grid=(ctx_count,),
                in_specs=[pl.BlockSpec(memory_space=pltpu.SMEM)]
                + [whole(shard, 3 * GROUP_COLS)] * 4
                + [whole(2, GROUP_COLS), block(rows, D)],
                out_specs=(
                    block(rows, GROUP_COLS),
                    block(rows, GROUP_COLS),
                    block(query_rows, GROUP_COLS),
                    block(GROUP_COLS, query_rows),
                ),
            )
        queries_t = widened(queries_t)
        queries = jnp.pad(queries, ((0, 0), (0, width - query_rows), (0, 0)))
        pairs = GROUP_HEADS * query_rows * rows * ctx_count * (ctx_count + 1) // 2
        outs, logs = call(
            attend_kernel,
            "attend",
            (
                shape((ctx_count, GROUP_COLS, width), bf16),
                shape((ctx_count, 1, GROUP_HEADS * width), f32),
            ),
            (place, queries, keys, values),
            flops=4 * HD * pairs,
            exps=pairs,
            scratch=[pltpu.VMEM((ctx_count, GROUP_HEADS * width, rows), f32)],
        )
        outs, *up_got = together(
            (outs, *(to_fsdp(up_sent[distance], distance) for distance in (1, 2, 3)))
        )
        attended = group_all_to_all(outs[:, :, :query_rows])
        w_out_all = (w_out, to_core(w_out), out_far, to_core(out_far))
        top = swap_sequences(grad_out)
        grad_result = jnp.pad(top.astype(f32), ((0, 0), (0, 1)))
        grad_branch_mlp = centered(grad_result).astype(bf16)
        grads_mlp = over_fsdp(grad_branch_mlp)
        middle, normed_mlp = call(
            middle_kernel,
            "middle",
            (shape((rows, D), f32), shape((rows, D), bf16)),
            (place, attended, resid, vec, *w_out_all),
            flops=2 * rows * D * D,
            scratch=[pltpu.VMEM((rows, D), f32)],
        )
        piece = shard // PIECES
        normed_mlp, *late_pieces = together((normed_mlp, *pieces))
        if 4 * tokens * D * 2 < VMEM_LIMIT:
            normed_t, query_t = call(
                collect_kernel,
                "collect",
                (
                    shape((D, tokens), bf16),
                    shape((D, ctx_count * query_rows), bf16),
                ),
                (place, vec, *late_pieces),
                scratch=[pltpu.VMEM((ctx_count, rows, D), bf16)],
            )
        else:
            normed = (jnp.concatenate(late_pieces).astype(f32) * vec[0:1]).astype(bf16)
            normed_query = lax.dynamic_index_in_dim(
                normed.reshape(ctx_count, splits, query_rows, D), place[2], 1, keepdims=False
            )
            normed_t, query_t = normed.reshape(tokens, D).T, normed_query.reshape(-1, D).T
        normed_all = over_fsdp(normed_mlp)
        far_normed, normed_t, query_t = together((normed_all[2], normed_t, query_t))
        normed_all = (normed_all[0], normed_all[1], far_normed, to_core(far_normed))
        norm_own, norm_far, norm_give, active, grad_hidden, bias_up_sum = call(
            mlp_kernel,
            "mlp",
            (
                shape((rows, D), f32),
                shape((rows, D), f32),
                shape((2, rows, D), bf16),
                shape((2, 2 * rows, hidden), bf16),
                shape((2, 2 * rows, hidden), bf16),
                shape((1, hidden), f32),
            ),
            (place, *normed_all, *grads_mlp, up_sent[0], *up_got, w_down, bias_hidden),
            flops=24 * rows * D * hidden,
            exps=4 * rows * hidden,
            scratch=[pltpu.VMEM((D, hidden), bf16)],
        )
        norm_got = to_core(norm_give)
        norm_far_got = to_chip_row((norm_far + norm_got[1]).astype(bf16))
        norm_sent, active, grad_hidden = together((norm_got, active, grad_hidden))
        branch_own, branch_far, branch_give, *both_sums = call(
            mlp_back_kernel,
            "mlp_back",
            (
                shape((rows, D), f32),
                shape((rows, D), f32),
                shape((2, rows, D), bf16),
                *(shape((2, hidden // PIECES + 4 * piece, D), bf16) for _ in range(4)),
            ),
            (place, *normed_all, *grads_mlp, active, grad_hidden, w_down),
            flops=LONG,
            scratch=[pltpu.VMEM((hidden, D), f32), pltpu.VMEM((D, hidden), f32)],
        )
        norm_far_got, branch_own, branch_far, branch_give, *both_sums = together(
            (norm_far_got, branch_own, branch_far, branch_give, *both_sums)
        )
        grad_middle, grad_branch, grad_attended, row_sums = call(
            branch_back_kernel,
            "branch_back",
            (
                shape((rows, D), f32),
                shape((rows, D), bf16),
                shape((ctx_count, GROUP_COLS, query_rows), bf16),
                shape((8, D), f32),
            ),
            (place, norm_own, norm_got, norm_far_got, middle, top, vec, *w_out_all),
            flops=4 * rows * D * D,
        )
        grads = group_all_to_all(grad_attended)
        out_near, out_give = call(
            out_back_kernel,
            "out_back",
            (shape((2, PIECES, piece + EXTRA, D), bf16), shape((2, PIECES, piece + EXTRA, D), bf16)),
            (place, attended, grad_branch, row_sums, bias_up_sum),
            flops=2 * rows * D * D,
            scratch=[pltpu.VMEM((D + 8, D), f32)],
        )
        grads, out_near = together((grads, out_near))
        out_sum = out_near + to_core(out_give)
        grads, out_sum = together((grads, out_sum))
        out_got = to_chip_row(out_sum[1])
        both_got = to_square(both_sums[1:])
        dq, dkv, head_sums = call(
            attend_back_kernel,
            "attend_back",
            (
                shape((ctx_count, width, GROUP_COLS), bf16),
                shape((ctx_count, rows, 2 * GROUP_COLS), bf16),
                shape((8, GROUP_COLS), f32),
            ),
            (place, queries_t, keys, values, widened(grads), outs, logs),
            flops=10 * HD * pairs,
            exps=pairs,
            scratch=[
                pltpu.VMEM((rows, GROUP_COLS), f32),
                pltpu.VMEM((rows, GROUP_COLS), f32),
                pltpu.VMEM((ctx_count, width, GROUP_COLS), f32),
                pltpu.VMEM((ctx_count, 1, GROUP_HEADS * width), f32),
            ],
        )
        dq = dq[:, :query_rows]
        dq, dkv, out_got = together((dq, dkv, out_got))

        head_shapes = tuple(
            shape((2, 2, shard // 2 + EXTRA, 3 * GROUP_COLS), bf16) for _ in range(2)
        )
        if 4 * tokens * D * 2 < VMEM_LIMIT:
            head_near, head_give = call(
                heads_back_kernel,
                "heads_back",
                head_shapes,
                (place, normed_t, query_t, dq, dkv, head_sums),
                flops=work,
                scratch=[pltpu.VMEM((D, GROUP_COLS), f32), pltpu.VMEM((D, 2 * GROUP_COLS), f32)],
            )
        else:
            flat_q, flat_kv = dq.reshape(-1, GROUP_COLS), dkv.reshape(tokens, 2 * GROUP_COLS)
            head_near, head_give = call(
                arrange_heads,
                "arrange_heads",
                head_shapes,
                (place, dot(query_t, flat_q), dot(normed_t, flat_kv), head_sums),
            )
        head_near, head_give, out_got, *both_got = together(
            (head_near, head_give, out_got, *both_got)
        )
        wide = hidden // PIECES
        (both_sum,) = call(
            sum_kernel,
            "sum",
            (shape((2, wide + fsdp_count * piece, D), bf16),),
            (place, both_sums[0], *both_got),
        )
        out_sums = [
            out_sum[0, 2 * near : 2 * near + 2] + out_got[2 * near : 2 * near + 2] for near in range(4)
        ]
        head_sum = head_near + to_core(head_give)
        dq, head_near, head_give, both_sum, *out_sums = together(
            (dq, head_sum[0], head_sum[1], both_sum, *out_sums)
        )
        head_got = to_chip_row(head_give)
        both_got = to_ctx(both_sum, 4)
        out_got = to_square(out_sums[1:])

        row_shapes = (shape((half, rows, D), bf16), shape((half, rows, D), bf16))
        if 4 * tokens * D * 2 < VMEM_LIMIT:
            keep_rows, give_rows = call(
                rows_back_kernel,
                "rows_back",
                row_shapes,
                (place, dq, dkv, *w_heads),
                flops=work,
                scratch=head_weights,
            )
        else:
            weights = by_row(w_heads)
            flat_q, flat_kv = dq.reshape(-1, GROUP_COLS), dkv.reshape(tokens, 2 * GROUP_COLS)
            grad_rows = dot_nt(flat_kv, weights[:, GROUP_COLS:]).reshape(
                ctx_count, splits, query_rows, D
            )
            grad_query = dot_nt(flat_q, weights[:, :GROUP_COLS]).reshape(ctx_count, 1, query_rows, D)
            chosen = (jnp.arange(splits) == place[2])[None, :, None, None]
            grad_rows = (grad_rows + jnp.where(chosen, grad_query, 0.0)).astype(bf16)
            grad_rows = grad_rows.reshape(ctx_count, rows, D)
            keep_rows, give_rows = grad_rows[:half], grad_rows[half:]
        keep_rows, give_rows, head_got, both_got, *out_got = together(
            (keep_rows, give_rows, head_got, both_got, *out_got)
        )

        def both_sides(own, other):
            return over_rest(jnp.stack([own[0] + other[1], own[1] + other[0]]))

        rows_got = to_core(give_rows)
        head_sum = head_near + head_got
        out_sum = sum(out_got, start=out_sums[0])
        rows_got, head_sum, out_sum, both_got = together((rows_got, head_sum, out_sum, both_got))
        head_got, out_got = to_ctx(head_sum, 4), to_ctx(out_sum, 4)
        up_sum = both_sides(both_sum[:, wide:], both_got[:, wide:])
        ups = [up_sum[:, distance * piece : (distance + 1) * piece] for distance in range(fsdp_count)]
        ups = [ups[0]] + [to_fsdp(ups[distance], distance) for distance in (1, 2, 3)]
        keep_rows, both_got, branch_give, *ups = together((keep_rows, both_got, branch_give, *ups))
        if steps == 2:
            near_rows, far_rows = (keep_rows[at::2] + rows_got[at::2] for at in range(2))
        else:
            both = keep_rows + rows_got
            for bit in reversed(range(2, steps)):
                both = both[: 1 << bit] + to_ctx(both[1 << bit :], 1 << bit)
            near_rows, far_rows = both[0::2], both[1::2]
        far_got = to_ctx(far_rows, 1)
        last_got = to_ctx(near_rows[1] + far_got[1], 2)
        downs = both_sides(both_sum[:, :wide], both_got[:, :wide])
        downs = gather_square(downs, DOWN_FIRST)
        branch_got = to_core(branch_give)
        branch_far_got = to_chip_row((branch_far + branch_got[1]).astype(bf16))
        head_got, out_got = together((head_got, out_got))
        branch_mlp = branch_own + branch_got[0] + branch_far_got + vec[3:4]
        stream_out = (middle + centered(branch_mlp)).astype(bf16)[:, : D - 1]
        stream_out = swap_sequences(stream_out)
        outs = both_sides(out_sum, out_got)
        sums = outs[0, piece:].astype(f32)
        ups = jnp.concatenate([*ups, outs[:, :piece]], axis=1)
        ups = gather_square(ups, UP_FIRST)
        heads = both_sides(head_sum, head_got)
        heads = gather_square(heads, HEADS_FIRST)
        (grad_stream,) = call(
            stream_back_kernel,
            "stream_back",
            (shape((rows, D - 1), bf16),),
            (place, near_rows, far_got, last_got, resid, grad_middle, vec),
        )
        grad_stream = swap_sequences(grad_stream)
        (grad_w_down,) = call(down_out_kernel, "down_out", (shape((hidden, D), f32),), (place, *downs))
        grad_w_up, grad_w_out = call(
            up_out_kernel,
            "up_out",
            (shape((shard, fsdp_count * hidden), f32), shape((shard, D), f32)),
            (place, *ups),
        )
        grad_w_down, grad_w_up, *heads = together((grad_w_down, grad_w_up, *heads))
        grad_w_qkv, grad_gain_attn, grad_bias_qv = call(
            heads_out_kernel,
            "heads_out",
            (
                shape((shard, 3 * D), f32),
                shape((shard, 1), f32),
                shape((1, 2 * shard), f32),
            ),
            (place, *heads, w_qkv),
            scratch=[pltpu.VMEM((4, 2, shard // 2 + EXTRA, 3 * GROUP_COLS), bf16)],
        )

        return (
            stream_out,
            grad_stream.astype(f32),
            grad_gain_attn.reshape(-1) / gain_attn.astype(f32),
            grad_w_qkv,
            grad_bias_qv.reshape(-1),
            grad_w_out,
            sums[0, :shard],
            sums[0, shard : 2 * shard],
            grad_w_up,
            sums[1],
            grad_w_down,
            sums[0, 2 * shard : 3 * shard],
        )

    rows_spec, matrix_spec, vector_spec = P(AXES, None), P("fsdp", None), P("fsdp")
    return jax.shard_map(
        local,
        mesh=mesh,
        in_specs=(
            rows_spec,
            vector_spec,
            matrix_spec,
            vector_spec,
            matrix_spec,
            vector_spec,
            vector_spec,
            matrix_spec,
            vector_spec,
            matrix_spec,
            vector_spec,
            rows_spec,
        ),
        out_specs=(
            rows_spec,
            rows_spec,
            vector_spec,
            matrix_spec,
            vector_spec,
            matrix_spec,
            vector_spec,
            vector_spec,
            matrix_spec,
            vector_spec,
            matrix_spec,
            vector_spec,
        ),
        check_vma=False,
    )
```
